32 devices in a mesh: dp: 4 (over z), expert: 8 (over y, x, core).
Axes of the slice: x: 2, y: 2, z: 4, core: 2. Of those that a mesh axis runs over, the one named last changes fastest.
Arguments:
- tokens_in: bfloat16 [10240, 2048], P(('dp', 'expert')), may hold values from -6 to 6
- cotangent: bfloat16 [10240, 2048], P(('dp', 'expert')), may hold values from -6 to 6
- segment_id: int32 [10240], P('dp'), may hold values from 0 to 12, as said below
- parent_id: int32 [10240], P('dp'), may hold values from 0 to 4, as said below
- adapter_index: int32 [4], replicated, may hold values from 0 to 7
- routes: int32 [10240, 6], P(('dp', 'expert')), may hold values from 0 to 63, all different within a row; in each aligned block of 320 rows (0 to 319, 320 to 639, ...) at most 40 rows name the same one
- mixer_gain: float32 [2048], replicated, may hold values from 0.5 to 1.5
- latent_gain: float32 [512], replicated, may hold values from 0.5 to 1.5
- feed_gain: float32 [2048], replicated, may hold values from 0.5 to 1.5
- query_matrix: bfloat16 [2048, 3072], P(('dp', 'expert')), may hold values from -0.125 to 0.125
- latent_down: bfloat16 [2048, 576], P(('dp', 'expert')), may hold values from -0.125 to 0.125
- latent_up: bfloat16 [512, 4096], P(('dp', 'expert')), may hold values from -0.25 to 0.25
- output_matrix: bfloat16 [2048, 2048], P(('dp', 'expert')), may hold values from -0.75 to 0.75
- router_matrix: bfloat16 [2048, 64], P(('dp', 'expert')), may hold values from -0.0625 to 0.0625
- shared_in: bfloat16 [2048, 5632], P(('dp', 'expert')), may hold values from -0.125 to 0.125
- shared_out: bfloat16 [2816, 2048], P(('dp', 'expert')), may hold values from -0.109375 to 0.109375
- expert_in: bfloat16 [64, 2048, 2816], P('expert'), may hold values from -0.125 to 0.125
- expert_out: bfloat16 [64, 1408, 2048], P('expert'), may hold values from -6 to 6
- query_entry: bfloat16 [8, 16, 2048], replicated, may hold values from -0.125 to 0.125
- query_exit: bfloat16 [8, 16, 3072], replicated, may hold values from -0.625 to 0.625
- lower_entry: bfloat16 [8, 16, 2048], replicated, may hold values from -0.125 to 0.125
- lower_exit: bfloat16 [8, 16, 576], replicated, may hold values from -0.625 to 0.625
- upper_entry: bfloat16 [8, 16, 512], replicated, may hold values from -0.25 to 0.25
- upper_exit: bfloat16 [8, 16, 4096], replicated, may hold values from -0.625 to 0.625
- output_entry: bfloat16 [8, 16, 2048], replicated, may hold values from -0.125 to 0.125
- output_exit: bfloat16 [8, 16, 2048], replicated, may hold values from -3 to 3
Outputs:
- block_output: bfloat16 [10240, 2048], P(('dp', 'expert'))
- grad_input: bfloat16 [10240, 2048], P(('dp', 'expert'))
- grad_query_entry: float32 [8, 16, 2048], replicated
- grad_query_exit: float32 [8, 16, 3072], replicated
- grad_lower_entry: float32 [8, 16, 2048], replicated
- grad_lower_exit: float32 [8, 16, 576], replicated
- grad_upper_entry: float32 [8, 16, 512], replicated
- grad_upper_exit: float32 [8, 16, 4096], replicated
- grad_output_entry: float32 [8, 16, 2048], replicated
- grad_output_exit: float32 [8, 16, 2048], replicated
The draws below stay inside these ranges and needn't reach their ends.
Inputs may be any that keep to these rules, and one draw needn't show every extreme that they name: `segment_id`: each tree is 20 aligned blocks of 128 tokens: the first 8 blocks are segment 0 (the trunk), the other 12 hold segments 1 to 12, one block each, in some order; segments 1 to 4 are branches, 5 to 12 leaves. `parent_id`: 0 for the trunk and the branches; a leaf's parent is a branch, and each branch has two leaves. `routes`: each row names 6 different experts; in the 320 rows of one device no expert is named more than 40 times.
All inputs are finite; a program needn't handle non-finite values.
Results may differ from the reference program's by a relative error of at most 0.025.
Values may be sent and summed in bfloat16 or wider, within the bound.
A program may use at most 640 MiB of HBM per device.

```python
import math
import jax
import jax.numpy as jnp
import numpy as np
from jax import lax

D = 2048
HEADS = 16
NOPE = 128
ROPE = 64
VDIM = 128
KVR = 512
FFE = 1408
SHARED = 2816
EXPERTS = 64
TOPK = 6
RANK = 16
ADAPTERS = 8
SEGLEN = 128
TRUNK = 1024
TREE = 2560
TREES = 4
TOK_DEV = 320
TOKENS = 10240
CAP = 40


def tree_layout(key):
    tree_keys = jax.random.split(jax.random.fold_in(key, 4099), TREES)

    def one_tree(tree_key):
        order_key, leaf_key = jax.random.split(tree_key)
        block_order = jax.random.permutation(order_key, 12).astype(jnp.int32) + 1
        block_labels = jnp.concatenate([jnp.zeros((8,), jnp.int32), block_order])
        leaf_parent = 1 + jax.random.permutation(leaf_key, 8).astype(jnp.int32) // 2
        parent_table = jnp.concatenate([jnp.zeros((5,), jnp.int32), leaf_parent])
        segment = jnp.repeat(block_labels, SEGLEN)
        return (segment, parent_table[segment])
    segment, parent = jax.vmap(one_tree)(tree_keys)
    return (segment.reshape(-1), parent.reshape(-1))


def draw_segment_id(key, part):
    return tree_layout(key)[0]


def draw_parent_id(key, part):
    return tree_layout(key)[1]


def touch_ends(array, own_key, smallest, largest):
    shape = array.shape
    spot = [jax.random.randint(jax.random.fold_in(own_key, axis), (), 0, shape[axis]) for axis in range(len(shape))]
    array = array.at[tuple(spot)].set(smallest)
    longest = shape.index(max(shape))
    spot[longest] = (spot[longest] + 1) % shape[longest]
    return array.at[tuple(spot)].set(largest)


def block_scale(own_key, extent, shards, least, high):
    level, own = 1.0, jax.random.fold_in(own_key, 6)
    for axis_at, shards_of in shards:
        steps = jnp.exp(jax.random.uniform(jax.random.fold_in(own, axis_at), (shards_of,), jnp.float32, least / len(shards), high / len(shards)))
        level = level * jnp.repeat(steps, extent[axis_at] // shards_of).reshape([-1 if axis == axis_at else 1 for axis in range(len(extent))])
    return level


def assign_block(rng, own, number, rows, count, top, most, slope):
    ranking = jax.random.permutation(rng, count)
    heavy_load, usual = load_shares(count, rows * top, most, slope, True), load_shares(count, rows * top, most, slope, False)
    places = jnp.arange(count)

    def named(sizes, offset_by):
        used = int((sizes > 0).sum())
        fixed = max(1, used // 4)
        passed = fixed + (places - fixed + offset_by * (used - fixed)) % max(1, count - fixed)
        return jnp.zeros((count,), jnp.int32).at[ranking[jnp.where(places < fixed, places, passed)]].set(jnp.asarray(sizes, jnp.int32))

    sizes = jnp.where(number % 4 == 0, named(heavy_load, number // 4), named(usual, number - number // 4 - 1))
    mixed = jax.random.permutation(jax.random.fold_in(own, 3), count)
    donor, receiver = mixed[0:count // 2 * 2:2], mixed[1:count // 2 * 2:2]
    room = jnp.minimum(sizes[donor] - 1, most - sizes[receiver]) // 2
    room = jnp.where((donor == ranking[0]) | (receiver == ranking[0]) | (sizes[receiver] == 0), 0, jnp.maximum(room, 0))
    passed = jax.random.randint(jax.random.fold_in(own, 4), (count // 2,), 0, 1 << 20) % (room + 1)
    sizes = sizes.at[donor].add(-passed).at[receiver].add(passed)
    labels = jnp.searchsorted(jnp.cumsum(sizes), jnp.arange(rows * top), side="right").astype(jnp.int32)
    grid = labels.reshape(top, rows).T
    grid = grid[jax.random.permutation(jax.random.fold_in(own, 1), rows)]
    offset_by = jax.random.randint(jax.random.fold_in(own, 2), (rows, 1), 0, top)
    return jnp.take_along_axis(grid, (jnp.arange(top)[None, :] + offset_by) % top, axis=1)


def load_shares(count, total, reach, lean, full):
    portions = [(1 << 20) // math.isqrt(rank ** lean) + 1 for rank in range(1, count + 1)]
    largest = reach if full else min(reach, max(-(-total // count), total * portions[0] // sum(portions)))
    least = 1 if total - largest >= count - 1 else 0
    given, spare = [largest] + [least] * (count - 1), total - largest - least * (count - 1)
    while spare > 0:
        movable = [i for i in range(1, count) if given[i] < largest] or [i for i in range(1, count) if given[i] < reach]
        pool, left = sum([portions[i] for i in movable]), spare
        for i in movable:
            more = min(reach - given[i], max(1, left * portions[i] // pool), spare)
            given[i] = given[i] + more
            spare = spare - more
    return np.array(given)


def noise(key, dims, deviation, reach, shards=(), kind=jnp.bfloat16):
    level = block_scale(key, dims, shards, -0.22, 0.18) if shards else 1.0
    entries = jax.random.normal(key, dims, jnp.float32) * deviation * level
    return jnp.minimum(jnp.maximum(entries, -reach), reach).astype(kind)


def setup_inputs(seed: int = 0) -> dict:
    key_of = jax.random.split(jax.random.key(seed), 27)
    tokens_in = noise(key_of[0], (TOKENS, D), 1.0, 6.0, ((0, 32),))
    cotangent = noise(key_of[1], (TOKENS, D), 1.0, 6.0, ((0, 32),))
    segment_id = draw_segment_id(jax.random.fold_in(key_of[26], 71), 0)
    parent_id = draw_parent_id(jax.random.fold_in(key_of[26], 71), 0)
    adapter_index = touch_ends(jax.random.randint(key_of[4], (TREES,), 0, ADAPTERS), jax.random.fold_in(key_of[4], 1), 0, ADAPTERS - 1).astype(jnp.int32)
    routes_keys = jax.random.split(jax.random.fold_in(key_of[5], 1), TOKENS // TOK_DEV)
    routes_turns = jax.random.permutation(jax.random.fold_in(key_of[5], 3), TOKENS // TOK_DEV)
    routes = jax.vmap(lambda own, number: assign_block(jax.random.fold_in(key_of[5], 2), own, number, TOK_DEV, EXPERTS, TOPK, CAP, 2))(routes_keys, routes_turns).reshape((TOKENS, TOPK))
    mixer_gain = jnp.clip(1.0 + 0.1 * jax.random.normal(key_of[6], (D,), jnp.float32), 0.5, 1.5)
    latent_gain = jnp.clip(1.0 + 0.1 * jax.random.normal(key_of[7], (KVR,), jnp.float32), 0.5, 1.5)
    feed_gain = jnp.clip(1.0 + 0.1 * jax.random.normal(key_of[8], (D,), jnp.float32), 0.5, 1.5)
    query_matrix = noise(key_of[9], (D, HEADS * (NOPE + ROPE)), D ** -0.5, 0.125, ((0, 32),))
    latent_down = noise(key_of[10], (D, KVR + ROPE), D ** -0.5, 0.125, ((0, 32),))
    latent_up = noise(key_of[11], (KVR, HEADS * (NOPE + VDIM)), KVR ** -0.5, 0.25, ((0, 32),))
    output_matrix = noise(key_of[12], (HEADS * VDIM, D), (HEADS * VDIM // 32) ** -0.5, 0.75, ((0, 32),))
    router_matrix = noise(key_of[13], (D, EXPERTS), (4 * D) ** -0.5, 0.0625, ((0, 32),))
    shared_in = noise(key_of[14], (D, 2 * SHARED), D ** -0.5, 0.125, ((0, 32),))
    shared_out = noise(key_of[15], (SHARED, D), SHARED ** -0.5, 0.109375, ((0, 32),))
    expert_in = noise(key_of[16], (EXPERTS, D, 2 * FFE), D ** -0.5, 0.125, ((0, 8),))
    expert_out = noise(key_of[17], (EXPERTS, FFE, D), (40.0 / FFE ** 0.5), 6.0, ((0, 8),))
    query_entry = noise(key_of[18], (ADAPTERS, RANK, D), D ** -0.5, 0.125)
    query_exit = noise(key_of[19], (ADAPTERS, RANK, HEADS * (NOPE + ROPE)), 0.1, 0.625)
    lower_entry = noise(key_of[20], (ADAPTERS, RANK, D), D ** -0.5, 0.125)
    lower_exit = noise(key_of[21], (ADAPTERS, RANK, KVR + ROPE), 0.1, 0.625)
    upper_entry = noise(key_of[22], (ADAPTERS, RANK, KVR), KVR ** -0.5, 0.25)
    upper_exit = noise(key_of[23], (ADAPTERS, RANK, HEADS * (NOPE + VDIM)), 0.1, 0.625)
    output_entry = noise(key_of[24], (ADAPTERS, RANK, HEADS * VDIM), (HEADS * VDIM) ** -0.5, 0.125)
    output_exit = noise(key_of[25], (ADAPTERS, RANK, D), 0.5, 3.0)
    return dict(tokens_in=tokens_in, cotangent=cotangent, segment_id=segment_id, parent_id=parent_id, adapter_index=adapter_index, routes=routes, mixer_gain=mixer_gain, latent_gain=latent_gain, feed_gain=feed_gain, query_matrix=query_matrix, latent_down=latent_down, latent_up=latent_up, output_matrix=output_matrix, router_matrix=router_matrix, shared_in=shared_in, shared_out=shared_out, expert_in=expert_in, expert_out=expert_out, query_entry=query_entry, query_exit=query_exit, lower_entry=lower_entry, lower_exit=lower_exit, upper_entry=upper_entry, upper_exit=upper_exit, output_entry=output_entry, output_exit=output_exit)


@jax.custom_vjp
def low(v):
    return lax.optimization_barrier(v.astype(jnp.bfloat16)).astype(jnp.float32)

@jax.custom_vjp
def low_back(v):
    return v

def low_keep(v):
    return (low(v), None)

def low_pass(kept, grad):
    return (grad,)

def back_keep(v):
    return (v, None)

def back_low(kept, grad):
    return (low(grad),)
low.defvjp(low_keep, low_pass)
low_back.defvjp(back_keep, back_low)
HIGHEST = lax.Precision.HIGHEST

def both_ways(operand):
    return low_back(low(operand))

def matmul(left, right):
    return jnp.dot(left, right, precision=HIGHEST)

def widen(operand):
    return operand.astype(jnp.float32)

def normed(operand, gain):
    return operand * lax.rsqrt(lax.optimization_barrier(jnp.mean(operand * operand, axis=-1, keepdims=True)) + 1e-06) * gain

def swish(operand):
    return operand / (1.0 + jnp.exp(-operand))

def gated(gate_up):
    half_width = gate_up.shape[-1] // 2
    return swish(gate_up[..., :half_width]) * gate_up[..., half_width:]

def softmax_rows(operand):
    row_peak = lax.optimization_barrier(jnp.max(operand, axis=-1, keepdims=True))
    exp_scores = jnp.exp(operand - row_peak)
    return exp_scores / lax.optimization_barrier(jnp.sum(exp_scores, axis=-1, keepdims=True))

def rope_tables(position, width):
    half_width = width // 2
    inverse = 10000.0 ** (-(jnp.arange(half_width, dtype=jnp.float32) * 2.0 / width))
    angles = position.astype(jnp.float32)[:, None] * inverse[None, :]
    return (jnp.concatenate([jnp.cos(angles), jnp.cos(angles)], -1), jnp.concatenate([jnp.sin(angles), jnp.sin(angles)], -1))

def rotate(operand, cosine, sine):
    half_width = operand.shape[-1] // 2
    turned = jnp.concatenate([-operand[..., half_width:], operand[..., :half_width]], -1)
    return operand * cosine + turned * sine

def reference(tokens_in, cotangent, segment_id, parent_id, adapter_index, routes, mixer_gain, latent_gain, feed_gain, query_matrix, latent_down, latent_up, output_matrix, router_matrix, shared_in, shared_out, expert_in, expert_out, query_entry, query_exit, lower_entry, lower_exit, upper_entry, upper_exit, output_entry, output_exit):
    mix_query = widen(query_matrix)
    mix_down = widen(latent_down)
    mix_up = widen(latent_up)
    mix_out = widen(output_matrix)
    feed_router = widen(router_matrix)
    feed_in = widen(shared_in)
    feed_out = widen(shared_out)
    gain_one = widen(mixer_gain)
    gain_latent = widen(latent_gain)
    gain_two = widen(feed_gain)
    scaling = 1.0 / (NOPE + ROPE) ** 0.5
    blocks_tree = TREE // TOK_DEV
    seg_trees = segment_id.reshape(TREES, TREE)
    par_trees = parent_id.reshape(TREES, TREE)
    device_blocks = TOKENS // TOK_DEV
    flat_routes = routes.reshape(device_blocks, TOK_DEV * TOPK)
    flat_hot = (flat_routes[:, :, None] == jnp.arange(EXPERTS, dtype=jnp.int32)).astype(jnp.int32)
    before = jnp.cumsum(flat_hot, axis=1) - flat_hot
    slot_index = lax.optimization_barrier(jnp.sum(before * flat_hot, axis=2))
    block_number = jnp.arange(device_blocks, dtype=jnp.int32)[:, None]
    target = ((flat_routes * device_blocks + block_number) * CAP + slot_index).reshape(TOKENS, TOPK)
    owner_token = jnp.broadcast_to(jnp.arange(TOKENS, dtype=jnp.int32)[:, None], (TOKENS, TOPK))
    slot_token = jnp.full((EXPERTS * device_blocks * CAP,), TOKENS, jnp.int32).at[target.reshape(-1)].set(owner_token.reshape(-1)).reshape(EXPERTS, device_blocks * CAP)
    banks = (widen(query_entry), widen(query_exit), widen(lower_entry), widen(lower_exit), widen(upper_entry), widen(upper_exit), widen(output_entry), widen(output_exit))

    def forward(inputs, bank_list):
        q_in_bank, q_out_bank, k_in_bank, k_out_bank, u_in_bank, u_out_bank, o_in_bank, o_out_bank = bank_list

        def one_tree(pieces):
            tree_inputs, segment, parent, chosen = pieces
            query_in = q_in_bank[chosen]
            query_out = q_out_bank[chosen]
            lower_in = k_in_bank[chosen]
            lower_out = k_out_bank[chosen]
            upper_in = u_in_bank[chosen]
            upper_out = u_out_bank[chosen]
            output_in = o_in_bank[chosen]
            output_out = o_out_bank[chosen]
            hidden = low(normed(tree_inputs, gain_one))
            query_mid = both_ways(matmul(hidden, query_in.T))
            query_lin = low_back(matmul(hidden, mix_query) + matmul(query_mid, query_out))
            key_index = jnp.arange(TREE, dtype=jnp.int32)
            start_pos = jnp.where(parent == 0, TRUNK, TRUNK + SEGLEN)
            position = jnp.where(segment == 0, key_index, start_pos + key_index % SEGLEN)
            cosine, sine = rope_tables(position, ROPE)
            query_three = query_lin.reshape(TREE, HEADS, NOPE + ROPE)
            query_all = low(jnp.concatenate([query_three[:, :, :NOPE], rotate(query_three[:, :, NOPE:], cosine[:, None, :], sine[:, None, :])], -1))
            lower_mid = both_ways(matmul(hidden, lower_in.T))
            latent_full = low_back(matmul(hidden, mix_down) + matmul(lower_mid, lower_out))
            latent_norm = low(normed(latent_full[:, :KVR], gain_latent))
            key_rope = low(rotate(latent_full[:, KVR:], cosine, sine))

            def one_block(block):
                queries, row_index, row_seg, row_par = block
                upper_mid = both_ways(matmul(latent_norm, upper_in.T))
                key_value = both_ways(matmul(latent_norm, mix_up) + matmul(upper_mid, upper_out)).reshape(TREE, HEADS, NOPE + VDIM)
                scores = jnp.einsum('qhd,khd->hqk', queries[:, :, :NOPE], key_value[:, :, :NOPE], precision=HIGHEST)
                scores = scores + jnp.einsum('qhd,kd->hqk', queries[:, :, NOPE:], key_rope, precision=HIGHEST)
                scores = low_back(scores * scaling)
                visible = (segment[None, :] == row_seg[:, None]) & (key_index[None, :] <= row_index[:, None]) | (row_seg[:, None] != 0) & ((segment[None, :] == 0) | (segment[None, :] == row_par[:, None]))
                weights_soft = softmax_rows(jnp.where(visible[None], scores, -1e+30))
                attended = jnp.einsum('hqk,khd->qhd', low(weights_soft), key_value[:, :, NOPE:], precision=HIGHEST)
                return both_ways(attended.reshape(TOK_DEV, HEADS * VDIM))
            attended_all = lax.map(jax.checkpoint(one_block), (query_all.reshape(blocks_tree, TOK_DEV, HEADS, NOPE + ROPE), key_index.reshape(blocks_tree, TOK_DEV), segment.reshape(blocks_tree, TOK_DEV), parent.reshape(blocks_tree, TOK_DEV))).reshape(TREE, HEADS * VDIM)
            output_mid = both_ways(matmul(attended_all, output_in.T))
            return tree_inputs + low_back(matmul(attended_all, mix_out) + matmul(output_mid, output_out))
        mixed_state = lax.map(jax.checkpoint(one_tree), (inputs.reshape(TREES, TREE, D), seg_trees, par_trees, adapter_index)).reshape(TOKENS, D)
        feed_hidden = low(normed(mixed_state, gain_two))
        logits = low_back(matmul(feed_hidden, feed_router))
        router_probs = softmax_rows(logits)
        gate_weights = jnp.take_along_axis(router_probs, routes, axis=1)
        shared_act = low_back(matmul(feed_hidden, feed_in))
        shared_inner = low(gated(shared_act))
        shared_res = low_back(matmul(shared_inner, feed_out))
        padded = jnp.concatenate([feed_hidden, jnp.zeros((1, D), jnp.float32)], 0)

        def one_expert(pieces):
            weight_in, weight_out, rows = pieces
            received = low_back(padded[rows])
            gate_up = low_back(matmul(received, weight_in.astype(jnp.float32)))
            inner_act = low(gated(gate_up))
            return both_ways(matmul(inner_act, weight_out.astype(jnp.float32)))
        results = lax.map(jax.checkpoint(one_expert), (expert_in, expert_out, slot_token)).reshape(-1, D)
        routed = jnp.zeros((TOKENS, D), jnp.float32)
        for route_pos in range(TOPK):
            routed = routed + gate_weights[:, route_pos:route_pos + 1] * results[target[:, route_pos]]
        return mixed_state + routed + shared_res
    result, pullback = jax.vjp(forward, widen(tokens_in), banks)
    grad_inputs, grad_banks = pullback(widen(cotangent))
    return (result.astype(jnp.bfloat16), grad_inputs.astype(jnp.bfloat16), grad_banks[0], grad_banks[1], grad_banks[2], grad_banks[3], grad_banks[4], grad_banks[5], grad_banks[6], grad_banks[7])
```

```python
import functools

import jax
import jax.numpy as jnp
from jax import lax
from jax.experimental import pallas as pl
from jax.experimental.pallas import tpu as pltpu
from jax.sharding import PartitionSpec as P

D = 2048
HEADS = 16
NOPE = 128
ROPE = 64
VDIM = 128
KVR = 512
TOPK = 6
SEGLEN = 128
TRUNK = 1024
TREE = 2560
LATW = 640
HALF = ROPE // 2
VMEM_LIMIT = 66_000_000
BF = jnp.bfloat16
F32 = jnp.float32


def product(left, right):
    return jnp.dot(left, right, preferred_element_type=F32)


def product_t(left, right):
    return lax.dot_general(left, right, (((1,), (1,)), ((), ())), preferred_element_type=F32)


def product_left(left, right):
    return lax.dot_general(left, right, (((0,), (0,)), ((), ())), preferred_element_type=F32)


def normed(operand, gain):
    return operand * lax.rsqrt(jnp.mean(operand * operand, axis=-1, keepdims=True) + 1e-06) * gain


def rotate(operand, cosine, sine):
    half_width = operand.shape[-1] // 2
    turned = jnp.concatenate([-operand[..., half_width:], operand[..., :half_width]], -1)
    return operand * cosine + turned * sine


def select_slot(bank, chosen):
    return lax.dynamic_index_in_dim(bank, chosen, 0, keepdims=False)


def split_heads(matrix):
    rows = matrix.shape[0]
    three = matrix.reshape(rows, HEADS, NOPE + ROPE)
    nope = three[:, :, :NOPE].reshape(rows, HEADS * NOPE)
    rope = three[:, :, NOPE:].reshape(rows, HEADS // 2, 2, 2, HALF)
    return nope, rope.transpose(0, 1, 3, 2, 4).reshape(rows, HEADS * ROPE)


def join_heads(nope, rope):
    rows = nope.shape[0]
    turned = rope.reshape(rows, HEADS // 2, 2, 2, HALF).transpose(0, 1, 3, 2, 4)
    return jnp.concatenate(
        [nope.reshape(rows, HEADS, NOPE), turned.reshape(rows, HEADS, ROPE)], -1
    ).reshape(rows, HEADS * (NOPE + ROPE))


def lane_iota(shape):
    return lax.broadcasted_iota(jnp.int32, shape, len(shape) - 1)


def row_iota(shape):
    return lax.broadcasted_iota(jnp.int32, shape, len(shape) - 2)


LOG2E = 1.4426950408889634
SCALING = 1.0 / (NOPE + ROPE) ** 0.5


def place_keys(nb, info, lat, latsel):
    latsel[:TRUNK, :] = lat[:TRUNK, :]
    for m in range(nb):
        for side in range(2):
            start = pl.multiple_of(info[side * nb + m] * SEGLEN, SEGLEN)
            at = TRUNK + (2 * m + side) * SEGLEN
            latsel[at : at + SEGLEN, :] = lat[pl.ds(start, SEGLEN), :]


def rotary_keys(tail, kr):
    tail = tail.astype(F32)
    first = jnp.where(lane_iota(tail.shape) % ROPE < HALF, tail, 0.0)
    kr[0] = first.astype(BF)
    kr[1] = pltpu.roll(first, HALF, 1).astype(BF)


def local_limit(nb, info, m, key, row):
    return jnp.where(
        key < SEGLEN,
        (row + 1) * info[2 * nb + m] - 1,
        SEGLEN + SEGLEN * info[3 * nb + m] - 1,
    )


def attend_kernel(
    nb, info, qn, qr, cosp, sinp, qlim, lat, up, upx, out, lse, kv,
    latsel, kr, bias, near, st, sl, pt,
):
    rows_all = qn.shape[0]

    @pl.when(pl.program_id(0) == 0)
    def _():
        place_keys(nb, info, lat, latsel)
        rotary_keys(latsel[:, KVR:], kr)
        bias[...] = jnp.where(row_iota((TRUNK, rows_all)) <= qlim[...], 0.0, -1e30)
        key = row_iota((2 * SEGLEN, SEGLEN))
        row = lane_iota((2 * SEGLEN, SEGLEN))
        for m in range(nb):
            near[m] = jnp.where(key <= local_limit(nb, info, m, key, row), 0.0, -1e30)

    raw = qr[...]
    qrot = (raw * cosp[...] + pltpu.roll(raw, ROPE, 1) * sinp[...]).astype(BF)
    keys = latsel.shape[0]
    rows = keys // 2 if keys % 512 == 0 else keys
    for at in range(0, keys, rows):
        kv[at : at + rows, :] = (
            product(latsel[at : at + rows, :KVR], up[...])
            + product(latsel[at : at + rows, KVR:], upx[...])
        ).astype(BF)
    blocks = [slice(m * SEGLEN, (m + 1) * SEGLEN) for m in range(nb)]
    nears = [slice(TRUNK + 2 * m * SEGLEN, TRUNK + 2 * (m + 1) * SEGLEN) for m in range(nb)]
    chunks = [slice(at, at + 256) for at in range(0, TRUNK, 256)]
    peaks = []
    for a in range(2):
        q = jnp.concatenate([qn[:, a * 128 : a * 128 + 128], qrot], 1)
        k = jnp.concatenate([kv[:, a * 256 : a * 256 + 128], kr[a]], 1)
        peak = None
        for there in chunks:
            scores = product_t(k[there], q) + bias[there, :]
            st[a, there, :] = scores
            top = jnp.max(scores, axis=0, keepdims=True)
            peak = top if peak is None else jnp.maximum(peak, top)
        tops = []
        for m in range(nb):
            scores = product_t(k[nears[m]], q[blocks[m]]) + near[m]
            sl[a, m] = scores
            tops.append(jnp.max(scores, axis=0, keepdims=True))
        peak = jnp.maximum(peak, jnp.concatenate(tops, 1))
        peaks.append(peak * (SCALING * LOG2E))
    levels = []
    for a in range(2):
        v = kv[:, a * 256 + 128 : a * 256 + 256]
        total = None
        for there in chunks:
            e = jnp.exp2(st[a, there, :] * (SCALING * LOG2E) - peaks[a])
            part = jnp.sum(e, axis=0, keepdims=True)
            total = part if total is None else total + part
            pt[a, there, :] = e.astype(BF)
        parts, sums = [], []
        for m in range(nb):
            e = jnp.exp2(sl[a, m] * (SCALING * LOG2E) - peaks[a][:, blocks[m]])
            sums.append(jnp.sum(e, axis=0, keepdims=True))
            parts.append(product_left(e.astype(BF), v[nears[m]]))
        total = total + jnp.concatenate(sums, 1)
        got = product_left(pt[a], v[:TRUNK]) + jnp.concatenate(parts, 0)
        inverse = jnp.broadcast_to(1.0 / total, (128, rows_all)).T
        out[:, a * 128 : a * 128 + 128] = (got * inverse).astype(BF)
        levels.append(peaks[a] + jnp.log(total) * LOG2E)
    lse[0] = jnp.concatenate(levels + [jnp.zeros((6, rows_all), F32)], 0)


def attend_back_kernel(
    nb, info, qn, qr, cosp, sinp, qlim, tails, kv, up, upx, do, stats,
    dqn, dqr, gup, dlat, tail, kr, bias, near, dss, dkv, acc, dkr,
):
    step = pl.program_id(0)
    rows_all = qn.shape[0]

    @pl.when(step == 0)
    def _():
        place_keys(nb, info, tails, tail)
        rotary_keys(tail[...], kr)
        bias[...] = jnp.where(row_iota((TRUNK, rows_all)) <= qlim[...], 0.0, -1e30)
        key = row_iota((2 * SEGLEN, SEGLEN))
        row = lane_iota((2 * SEGLEN, SEGLEN))
        for m in range(nb):
            near[m] = jnp.where(key <= local_limit(nb, info, m, key, row), 0.0, -1e30)
        acc[...] = jnp.zeros_like(acc)
        dkr[...] = jnp.zeros_like(dkr)

    raw = qr[...]
    qrot = (raw * cosp[...] + pltpu.roll(raw, ROPE, 1) * sinp[...]).astype(BF)
    dq_rope = None
    for a in range(2):
        q = jnp.concatenate([qn[:, a * 128 : a * 128 + 128], qrot], 1)
        k = jnp.concatenate([kv[:, a * 256 : a * 256 + 128], kr[a]], 1)
        v = kv[:, a * 256 + 128 : a * 256 + 256]
        g = do[:, a * 128 : a * 128 + 128]
        level = stats[0, a : a + 1, :]
        delta = stats[0, 2 + a : 3 + a, :]
        mine = lane_iota((1, 128)) % ROPE
        mine = (mine < HALF) if a == 0 else (mine >= HALF)

        def block(there, here, hide):
            scores = product_t(k[there], q[here]) + hide
            p = jnp.exp2(scores * (SCALING * LOG2E) - level[:, here])
            ds = (p * (product_t(v[there], g[here]) - delta[:, here])).astype(BF)
            dk = product(ds, q[here]) * SCALING
            dkv[there, a * 256 : a * 256 + 128] = dk[:, :128].astype(BF)
            dkv[there, a * 256 + 128 : a * 256 + 256] = product(p.astype(BF), g[here]).astype(BF)
            dkr[there, :] += jnp.where(mine, dk[:, 128:], 0.0)
            return ds

        for at in range(0, TRUNK, 256):
            there = slice(at, at + 256)
            dss[there, :] = block(there, slice(0, rows_all), bias[there, :])
        parts = []
        for m in range(nb):
            here = slice(m * SEGLEN, (m + 1) * SEGLEN)
            there = slice(TRUNK + 2 * m * SEGLEN, TRUNK + 2 * (m + 1) * SEGLEN)
            parts.append(product_left(block(there, here, near[m]), k[there]))
        dq = (product_left(dss[...], k[:TRUNK]) + jnp.concatenate(parts, 0)) * SCALING
        dqn[:, a * 128 : a * 128 + 128] = dq[:, :128].astype(BF)
        dq_rope = dq[:, 128:] if dq_rope is None else dq_rope + dq[:, 128:]
    dqr[...] = (dq_rope * cosp[...] + pltpu.roll(dq_rope * sinp[...], ROPE, 1)).astype(BF)
    gup[...] = product_left(tail[...], dkv[...])
    for at in range(0, tail.shape[0], 256):
        acc[at : at + 256, :KVR] += product_t(dkv[at : at + 256, :], up[...])
        acc[at : at + 256, KVR:] += product_t(dkv[at : at + 256, :], upx[...])

    @pl.when(step == pl.num_programs(0) - 1)
    def _():
        rope = dkr[...]
        folded = rope + pltpu.roll(rope, 128 - HALF, 1)
        keep = lane_iota(rope.shape) % ROPE < HALF
        acc[:, KVR:] += jnp.where(keep, folded, 0.0)
        dlat[:TRUNK, :] = acc[:TRUNK, :]
        dlat[TRUNK:, :] = jnp.zeros((TREE - TRUNK, LATW), F32)
        for m in range(nb):
            for side in range(2):
                start = pl.multiple_of(info[side * nb + m] * SEGLEN, SEGLEN)
                at = TRUNK + (2 * m + side) * SEGLEN
                dlat[pl.ds(start, SEGLEN), :] += acc[at : at + SEGLEN, :]


def pair_spec(rows, width):
    return pl.BlockSpec((rows, width), lambda i, info: (0, i))


def lead_spec(rows, width):
    return pl.BlockSpec((1, rows, width), lambda i, info: (i, 0, 0))


def whole_spec(shape):
    return pl.BlockSpec(shape, lambda i, info: (0, 0))


def attend(nb, info, qn, qr, cosp, sinp, qlim, lat, up, upx):
    rows, keys = qn.shape[0], TRUNK + 2 * nb * SEGLEN
    return pl.pallas_call(
        functools.partial(attend_kernel, nb),
        out_shape=(
            jax.ShapeDtypeStruct((rows, HEADS * VDIM), BF),
            jax.ShapeDtypeStruct((HEADS // 2, 8, rows), F32),
            jax.ShapeDtypeStruct((keys, HEADS * (NOPE + VDIM)), BF),
        ),
        grid_spec=pltpu.PrefetchScalarGridSpec(
            num_scalar_prefetch=1,
            grid=(HEADS // 2,),
            in_specs=[
                pair_spec(rows, 256),
                pair_spec(rows, 128),
                whole_spec((rows, 128)),
                whole_spec((rows, 128)),
                whole_spec((1, rows)),
                whole_spec((TREE, LATW)),
                pair_spec(KVR, 512),
                pair_spec(LATW - KVR, 512),
            ],
            out_specs=(pair_spec(rows, 256), lead_spec(8, rows), pair_spec(keys, 512)),
            scratch_shapes=[
                pltpu.VMEM((keys, LATW), BF),
                pltpu.VMEM((2, keys, 128), BF),
                pltpu.VMEM((TRUNK, rows), F32),
                pltpu.VMEM((nb, 2 * SEGLEN, SEGLEN), F32),
                pltpu.VMEM((2, TRUNK, rows), F32),
                pltpu.VMEM((2, nb, 2 * SEGLEN, SEGLEN), F32),
                pltpu.VMEM((2, TRUNK, rows), BF),
            ],
        ),
        name="attend",
        **costs(30e9, 25e6),
    )(info, qn, qr, cosp, sinp, qlim[None, :], lat, up, upx)


def attend_back(nb, info, qn, qr, cosp, sinp, qlim, lat, kv, up, upx, do, stats):
    rows, keys = qn.shape[0], TRUNK + 2 * nb * SEGLEN
    return pl.pallas_call(
        functools.partial(attend_back_kernel, nb),
        out_shape=(
            jax.ShapeDtypeStruct((rows, HEADS * NOPE), BF),
            jax.ShapeDtypeStruct((rows, HEADS * ROPE), BF),
            jax.ShapeDtypeStruct((128, HEADS * (NOPE + VDIM)), F32),
            jax.ShapeDtypeStruct((TREE, LATW), F32),
        ),
        grid_spec=pltpu.PrefetchScalarGridSpec(
            num_scalar_prefetch=1,
            grid=(HEADS // 2,),
            in_specs=[
                pair_spec(rows, 256),
                pair_spec(rows, 128),
                whole_spec((rows, 128)),
                whole_spec((rows, 128)),
                whole_spec((1, rows)),
                pl.BlockSpec((TREE, 128), lambda i, info: (0, KVR // 128)),
                pair_spec(keys, 512),
                pair_spec(KVR, 512),
                pair_spec(LATW - KVR, 512),
                pair_spec(rows, 256),
                lead_spec(8, rows),
            ],
            out_specs=(
                pair_spec(rows, 256),
                pair_spec(rows, 128),
                pair_spec(128, 512),
                whole_spec((TREE, LATW)),
            ),
            scratch_shapes=[
                pltpu.VMEM((keys, 128), BF),
                pltpu.VMEM((2, keys, 128), BF),
                pltpu.VMEM((TRUNK, rows), F32),
                pltpu.VMEM((nb, 2 * SEGLEN, SEGLEN), F32),
                pltpu.VMEM((TRUNK, rows), BF),
                pltpu.VMEM((keys, 512), BF),
                pltpu.VMEM((keys, LATW), F32),
                pltpu.VMEM((keys, 128), F32),
            ],
        ),
        name="attend_back",
        **costs(54e9, 30e6),
    )(info, qn, qr, cosp, sinp, qlim[None, :], lat, kv, up, upx, do, stats)


def gated_parts(gate, up):
    sig = 1.0 / (1.0 + jnp.exp(-gate))
    swish = gate * sig
    return swish * up, swish, up * (sig * (1.0 + gate * (1.0 - sig)))


def slot_matrix(slots, owned, cap, rows):
    wanted = row_iota((cap, rows)) + 1
    return [slots[e : e + 1, :] == wanted for e in range(owned)]


def spread_grad_kernel(owned, cap, pay, slots, sh_out, perm, gsh):
    rows = pay.shape[0]
    pick = slot_matrix(slots[0].astype(jnp.int32), owned, cap, rows)
    hot = jnp.concatenate([p.astype(F32) for p in pick], 0).astype(BF)
    values = pay[:, :D]
    got = product(hot, values)
    for e in range(owned):
        perm[e, 0] = got[e * cap : (e + 1) * cap].astype(BF)
    gsh[...] = product_t(values, sh_out[...])


def spread_feed_kernel(owned, cap, pay, slots, probs, gsh, sh_in, perm, gates, inner, gact):
    rows = pay.shape[0]
    pick = slot_matrix(slots[0].astype(jnp.int32), owned, cap, rows)
    hot = jnp.concatenate([p.astype(F32) for p in pick], 0).astype(BF)
    values = pay[:, :D]
    got = product(hot, values)
    for e in range(owned):
        perm[e, 0] = got[e * cap : (e + 1) * cap].astype(BF)
        gate = jnp.sum(jnp.where(pick[e], probs[0, e : e + 1, :], 0.0), axis=1, keepdims=True)
        gates[e, 0] = jnp.broadcast_to(gate, (cap, 128))
    width = gsh.shape[1]
    act = product(values, sh_in[...])
    value, by_up, by_gate = gated_parts(act[:, :width], act[:, width:])
    inner[...] = value.astype(BF)
    gact[:, :width] = (gsh[...] * by_gate).astype(BF)
    gact[:, width:] = (gsh[...] * by_up).astype(BF)


def expert_grad_kernel(g, w_out, back):
    hidden = w_out.shape[1]
    for at in range(0, hidden, 256):
        width = min(256, hidden - at)
        back[0, :, at : at + width] = product_t(g[0], w_out[0, at : at + width, :]).astype(BF)


def expert_kernel(experts, first, x, back, gates, w_in, slot_out, inner, ggu):
    hidden = back.shape[2]
    x_here = x[0]
    gate_here = gates[0][:, :1]
    total = jnp.zeros((x_here.shape[0], 1), F32)
    for at in range(0, hidden, 256):
        width = min(256, hidden - at)
        gate = product(x_here, w_in[0, :, at : at + width])
        up = product(x_here, w_in[0, :, hidden + at : hidden + at + width])
        value, by_up, by_gate = gated_parts(gate, up)
        low = value.astype(BF)
        inner[0, :, at : at + width] = low
        here = back[0, :, at : at + width].astype(F32)
        scaled = here * gate_here
        ggu[:, at : at + width] = (scaled * by_gate).astype(BF)
        ggu[:, hidden + at : hidden + at + width] = (scaled * by_up).astype(BF)
        total = total + jnp.sum(low.astype(F32) * here, axis=1, keepdims=True)
    for at in range(0, D, 256):
        slot_out[0, :, at : at + 256] = product_t(ggu[...], w_in[0, at : at + 256, :]).astype(BF)
    high = total.astype(BF).astype(F32)
    mine = first[0] + pl.program_id(0)
    lane = lane_iota((x_here.shape[0], slot_out.shape[2] - D))
    extra = jnp.where(lane == mine, high, jnp.where(lane == experts + mine, total - high, 0.0))
    slot_out[0, :, D:] = extra.astype(BF)


def expert_rows_kernel(inner, gates, w_out, rows_out):
    gate_here = gates[0][:, :1]
    for at in range(0, D, 256):
        rows = product(inner[0], w_out[0, :, at : at + 256]) * gate_here
        rows_out[0, :, at : at + 256] = rows.astype(BF)


def collect_kernel(owned, cap, rows_perm, slots, inner, weight, out, *, transposed):
    rows = out.shape[0]
    spread = (
        lane_iota((128, owned * cap)) // cap == row_iota((128, owned * cap))
    ).astype(F32).astype(BF)
    named = product(slots[...], spread)
    wanted = (lane_iota((rows, owned * cap)) % cap + 1).astype(F32)
    hot = (named == wanted).astype(F32).astype(BF)
    values = jnp.concatenate([rows_perm[e, 0].astype(F32) for e in range(owned)], 0).astype(BF)
    if transposed:
        shared = product_t(inner[...], weight[...])
    else:
        shared = product(inner[...], weight[...])
    out[:, :D] = (product(hot, values[:, :D]) + shared).astype(BF)
    if out.shape[1] > D:
        out[:, D:] = product(hot, values[:, D:]).astype(BF)


def row_block(rows, width):
    return pl.BlockSpec((rows, width), lambda b: (b, 0))


def fixed(shape):
    return pl.BlockSpec(shape, lambda b: (0,) * len(shape))


def token_block(owned, rows):
    return pl.BlockSpec((1, owned, rows), lambda b: (b, 0, 0))


def perm_block(owned, cap, width):
    return pl.BlockSpec((owned, 1, cap, width), lambda b: (0, b, 0, 0))


def costs(flops, moved):
    return dict(
        compiler_params=pltpu.CompilerParams(
            vmem_limit_bytes=VMEM_LIMIT
        ),
        cost_estimate=pl.CostEstimate(
            flops=int(flops), bytes_accessed=int(moved), transcendentals=0
        ),
    )


def spread_grad(payload, slots, sh_out, cap):
    groups, owned, rows = slots.shape
    width = sh_out.shape[0]
    return pl.pallas_call(
        functools.partial(spread_grad_kernel, owned, cap),
        grid=(groups,),
        out_shape=(
            jax.ShapeDtypeStruct((owned, groups, cap, D), BF),
            jax.ShapeDtypeStruct((groups * rows, width), F32),
        ),
        in_specs=[
            row_block(rows, payload.shape[1]),
            token_block(owned, rows),
            fixed(sh_out.shape),
        ],
        out_specs=(perm_block(owned, cap, D), row_block(rows, width)),
        name="spread_grad",
        **costs(12e9, 28e6),
    )(payload, slots, sh_out)


def spread_feed(payload, slots, probs, gsh, sh_in, cap):
    groups, owned, rows = slots.shape
    width = gsh.shape[1]
    return pl.pallas_call(
        functools.partial(spread_feed_kernel, owned, cap),
        grid=(groups,),
        out_shape=(
            jax.ShapeDtypeStruct((owned, groups, cap, D), BF),
            jax.ShapeDtypeStruct((owned, groups, cap, 128), F32),
            jax.ShapeDtypeStruct((groups * rows, width), BF),
            jax.ShapeDtypeStruct((groups * rows, 2 * width), BF),
        ),
        in_specs=[
            row_block(rows, payload.shape[1]),
            token_block(owned, rows),
            token_block(owned, rows),
            row_block(rows, width),
            fixed(sh_in.shape),
        ],
        out_specs=(
            perm_block(owned, cap, D),
            perm_block(owned, cap, 128),
            row_block(rows, width),
            row_block(rows, 2 * width),
        ),
        name="spread_feed",
        **costs(14e9, 28e6),
    )(payload, slots, probs, gsh, sh_in)


def row_chunk(rows):
    count = 1
    while rows // count > 384 or rows % count or rows // count % 8:
        count += 1
    return rows // count


def expert_specs(owned, rows):
    chunk = row_chunk(rows)

    def at(width):
        return pl.BlockSpec((1, chunk, width), lambda e, i, *_: (e, i, 0))

    def weight(shape):
        return pl.BlockSpec((1,) + shape, lambda e, i, *_: (e, 0, 0))

    return (owned, rows // chunk), chunk, at, weight


def expert_grads(g, w_out):
    owned, rows, _ = g.shape
    hidden = w_out.shape[1]
    grid, _, at, weight = expert_specs(owned, rows)
    return pl.pallas_call(
        expert_grad_kernel,
        out_shape=jax.ShapeDtypeStruct((owned, rows, hidden), BF),
        grid=grid,
        in_specs=[at(D), weight((hidden, D))],
        out_specs=at(hidden),
        name="expert_grads",
        **costs(2 * owned * rows * D * hidden, owned * (D * hidden * 2 + rows * D * 4)),
    )(g, w_out)


def run_experts(first, x, back, gates, w_in, experts):
    owned, rows, _ = x.shape
    hidden = back.shape[2]
    grid, chunk, at, weight = expert_specs(owned, rows)
    return pl.pallas_call(
        functools.partial(expert_kernel, experts),
        out_shape=(
            jax.ShapeDtypeStruct((owned, rows, D + 128), BF),
            jax.ShapeDtypeStruct((owned, rows, hidden), BF),
        ),
        grid_spec=pltpu.PrefetchScalarGridSpec(
            num_scalar_prefetch=1,
            grid=grid,
            in_specs=[at(D), at(hidden), at(128), weight((D, 2 * hidden))],
            out_specs=(at(D + 128), at(hidden)),
            scratch_shapes=[pltpu.VMEM((chunk, 2 * hidden), BF)],
        ),
        name="experts",
        **costs(8 * owned * rows * D * hidden, owned * D * hidden * 4),
    )(first, x, back, gates, w_in)


def expert_rows(inner, gates, w_out):
    owned, rows, hidden = inner.shape
    grid, _, at, weight = expert_specs(owned, rows)
    return pl.pallas_call(
        expert_rows_kernel,
        out_shape=jax.ShapeDtypeStruct((owned, rows, D), BF),
        grid=grid,
        in_specs=[at(hidden), at(128), weight((hidden, D))],
        out_specs=at(D),
        name="expert_rows",
        **costs(2 * owned * rows * D * hidden, owned * (D * hidden * 2 + rows * D * 4)),
    )(inner, gates, w_out)


def collect(rows_perm, slots, inner, weight, transposed):
    owned, groups, cap, width = rows_perm.shape
    rows = slots.shape[0] // groups
    return pl.pallas_call(
        functools.partial(collect_kernel, owned, cap, transposed=transposed),
        grid=(groups,),
        out_shape=jax.ShapeDtypeStruct((groups * rows, width), BF),
        in_specs=[
            perm_block(owned, cap, width),
            row_block(rows, 128),
            row_block(rows, inner.shape[1]),
            fixed(weight.shape),
        ],
        out_specs=row_block(rows, width),
        name="collect_grad" if transposed else "collect_rows",
        **costs(14e9, 28e6),
    )(rows_perm, slots, inner, weight)


MESH = pl.DeviceIdType.MESH
PLANE = 8


def neighbours():
    e = lax.axis_index("expert")
    core, x, y = e % 2, (e // 2) % 2, e // 4
    return e, 1 - 2 * core, 2 - 4 * x, 4 - 8 * y


def remote(src, dst, send_sem, recv_sem, **where):
    return pltpu.make_async_remote_copy(
        src_ref=src,
        dst_ref=dst,
        send_sem=send_sem,
        recv_sem=recv_sem,
        device_id=where,
        device_id_type=MESH,
    )


def greet(plane, levels):
    barrier = pltpu.get_barrier_semaphore()
    for who in plane:
        pl.semaphore_signal(barrier, inc=1, device_id={"expert": who}, device_id_type=MESH)
    for level in levels:
        pl.semaphore_signal(barrier, inc=1, device_id={"dp": level}, device_id_type=MESH)
    pl.semaphore_wait(barrier, len(plane) + len(levels))


class Mail:
    def __init__(self):
        self.sent = []

    def start(self, src, dst, pair, index, **where):
        copy = remote(src, dst, pair[0].at[index], pair[1].at[index], **where)
        copy.start()
        self.sent.append((None, copy))

    def arrived(self, dst, pair, index):
        here = neighbours()[0]
        remote(dst, dst, pair[0].at[index], pair[1].at[index], expert=here).wait_recv()

    def along(self, level, planes, src, dst, pair, index):
        z = lax.axis_index("dp")
        for way, fits, ahead in (
            (0, (level <= z) & (z < planes - 1), z + 1),
            (1, (level >= z) & (z > 0), z - 1),
        ):
            copy = remote(src, dst, pair[0].at[(way, *index)], pair[1].at[index], dp=ahead)
            pl.when(fits)(copy.start)
            self.sent.append((fits, copy))

    def line_arrived(self, dst, pair, index):
        here = neighbours()[0]
        remote(dst, dst, pair[0].at[(0, *index)], pair[1].at[index], expert=here).wait_recv()

    def drain(self):
        for fits, copy in self.sent:
            if fits is None:
                copy.wait_send()
            else:
                pl.when(fits)(copy.wait_send)


def nearest_levels(planes):
    if planes == 1:
        return [0]
    z = lax.axis_index("dp")
    power = 1 + 3 * z + 9 * (z * (z - 1) // 2) + 27 * (z * (z - 1) * (z - 2) // 6)
    order = ((1, 2, 3), (0, 2, 3), (1, 3, 0), (2, 1, 0))
    packed = [sum(order[at][m] * 4**at for at in range(4)) for m in range(3)]
    return [z] + [(code // power) % 4 for code in packed]


def spread_pieces(planes, count, source, place, mail, sems, meanwhile=None):
    line, by_x, by_y, by_far, by_core = [sems[2 * n : 2 * n + 2] for n in range(5)]
    e, to_core, to_x, to_y = neighbours()
    levels = nearest_levels(planes)
    partner, xn, yn, dg = e + to_core, e + to_x, e + to_y, e + to_x + to_y

    def at(k, who, i):
        return place(levels[k], who, i)

    def stage_a(k):
        for i in range(count):
            here = at(k, e, i)
            src = source(i) if k == 0 else here
            if k:
                mail.line_arrived(here, line, (levels[k], i))
            if planes > 1:
                mail.along(levels[k], planes, src, here, line, (levels[k], i))
            if i % 2 == 0:
                mail.start(src, here, by_x, (k, i), expert=xn)
                mail.start(src, here, by_y, (k, i), expert=yn)
            else:
                mail.start(src, here, by_y, (k, i), expert=yn)
                mail.start(src, here, by_x, (k, i), expert=xn)
            mail.start(src, here, by_core, (0, k, i), expert=partner)

    def stage_b(k):
        for i in range(count):
            left, up = at(k, xn, i), at(k, yn, i)
            mail.arrived(left, by_x, (k, i))
            if i % 2 == 0:
                mail.start(left, left, by_far, (k, i), expert=yn)
            mail.start(left, left, by_core, (1, k, i), expert=partner)
            mail.arrived(up, by_y, (k, i))
            if i % 2:
                mail.start(up, up, by_far, (k, i), expert=xn)
            mail.start(up, up, by_core, (2, k, i), expert=partner)

    def stage_c(k):
        for i in range(count):
            here = at(k, dg, i)
            mail.arrived(here, by_far, (k, i))
            mail.start(here, here, by_core, (3, k, i), expert=partner)

    for s in range(planes + 2):
        if s < planes:
            stage_a(s)
        if meanwhile is not None:
            meanwhile(s)
        if 0 <= s - 1 < planes:
            stage_b(s - 1)
        if 0 <= s - 2:
            stage_c(s - 2)
    for k in range(planes):
        for n, who in enumerate((e, xn, yn, dg)):
            for i in range(count):
                mail.arrived(at(k, who + to_core, i), by_core, (n, k, i))


def spread_sems(planes, count):
    dma = pltpu.SemaphoreType.DMA
    each, core = dma((planes, count)), dma((4, planes, count))
    return [dma((2, planes, count)), *([each] * 7), core, core]


def plane_peers(swaps):
    e, to_core, to_x, to_y = neighbours()
    if swaps:
        return [(e + j) % PLANE for j in range(1, PLANE)]
    return [e + to_core, e + to_x, e + to_y]


def other_levels(planes):
    if planes == 1:
        return []
    z = lax.axis_index("dp")
    return [(z + k) % planes for k in range(1, planes)]


def swap_out(mail, src, landing, pair, n):
    e = neighbours()[0]
    for j in range(1, PLANE):
        who = (e + j) % PLANE
        mail.start(src(who), landing(e), pair, (n, j - 1), expert=who)


def swap_in(mail, landing, pair, n):
    e = neighbours()[0]
    for j in range(1, PLANE):
        mail.arrived(landing((e + PLANE - j) % PLANE), pair, (n, j - 1))


def gather_kernel(planes, pieces, count, swaps, lines, *refs):
    total = count + swaps + lines
    shards, outs = refs[:total], refs[total : 2 * total]
    sems = refs[2 * total :]
    own_sem, swap, line = sems[10], sems[11:13], sems[13:15]
    e = neighbours()[0]
    levels = nearest_levels(planes)
    z = levels[0]
    mail = Mail()
    greet(plane_peers(swaps), other_levels(planes))

    def place(level, who, i):
        array, first, rows = pieces[i]
        return outs[array].at[level, who, pl.ds(first, rows)]

    def source(i):
        array, first, rows = pieces[i]
        return shards[array].at[pl.ds(first, rows)]

    mine = [pltpu.make_async_copy(shards[a], outs[a].at[z, e], own_sem.at[a]) for a in range(count)]
    for a in range(count, count + swaps):
        mine.append(pltpu.make_async_copy(shards[a].at[e], outs[a].at[z, e], own_sem.at[a]))
    for a in range(count + swaps, total):
        mine.append(pltpu.make_async_copy(shards[a], outs[a].at[z], own_sem.at[a]))
    for copy in mine:
        copy.start()
    for n in range(swaps):
        a = count + n
        swap_out(
            mail, lambda who: shards[a].at[who], lambda who: outs[a].at[z, who], swap, n
        )
    cuts = []
    for a in range(count, total):
        size = outs[a].shape[1]
        half = size // 2
        cuts += [(a, pl.ds(0, half)), (a, pl.ds(half, size - half))]

    def line_step(k):
        for i, (a, rows) in enumerate(cuts):
            here = outs[a].at[levels[k], rows]
            src = here if k or a < count + swaps else shards[a].at[rows]
            if k:
                mail.line_arrived(here, line, (levels[k], i))
            mail.along(levels[k], planes, src, here, line, (levels[k], i))

    def meanwhile(s):
        if s == planes - 1:
            for n in range(swaps):
                a = count + n
                swap_in(mail, lambda who: outs[a].at[z, who], swap, n)
                mine[a].wait()
            line_step(0)
        if s >= planes:
            line_step(s - planes + 1)

    spread_pieces(
        planes, len(pieces), source, place, mail, sems, meanwhile if cuts else None
    )
    if cuts:
        for k in range(3, planes):
            line_step(k)
    for n, copy in enumerate(mine):
        if not count <= n < count + swaps:
            copy.wait()
    mail.drain()


def gather_blocks(shards, planes, cuts, ident, swaps=(), lines=()):
    dma = pltpu.SemaphoreType.DMA
    pieces = []
    for array, (shard, cut) in enumerate(zip(shards, cuts)):
        rows = shard.shape[0] // cut
        pieces += [(array, at * rows, rows) for at in range(cut)]
    count, total = len(shards), len(shards) + len(swaps) + len(lines)
    shapes = [jax.ShapeDtypeStruct((planes, PLANE) + s.shape, s.dtype) for s in shards]
    shapes += [jax.ShapeDtypeStruct((planes,) + s.shape, s.dtype) for s in [*swaps, *lines]]
    return pl.pallas_call(
        functools.partial(gather_kernel, planes, pieces, count, len(swaps), len(lines)),
        out_shape=shapes,
        in_specs=[pl.BlockSpec(memory_space=pl.ANY)] * total,
        out_specs=[pl.BlockSpec(memory_space=pl.ANY)] * total,
        scratch_shapes=[
            *spread_sems(planes, len(pieces)),
            dma((total,)),
            dma((max(1, len(swaps)), PLANE - 1)),
            dma((max(1, len(swaps)), PLANE - 1)),
            dma((2, planes, max(1, 2 * (total - count)))),
            dma((planes, max(1, 2 * (total - count)))),
        ],
        compiler_params=pltpu.CompilerParams(collective_id=ident, has_side_effects=True),
        name=f"gather{ident}",
    )(*shards, *swaps, *lines)


def bank_kernel(planes, wide, parts, out, landing, part, *sems):
    e = neighbours()[0]
    z = lax.axis_index("dp")
    mail = Mail()
    swap = sems[10:12]
    greet(plane_peers(1), other_levels(planes))

    def chunk(who):
        return pl.ds(pl.multiple_of(who * wide, 128), wide)

    swap_out(mail, lambda who: parts.at[:, chunk(who)], lambda who: landing.at[who], swap, 0)
    total = parts[:, chunk(e)].astype(F32)
    for j in range(1, PLANE):
        who = (e + PLANE - j) % PLANE
        mail.arrived(landing.at[who], swap, (0, j - 1))
        total = total + landing[who].astype(F32)
    low = total.astype(BF)
    part[...] = low
    out[z, e] = low
    spread_pieces(
        planes, 1, lambda i: part, lambda level, who, i: out.at[level, who], mail, sems
    )
    mail.drain()


def exchange_banks(joined, planes, ident):
    rank, width = joined.shape
    wide = width // PLANE
    dma = pltpu.SemaphoreType.DMA
    vmem = pl.BlockSpec(memory_space=pltpu.VMEM)
    return pl.pallas_call(
        functools.partial(bank_kernel, planes, wide),
        out_shape=jax.ShapeDtypeStruct((planes, PLANE, rank, wide), BF),
        in_specs=[vmem],
        out_specs=vmem,
        scratch_shapes=[
            pltpu.VMEM((PLANE, rank, wide), BF),
            pltpu.VMEM((rank, wide), BF),
            *spread_sems(planes, 1),
            dma((1, PLANE - 1)),
            dma((1, PLANE - 1)),
        ],
        compiler_params=pltpu.CompilerParams(
            collective_id=ident, has_side_effects=True, vmem_limit_bytes=VMEM_LIMIT
        ),
        name=f"banks{ident}",
    )(joined)


def place_kernel(trees, offsets, chosen, full, *outs):
    slot = pl.program_id(0)
    wide = full.shape[3]
    for n, (at, width) in enumerate(offsets):
        total = jnp.zeros(outs[n].shape[1:], F32)
        for t in range(trees):
            pick = (chosen[t] == slot).astype(F32)
            columns = []
            while sum(c.shape[1] for c in columns) < width:
                here = at + sum(c.shape[1] for c in columns)
                first = here % wide
                upto = min(wide, first + at + width - here)
                columns.append(full[t, here // wide, :, first:upto].astype(F32))
            total = total + pick * jnp.concatenate(columns, 1)
        outs[n][0] = total


def place_banks(full, adapter_index, offsets, adapters):
    trees, _, rank, _ = full.shape
    return pl.pallas_call(
        functools.partial(place_kernel, trees, offsets),
        out_shape=[jax.ShapeDtypeStruct((adapters, rank, w), F32) for _, w in offsets],
        grid_spec=pltpu.PrefetchScalarGridSpec(
            num_scalar_prefetch=1,
            grid=(adapters,),
            in_specs=[pl.BlockSpec(full.shape, lambda a, chosen: (0, 0, 0, 0))],
            out_specs=[pl.BlockSpec((1, rank, w), lambda a, chosen: (a, 0, 0)) for _, w in offsets],
        ),
        name="place_banks",
        **costs(1e6, 11e6),
    )(adapter_index, full)


def scatter_kernel(parts, blocks, out, core_in, x_in, y_in, chip, total, sends, sems):
    e, to_core, to_x, to_y = neighbours()
    partner, xn, yn, dg = e + to_core, e + to_x, e + to_y, e + to_x + to_y
    rows = out.shape[0] // parts
    half = parts // 2
    greet((partner, xn, yn), [])
    mail, pair = Mail(), (sends, sems)

    def start(src, dst, index, **where):
        mail.start(src, dst, pair, index, **where)

    def arrived(dst, index):
        mail.arrived(dst, pair, index)

    def cut(p):
        return pl.ds(p * rows, rows)

    order = [p // 2 + (p % 2) * half for p in range(parts)]
    whose = (0, to_x, to_y, to_x + to_y)
    for p in order:
        for b in (3, 1, 2, 0):
            start(
                blocks.at[partner + whose[b], cut(p)],
                core_in.at[b, cut(p)],
                (b, p),
                expert=partner,
            )

    def add_chip(p):
        for b in (3, 1, 2, 0):
            arrived(core_in.at[b, cut(p)], (b, p))
            chip[b, cut(p), :] = (
                blocks[e + whose[b], cut(p), :].astype(F32) + core_in[b, cut(p), :].astype(F32)
            ).astype(BF)

    def first_hop(p):
        if p < half:
            start(chip.at[3, cut(p)], x_in.at[1, cut(p)], (5, p), expert=xn)
            start(chip.at[1, cut(p)], x_in.at[0, cut(p)], (4, p), expert=xn)
        else:
            start(chip.at[3, cut(p)], x_in.at[1, cut(p)], (5, p), expert=yn)
            start(chip.at[2, cut(p)], x_in.at[0, cut(p)], (4, p), expert=yn)

    def add_first(p):
        passed = 2 if p < half else 1
        arrived(x_in.at[1, cut(p)], (5, p))
        chip[passed, cut(p), :] = (
            chip[passed, cut(p), :].astype(F32) + x_in[1, cut(p), :].astype(F32)
        ).astype(BF)
        arrived(x_in.at[0, cut(p)], (4, p))
        total[cut(p), :] = chip[0, cut(p), :].astype(F32) + x_in[0, cut(p), :].astype(F32)

    def second_hop(p):
        if p < half:
            start(chip.at[2, cut(p)], y_in.at[cut(p)], (6, p), expert=yn)
        else:
            start(chip.at[1, cut(p)], y_in.at[cut(p)], (6, p), expert=xn)

    def finish(p):
        arrived(y_in.at[cut(p)], (6, p))
        out[cut(p), :] = (total[cut(p), :] + y_in[cut(p), :].astype(F32)).astype(out.dtype)

    for n, p in enumerate(order):
        add_chip(p)
        if n:
            first_hop(order[n - 1])
    first_hop(order[-1])
    for n, p in enumerate(order):
        add_first(p)
        if n:
            second_hop(order[n - 1])
    second_hop(order[-1])
    for p in order:
        finish(p)
    mail.drain()


def scatter_blocks(blocks, parts, ident, dtype):
    _, rows, width = blocks.shape
    dma = pltpu.SemaphoreType.DMA
    vmem = pl.BlockSpec(memory_space=pltpu.VMEM)
    return pl.pallas_call(
        functools.partial(scatter_kernel, parts),
        out_shape=jax.ShapeDtypeStruct((rows, width), dtype),
        in_specs=[vmem],
        out_specs=vmem,
        scratch_shapes=[
            pltpu.VMEM((4, rows, width), BF),
            pltpu.VMEM((2, rows, width), BF),
            pltpu.VMEM((rows, width), BF),
            pltpu.VMEM((4, rows, width), BF),
            pltpu.VMEM((rows, width), F32),
            dma((7, parts)),
            dma((7, parts)),
        ],
        compiler_params=pltpu.CompilerParams(
            collective_id=ident, has_side_effects=True, vmem_limit_bytes=VMEM_LIMIT
        ),
        name=f"scatter{ident}",
    )(blocks)


def gather_dp(shard):
    size = lax.axis_size("dp")
    me = lax.axis_index("dp")
    pieces = [shard]
    for k in range(1, size):
        pieces.append(lax.ppermute(shard, "dp", [(i, (i + k) % size) for i in range(size)]))
    stacked = jnp.stack(pieces)
    return jnp.concatenate(
        [lax.dynamic_index_in_dim(stacked, (me - s) % size, 0, keepdims=True) for s in range(size)], 0
    )


def gather_plane(value):
    groups = lax.axis_size("expert")
    spread = jnp.broadcast_to(value[None], (groups,) + value.shape)
    return lax.all_to_all(spread, "expert", split_axis=0, concat_axis=0, tiled=True)


def reduce_banks(gradients, local_tree, trees_here, adapter_index, adapters):
    groups = lax.axis_size("expert")
    rank = gradients[0].shape[0]
    widths = [g.shape[1] for g in gradients]
    joined = jnp.concatenate(gradients, 1).astype(BF)
    if trees_here > 1:
        joined = jnp.where(
            (jnp.arange(trees_here) == local_tree)[:, None, None], joined[None], 0.0
        ).astype(BF)
    joined = joined.reshape(groups, -1)
    parts = lax.all_to_all(joined, "expert", split_axis=0, concat_axis=0, tiled=True)
    part = jnp.sum(parts.astype(F32), axis=0).astype(BF)
    lanes = gather_dp(part)
    full = gather_plane(lanes)
    trees = lax.axis_size("dp") * trees_here
    full = full.transpose(1, 0, 2).reshape(trees, rank, sum(widths))
    outs, at = [], 0
    for width in widths:
        piece = full[:, :, at : at + width].astype(F32)
        at += width
        outs.append(
            sum(
                jnp.where(
                    (jnp.arange(adapters) == adapter_index[t])[:, None, None], piece[t][None], 0.0
                )
                for t in range(trees)
            )
        )
    return outs


def body(
    tokens_in,
    cotangent,
    segment_id,
    parent_id,
    adapter_index,
    routes,
    mixer_gain,
    latent_gain,
    feed_gain,
    query_matrix,
    latent_down,
    latent_up,
    output_matrix,
    router_matrix,
    shared_in,
    shared_out,
    expert_in,
    expert_out,
    query_entry,
    query_exit,
    lower_entry,
    lower_exit,
    upper_entry,
    upper_exit,
    output_entry,
    output_exit,
):
    rows_here = tokens_in.shape[0]
    groups = lax.axis_size("expert")
    planes = lax.axis_size("dp")
    group_pos = lax.axis_index("expert")
    trees_here = segment_id.shape[0] // TREE
    local_tree = group_pos * rows_here // TREE
    tree_offset = group_pos * rows_here - local_tree * TREE
    chosen = adapter_index[lax.axis_index("dp") * trees_here + local_tree]
    query_in = select_slot(query_entry, chosen)
    qn_out, qr_out = split_heads(select_slot(query_exit, chosen))
    lower_in = select_slot(lower_entry, chosen)
    lower_out = select_slot(lower_exit, chosen)
    upper_in = select_slot(upper_entry, chosen)
    upper_out = select_slot(upper_exit, chosen)
    output_in = select_slot(output_entry, chosen)
    output_out = select_slot(output_exit, chosen)
    experts_all = router_matrix.shape[1]
    owned = expert_in.shape[0]
    capacity = max(2, 4 * rows_here * TOPK // (3 * experts_all))
    cap = -(-capacity // 8) * 8
    hidden_shared = shared_out.shape[0]
    both = ("dp", "expert")
    fast = groups == PLANE and planes == 4 and groups * rows_here == TREE and hidden_shared % 8 == 0

    weight_rows = query_matrix.shape[0]
    qn_here, qr_here = split_heads(query_matrix)
    front = jnp.concatenate([qn_here, qr_here, latent_down, router_matrix], 1)
    padded_shared = -(-planes * hidden_shared // 128) * 128
    fill = padded_shared - planes * hidden_shared
    cut = shared_in.reshape(weight_rows, 2, planes, groups, hidden_shared)
    cut = cut.transpose(3, 0, 1, 2, 4).reshape(groups, weight_rows, 2, planes * hidden_shared)
    cut = jnp.pad(cut, ((0, 0), (0, 0), (0, 0), (0, fill)))
    cut = cut.reshape(groups, weight_rows, 2 * padded_shared)
    if fast:
        lines = shared_out.reshape(hidden_shared // 8, 8, D)
        front, mix_up, mix_out, sh_in, sh_out = gather_blocks(
            [front, latent_up, output_matrix], planes, (4, 2, 2), 1, [cut], [lines]
        )
        front = front.reshape(D, -1)
        mix_up = mix_up.reshape(KVR, -1)
        mix_out = mix_out.reshape(-1, D)
    else:
        front = lax.all_gather(front, both, axis=0, tiled=True)
        mix_up = lax.all_gather(latent_up, both, axis=0, tiled=True)
        mix_out = lax.all_gather(output_matrix, both, axis=0, tiled=True)
        cut = lax.all_to_all(cut, "expert", split_axis=0, concat_axis=0, tiled=True)
        sh_in = gather_dp(cut.reshape(groups * weight_rows, -1))
        sh_out = gather_dp(shared_out)
    wide = HEADS * (NOPE + ROPE)
    feed_router = front[:, wide + KVR + ROPE :]

    sh_in = sh_in.reshape(D, 2 * padded_shared)
    sh_out = sh_out.reshape(planes * hidden_shared, D)
    sh_out = jnp.pad(sh_out, ((0, fill), (0, 0)))

    seg_tree = lax.dynamic_slice_in_dim(segment_id, local_tree * TREE, TREE)
    par_tree = lax.dynamic_slice_in_dim(parent_id, local_tree * TREE, TREE)
    key_index = jnp.arange(TREE, dtype=jnp.int32)
    start_pos = jnp.where(par_tree == 0, TRUNK, TRUNK + SEGLEN)
    key_pos = jnp.where(seg_tree == 0, key_index, start_pos + key_index % SEGLEN)
    row_pos = lax.dynamic_slice_in_dim(key_pos, tree_offset, rows_here)
    row_seg = lax.dynamic_slice_in_dim(seg_tree, tree_offset, rows_here)
    step = 128
    while rows_here % step:
        step //= 2
    nb = -(-(rows_here - step) // SEGLEN) + 1
    first_block = tree_offset // SEGLEN
    shift = tree_offset - first_block * SEGLEN
    seg_blocks = seg_tree.reshape(TREE // SEGLEN, SEGLEN)[:, 0]
    par_blocks = par_tree.reshape(TREE // SEGLEN, SEGLEN)[:, 0]
    own = jnp.minimum(first_block + jnp.arange(nb, dtype=jnp.int32), TREE // SEGLEN - 1)
    own_seg = seg_blocks[own]
    own_par = par_blocks[own]
    is_leaf = ((own_seg != 0) & (own_par != 0)).astype(jnp.int32)
    match = (seg_blocks[None, :] == own_par[:, None]) & (is_leaf[:, None] > 0)
    par_block = jnp.sum(
        jnp.where(match, jnp.arange(TREE // SEGLEN, dtype=jnp.int32)[None, :], 0), axis=1
    )
    info = jnp.concatenate([own, par_block, (own_seg != 0).astype(jnp.int32), is_leaf])
    query_limit = jnp.where(
        row_seg == 0, tree_offset + jnp.arange(rows_here, dtype=jnp.int32), TRUNK - 1
    )

    def pad_rows(value):
        empty = jnp.zeros((nb * SEGLEN,) + value.shape[1:], value.dtype)
        return lax.dynamic_update_slice_in_dim(empty, value, shift, 0)

    def cut_rows(value):
        return lax.dynamic_slice_in_dim(value, shift, rows_here, 0)

    inverse = 10000.0 ** (-(jnp.arange(HALF, dtype=F32) * 2.0 / ROPE))
    angles = row_pos.astype(F32)[:, None] * inverse[None, :]
    cos_half, sin_half = jnp.cos(angles), jnp.sin(angles)
    cosine = jnp.concatenate([cos_half, cos_half], -1)
    sine = jnp.concatenate([sin_half, sin_half], -1)
    cos_pair = pad_rows(jnp.concatenate([cos_half] * 4, -1))
    sin_pair = pad_rows(jnp.concatenate([-sin_half, -sin_half, sin_half, sin_half], -1))
    limit_rows = pad_rows(query_limit)

    mask = jnp.sum(
        (routes[:, :, None] == jnp.arange(experts_all, dtype=jnp.int32)).astype(F32), axis=1
    )
    lower = (
        jnp.arange(rows_here)[:, None] >= jnp.arange(rows_here)[None, :]
    ).astype(BF)
    slots_here = product(lower, mask.astype(BF)) * mask

    inputs = tokens_in.astype(F32)
    hidden = normed(inputs, mixer_gain).astype(BF)
    query_mid = product_t(hidden, query_in).astype(BF)
    lower_mid = product_t(hidden, lower_in).astype(BF)
    front_lin = product(hidden, front)
    latent_full = front_lin[:, wide : wide + KVR + ROPE] + product(lower_mid, lower_out)
    latent_raw = latent_full[:, :KVR]
    rope_raw = latent_full[:, KVR:]
    latent_norm = normed(latent_raw, latent_gain).astype(BF)
    key_rope = rotate(rope_raw, cosine, sine).astype(BF)
    upper_mid = product_t(latent_norm, upper_in).astype(BF)
    rank = upper_mid.shape[1]
    latent_ext = jnp.concatenate(
        [
            latent_norm,
            key_rope[:, :HALF],
            upper_mid,
            jnp.zeros((rows_here, HALF - rank), BF),
            key_rope[:, HALF:],
            jnp.zeros((rows_here, HALF), BF),
        ],
        1,
    )
    if fast:
        all_latent = gather_blocks([latent_ext], 1, (2,), 2)[0].reshape(TREE, LATW)
    else:
        all_latent = lax.all_gather(latent_ext, "expert", axis=0, tiled=True)
    tree_latent = lax.dynamic_slice_in_dim(all_latent, local_tree * TREE, TREE, 0)
    up_extra = jnp.concatenate(
        [
            jnp.zeros((HALF, mix_up.shape[1]), BF),
            upper_out,
            jnp.zeros((LATW - KVR - HALF - rank, mix_up.shape[1]), BF),
        ],
        0,
    )
    q_nope = pad_rows(
        (front_lin[:, : HEADS * NOPE] + product(query_mid, qn_out)).astype(BF)
    )
    q_rope = pad_rows(front_lin[:, HEADS * NOPE : wide] + product(query_mid, qr_out))
    grad_payload = jnp.concatenate(
        [cotangent, slots_here.astype(BF), jnp.zeros((rows_here, 128 - experts_all), BF)], 1
    )
    grad_payload, tree_latent = lax.optimization_barrier((grad_payload, tree_latent))
    all_grad = lax.all_gather(grad_payload, "expert", axis=0, tiled=True)

    attended, level, keys_values = attend(
        nb, info, q_nope, q_rope, cos_pair, sin_pair, limit_rows, tree_latent, mix_up, up_extra
    )
    attended = cut_rows(attended)
    output_mid = product_t(attended, output_in).astype(BF)
    mixed_state = inputs + product(attended, mix_out) + product(output_mid, output_out)
    feed_hidden = normed(mixed_state, feed_gain).astype(BF)
    logits = product(feed_hidden, feed_router)
    logit_peak = jnp.max(logits, axis=1, keepdims=True)
    logit_exp = jnp.exp(logits - logit_peak)
    router_probs = logit_exp / jnp.sum(logit_exp, axis=1, keepdims=True)

    my_slots = lax.dynamic_slice(all_grad, (0, D + group_pos * owned), (groups * rows_here, owned))
    slot_rows = jnp.pad(my_slots, ((0, 0), (0, 128 - owned)))
    slot_cols = my_slots.reshape(groups, rows_here, owned).transpose(0, 2, 1).astype(F32)
    grad_perm, grad_shared = spread_grad(all_grad, slot_cols, sh_out, cap)
    flat = (owned, groups * cap)
    grad_inner = expert_grads(grad_perm.reshape(*flat, D), expert_out)

    high = lax.reduce_precision(router_probs, 8, 7)
    feed_payload = jnp.concatenate(
        [feed_hidden, high.astype(BF), (router_probs - high).astype(BF)], 1
    )
    all_feed = lax.all_gather(feed_payload, "expert", axis=0, tiled=True)

    all_feed, grad_inner = lax.optimization_barrier((all_feed, grad_inner))

    def my_columns(start):
        return lax.dynamic_slice(
            all_feed, (0, start + group_pos * owned), (groups * rows_here, owned)
        ).astype(F32)

    my_probs = my_columns(D) + my_columns(D + experts_all)
    prob_cols = my_probs.reshape(groups, rows_here, owned).transpose(0, 2, 1)
    feed_perm, gates, inner_shared, gact_shared = spread_feed(
        all_feed, slot_cols, prob_cols, grad_shared, sh_in, cap
    )
    gates = gates.reshape(*flat, 128)
    slot_perm, inner = run_experts(
        (group_pos * owned).astype(jnp.int32).reshape(1),
        feed_perm.reshape(*flat, D),
        grad_inner,
        gates,
        expert_in,
        experts_all,
    )
    grad_part = collect(
        slot_perm.reshape(owned, groups, cap, D + 128), slot_rows, gact_shared, sh_in, True
    )
    grad_sum = lax.psum_scatter(grad_part, "expert", scatter_dimension=0, tiled=True)
    inner, grad_part = lax.optimization_barrier((inner, grad_part))
    rows_perm = expert_rows(inner, gates, expert_out)
    row_part = collect(
        rows_perm.reshape(owned, groups, cap, D), slot_rows, inner_shared, sh_out, False
    )
    row_sum = lax.psum_scatter(row_part, "expert", scatter_dimension=0, tiled=True)

    grad_output = cotangent.astype(F32)
    grad_sum = grad_sum.astype(F32)
    grad_probs = grad_sum[:, D : D + experts_all] + grad_sum[:, D + experts_all :]
    grad_logits = router_probs * (
        grad_probs - jnp.sum(router_probs * grad_probs, axis=1, keepdims=True)
    )
    grad_feed = grad_sum[:, :D] + product_t(grad_logits.astype(BF), feed_router)
    _, norm_two_back = jax.vjp(lambda operand: normed(operand, feed_gain), mixed_state)
    grad_mixed = grad_output + norm_two_back(grad_feed)[0]
    grad_attn = grad_mixed.astype(BF)
    grad_output_mid = product_t(grad_attn, output_out).astype(BF)
    grad_output_exit = product_left(output_mid, grad_attn)
    grad_output_entry = product_left(grad_output_mid, attended)
    grad_attended = (product_t(grad_attn, mix_out) + product(grad_output_mid, output_in)).astype(BF)

    delta = jnp.sum(
        (grad_attended.astype(F32) * attended.astype(F32)).reshape(rows_here, HEADS, VDIM), axis=2
    )
    padded = nb * SEGLEN
    stats = jnp.concatenate(
        [
            level[:, :2],
            pad_rows(delta).T.reshape(HEADS // 2, 2, padded),
            jnp.zeros((HEADS // 2, 4, padded), F32),
        ],
        1,
    )
    dq_nope, dq_rope, grad_up, grad_lat = attend_back(
        nb,
        info,
        q_nope,
        q_rope,
        cos_pair,
        sin_pair,
        limit_rows,
        tree_latent,
        keys_values,
        mix_up,
        up_extra,
        pad_rows(grad_attended),
        stats,
    )
    row_sum, dq_nope = lax.optimization_barrier((row_sum, dq_nope))
    block_output = (mixed_state + row_sum.astype(F32)).astype(BF)
    dq_nope, dq_rope = cut_rows(dq_nope), cut_rows(dq_rope)
    grad_upper_exit = grad_up[HALF : HALF + rank]
    grad_upper_mid = grad_lat[:, KVR + HALF : KVR + HALF + rank].astype(BF)
    grad_upper_entry = product_left(grad_upper_mid, tree_latent[:, :KVR])
    grad_tree = grad_lat[:, :KVR] + product(grad_upper_mid, upper_in)
    grad_tree = jnp.concatenate(
        [
            grad_tree,
            grad_lat[:, KVR : KVR + HALF],
            grad_lat[:, KVR + ROPE : KVR + ROPE + HALF],
            jnp.zeros((TREE, ROPE), F32),
        ],
        1,
    ).astype(BF)
    if trees_here > 1:
        grad_tree = lax.dynamic_update_slice_in_dim(
            jnp.zeros((groups * rows_here, grad_tree.shape[1]), BF), grad_tree, local_tree * TREE, 0
        )
    if fast:
        grad_latent = scatter_blocks(grad_tree.reshape(groups, rows_here, -1), 4, 5, F32)
    else:
        grad_latent = lax.psum_scatter(
            grad_tree, "expert", scatter_dimension=0, tiled=True
        ).astype(F32)
    _, latent_back = jax.vjp(lambda operand: normed(operand, latent_gain), latent_raw)
    _, key_back = jax.vjp(lambda operand: rotate(operand, cosine, sine), rope_raw)
    grad_latent_full = jnp.concatenate(
        [latent_back(grad_latent[:, :KVR])[0], key_back(grad_latent[:, KVR : KVR + ROPE])[0]], -1
    ).astype(BF)
    grad_lower_mid = product_t(grad_latent_full, lower_out).astype(BF)
    grad_lower_exit = product_left(lower_mid, grad_latent_full)
    grad_lower_entry = product_left(grad_lower_mid, hidden)
    dq_all = jnp.concatenate([dq_nope, dq_rope], 1)
    q_out = jnp.concatenate([qn_out, qr_out], 1)
    grad_query_mid = product_t(dq_all, q_out).astype(BF)
    grad_query_exit = product_left(query_mid, dq_all)
    grad_query_exit = join_heads(
        grad_query_exit[:, : HEADS * NOPE], grad_query_exit[:, HEADS * NOPE :]
    )
    grad_query_entry = product_left(grad_query_mid, hidden)
    grad_front = jnp.concatenate(
        [dq_all, grad_latent_full, jnp.zeros((rows_here, experts_all), BF)], 1
    )
    grad_hidden = (
        product_t(grad_front, front)
        + product(grad_query_mid, query_in)
        + product(grad_lower_mid, lower_in)
    )
    _, norm_one_back = jax.vjp(lambda operand: normed(operand, mixer_gain), inputs)
    grad_input = (grad_mixed + norm_one_back(grad_hidden)[0]).astype(BF)

    adapters = query_entry.shape[0]
    gradients = [
        grad_query_entry,
        grad_query_exit,
        grad_lower_entry,
        grad_lower_exit,
        grad_upper_entry,
        grad_upper_exit,
        grad_output_entry,
        grad_output_exit,
    ]
    if fast:
        offsets, pieces, at = [], [], 0
        for gradient in gradients:
            width = gradient.shape[1]
            offsets.append((at, width))
            pieces.append(jnp.pad(gradient, ((0, 0), (0, -width % 128))))
            at += width + -width % 128
        pieces.append(jnp.zeros((rank, -at % (128 * PLANE)), F32))
        joined = jnp.concatenate(pieces, 1).astype(BF)
        full = exchange_banks(joined, planes, 6)
        banks = place_banks(full, adapter_index, tuple(offsets), adapters)
    else:
        banks = reduce_banks(gradients, local_tree, trees_here, adapter_index, adapters)
    return (block_output, grad_input, *banks)


def solution(mesh):
    tokens = P(("dp", "expert"), None)
    in_specs = (
        tokens,
        tokens,
        P("dp"),
        P("dp"),
        P(),
        tokens,
        P(),
        P(),
        P(),
        *([tokens] * 7),
        P("expert", None, None),
        P("expert", None, None),
        *([P()] * 8),
    )
    out_specs = (tokens, tokens, *([P()] * 8))
    return jax.shard_map(body, mesh=mesh, in_specs=in_specs, out_specs=out_specs, check_vma=False)
```

```python
import functools

import jax
import jax.numpy as jnp
from jax import lax
from jax.experimental import pallas as pl
from jax.experimental.pallas import tpu as pltpu
from jax.sharding import PartitionSpec as P

D = 2048
HEADS = 16
NOPE = 128
ROPE = 64
VDIM = 128
KVR = 512
TOPK = 6
SEGLEN = 128
TRUNK = 1024
TREE = 2560
LATW = 640
HALF = ROPE // 2
VMEM_LIMIT = 66_000_000
BF = jnp.bfloat16
F32 = jnp.float32


def product(left, right):
    return jnp.dot(left, right, preferred_element_type=F32)


def product_t(left, right):
    return lax.dot_general(left, right, (((1,), (1,)), ((), ())), preferred_element_type=F32)


def product_left(left, right):
    return lax.dot_general(left, right, (((0,), (0,)), ((), ())), preferred_element_type=F32)


def normed(operand, gain):
    return operand * lax.rsqrt(jnp.mean(operand * operand, axis=-1, keepdims=True) + 1e-06) * gain


def rotate(operand, cosine, sine):
    half_width = operand.shape[-1] // 2
    turned = jnp.concatenate([-operand[..., half_width:], operand[..., :half_width]], -1)
    return operand * cosine + turned * sine


def select_slot(bank, chosen):
    return lax.dynamic_index_in_dim(bank, chosen, 0, keepdims=False)


def split_heads(matrix):
    rows = matrix.shape[0]
    three = matrix.reshape(rows, HEADS, NOPE + ROPE)
    nope = three[:, :, :NOPE].reshape(rows, HEADS * NOPE)
    rope = three[:, :, NOPE:].reshape(rows, HEADS // 2, 2, 2, HALF)
    return nope, rope.transpose(0, 1, 3, 2, 4).reshape(rows, HEADS * ROPE)


def join_heads(nope, rope):
    rows = nope.shape[0]
    turned = rope.reshape(rows, HEADS // 2, 2, 2, HALF).transpose(0, 1, 3, 2, 4)
    return jnp.concatenate(
        [nope.reshape(rows, HEADS, NOPE), turned.reshape(rows, HEADS, ROPE)], -1
    ).reshape(rows, HEADS * (NOPE + ROPE))


def lane_iota(shape):
    return lax.broadcasted_iota(jnp.int32, shape, len(shape) - 1)


def row_iota(shape):
    return lax.broadcasted_iota(jnp.int32, shape, len(shape) - 2)


LOG2E = 1.4426950408889634
SCALING = 1.0 / (NOPE + ROPE) ** 0.5


def place_keys(nb, info, lat, latsel):
    latsel[:TRUNK, :] = lat[:TRUNK, :]
    for m in range(nb):
        for side in range(2):
            start = pl.multiple_of(info[side * nb + m] * SEGLEN, SEGLEN)
            at = TRUNK + (2 * m + side) * SEGLEN
            latsel[at : at + SEGLEN, :] = lat[pl.ds(start, SEGLEN), :]


def rotary_keys(tail, kr):
    tail = tail.astype(F32)
    first = jnp.where(lane_iota(tail.shape) % ROPE < HALF, tail, 0.0)
    kr[0] = first.astype(BF)
    kr[1] = pltpu.roll(first, HALF, 1).astype(BF)


def local_limit(nb, info, m, key, row):
    return jnp.where(
        key < SEGLEN,
        (row + 1) * info[2 * nb + m] - 1,
        SEGLEN + SEGLEN * info[3 * nb + m] - 1,
    )


def attend_kernel(
    nb, info, qn, qr, cosp, sinp, qlim, lat, up, upx, out, lse, kv,
    latsel, kr, bias, near, st, sl, pt,
):
    rows_all = qn.shape[0]

    @pl.when(pl.program_id(0) == 0)
    def _():
        place_keys(nb, info, lat, latsel)
        rotary_keys(latsel[:, KVR:], kr)
        bias[...] = jnp.where(row_iota((TRUNK, rows_all)) <= qlim[...], 0.0, -1e30)
        key = row_iota((2 * SEGLEN, SEGLEN))
        row = lane_iota((2 * SEGLEN, SEGLEN))
        for m in range(nb):
            near[m] = jnp.where(key <= local_limit(nb, info, m, key, row), 0.0, -1e30)

    raw = qr[...]
    qrot = (raw * cosp[...] + pltpu.roll(raw, ROPE, 1) * sinp[...]).astype(BF)
    keys = latsel.shape[0]
    rows = keys // 2 if keys % 512 == 0 else keys
    for at in range(0, keys, rows):
        kv[at : at + rows, :] = (
            product(latsel[at : at + rows, :KVR], up[...])
            + product(latsel[at : at + rows, KVR:], upx[...])
        ).astype(BF)
    blocks = [slice(m * SEGLEN, (m + 1) * SEGLEN) for m in range(nb)]
    nears = [slice(TRUNK + 2 * m * SEGLEN, TRUNK + 2 * (m + 1) * SEGLEN) for m in range(nb)]
    chunks = [slice(at, at + 256) for at in range(0, TRUNK, 256)]
    peaks = []
    for a in range(2):
        q = jnp.concatenate([qn[:, a * 128 : a * 128 + 128], qrot], 1)
        k = jnp.concatenate([kv[:, a * 256 : a * 256 + 128], kr[a]], 1)
        peak = None
        for there in chunks:
            scores = product_t(k[there], q) + bias[there, :]
            st[a, there, :] = scores
            top = jnp.max(scores, axis=0, keepdims=True)
            peak = top if peak is None else jnp.maximum(peak, top)
        tops = []
        for m in range(nb):
            scores = product_t(k[nears[m]], q[blocks[m]]) + near[m]
            sl[a, m] = scores
            tops.append(jnp.max(scores, axis=0, keepdims=True))
        peak = jnp.maximum(peak, jnp.concatenate(tops, 1))
        peaks.append(peak * (SCALING * LOG2E))
    levels = []
    for a in range(2):
        v = kv[:, a * 256 + 128 : a * 256 + 256]
        total = None
        for there in chunks:
            e = jnp.exp2(st[a, there, :] * (SCALING * LOG2E) - peaks[a])
            part = jnp.sum(e, axis=0, keepdims=True)
            total = part if total is None else total + part
            pt[a, there, :] = e.astype(BF)
        parts, sums = [], []
        for m in range(nb):
            e = jnp.exp2(sl[a, m] * (SCALING * LOG2E) - peaks[a][:, blocks[m]])
            sums.append(jnp.sum(e, axis=0, keepdims=True))
            parts.append(product_left(e.astype(BF), v[nears[m]]))
        total = total + jnp.concatenate(sums, 1)
        got = product_left(pt[a], v[:TRUNK]) + jnp.concatenate(parts, 0)
        inverse = jnp.broadcast_to(1.0 / total, (128, rows_all)).T
        out[:, a * 128 : a * 128 + 128] = (got * inverse).astype(BF)
        levels.append(peaks[a] + jnp.log(total) * LOG2E)
    lse[0] = jnp.concatenate(levels + [jnp.zeros((6, rows_all), F32)], 0)


def attend_back_kernel(
    nb, info, qn, qr, cosp, sinp, qlim, tails, kv, up, upx, do, att, stats, upper,
    dqn, dqr, gup, dlow, tail, kr, bias, near, dss, dkv, acc, dkr, dlat,
):
    step = pl.program_id(0)
    rows_all = qn.shape[0]

    @pl.when(step == 0)
    def _():
        place_keys(nb, info, tails, tail)
        rotary_keys(tail[...], kr)
        bias[...] = jnp.where(row_iota((TRUNK, rows_all)) <= qlim[...], 0.0, -1e30)
        key = row_iota((2 * SEGLEN, SEGLEN))
        row = lane_iota((2 * SEGLEN, SEGLEN))
        for m in range(nb):
            near[m] = jnp.where(key <= local_limit(nb, info, m, key, row), 0.0, -1e30)
        acc[...] = jnp.zeros_like(acc)
        dkr[...] = jnp.zeros_like(dkr)

    raw = qr[...]
    qrot = (raw * cosp[...] + pltpu.roll(raw, ROPE, 1) * sinp[...]).astype(BF)
    dq_rope = None
    for a in range(2):
        q = jnp.concatenate([qn[:, a * 128 : a * 128 + 128], qrot], 1)
        k = jnp.concatenate([kv[:, a * 256 : a * 256 + 128], kr[a]], 1)
        v = kv[:, a * 256 + 128 : a * 256 + 256]
        g = do[:, a * 128 : a * 128 + 128]
        level = stats[0, a : a + 1, :]
        shares = g.astype(F32) * att[:, a * 128 : a * 128 + 128].astype(F32)
        main = shares.astype(BF)
        ones = jnp.ones((8, 128), BF)
        delta = product_t(ones, main) + product_t(ones, (shares - main.astype(F32)).astype(BF))
        delta = delta[:1]
        mine = lane_iota((1, 128)) % ROPE
        mine = (mine < HALF) if a == 0 else (mine >= HALF)

        def block(there, here, hide):
            scores = product_t(k[there], q[here]) + hide
            p = jnp.exp2(scores * (SCALING * LOG2E) - level[:, here])
            ds = (p * (product_t(v[there], g[here]) - delta[:, here])).astype(BF)
            dk = product(ds, q[here]) * SCALING
            dkv[there, a * 256 : a * 256 + 128] = dk[:, :128].astype(BF)
            dkv[there, a * 256 + 128 : a * 256 + 256] = product(p.astype(BF), g[here]).astype(BF)
            dkr[there, :] += jnp.where(mine, dk[:, 128:], 0.0)
            return ds

        for at in range(0, TRUNK, 256):
            there = slice(at, at + 256)
            dss[there, :] = block(there, slice(0, rows_all), bias[there, :])
        parts = []
        for m in range(nb):
            here = slice(m * SEGLEN, (m + 1) * SEGLEN)
            there = slice(TRUNK + 2 * m * SEGLEN, TRUNK + 2 * (m + 1) * SEGLEN)
            parts.append(product_left(block(there, here, near[m]), k[there]))
        dq = (product_left(dss[...], k[:TRUNK]) + jnp.concatenate(parts, 0)) * SCALING
        dqn[:, a * 128 : a * 128 + 128] = dq[:, :128].astype(BF)
        dq_rope = dq[:, 128:] if dq_rope is None else dq_rope + dq[:, 128:]
    dqr[...] = (dq_rope * cosp[...] + pltpu.roll(dq_rope * sinp[...], ROPE, 1)).astype(BF)
    gup[...] = product_left(tail[...], dkv[...])
    for at in range(0, tail.shape[0], 256):
        acc[at : at + 256, :KVR] += product_t(dkv[at : at + 256, :], up[...])
        acc[at : at + 256, KVR:] += product_t(dkv[at : at + 256, :], upx[...])

    @pl.when(step == pl.num_programs(0) - 1)
    def _():
        rope = dkr[...]
        folded = rope + pltpu.roll(rope, 128 - HALF, 1)
        keep = lane_iota(rope.shape) % ROPE < HALF
        acc[:, KVR:] += jnp.where(keep, folded, 0.0)
        dlat[:TRUNK, :] = acc[:TRUNK, :]
        dlat[TRUNK:, :] = jnp.zeros((TREE - TRUNK, LATW), F32)
        for m in range(nb):
            for side in range(2):
                start = pl.multiple_of(info[side * nb + m] * SEGLEN, SEGLEN)
                at = TRUNK + (2 * m + side) * SEGLEN
                dlat[pl.ds(start, SEGLEN), :] += acc[at : at + SEGLEN, :]
        low = dlat[:, KVR:].astype(BF)
        dlow[:, KVR:] = low
        dlow[:, :KVR] = (dlat[:, :KVR] + product(low, upper[...])).astype(BF)


def pair_spec(rows, width):
    return pl.BlockSpec((rows, width), lambda i, info: (0, i))


def lead_spec(rows, width):
    return pl.BlockSpec((1, rows, width), lambda i, info: (i, 0, 0))


def whole_spec(shape):
    return pl.BlockSpec(shape, lambda i, info: (0, 0))


def attend(nb, info, qn, qr, cosp, sinp, qlim, lat, up, upx):
    rows, keys = qn.shape[0], TRUNK + 2 * nb * SEGLEN
    return pl.pallas_call(
        functools.partial(attend_kernel, nb),
        out_shape=(
            jax.ShapeDtypeStruct((rows, HEADS * VDIM), BF),
            jax.ShapeDtypeStruct((HEADS // 2, 8, rows), F32),
            jax.ShapeDtypeStruct((keys, HEADS * (NOPE + VDIM)), BF),
        ),
        grid_spec=pltpu.PrefetchScalarGridSpec(
            num_scalar_prefetch=1,
            grid=(HEADS // 2,),
            in_specs=[
                pair_spec(rows, 256),
                pair_spec(rows, 128),
                whole_spec((rows, 128)),
                whole_spec((rows, 128)),
                whole_spec((1, rows)),
                whole_spec((TREE, LATW)),
                pair_spec(KVR, 512),
                pair_spec(LATW - KVR, 512),
            ],
            out_specs=(pair_spec(rows, 256), lead_spec(8, rows), pair_spec(keys, 512)),
            scratch_shapes=[
                pltpu.VMEM((keys, LATW), BF),
                pltpu.VMEM((2, keys, 128), BF),
                pltpu.VMEM((TRUNK, rows), F32),
                pltpu.VMEM((nb, 2 * SEGLEN, SEGLEN), F32),
                pltpu.VMEM((2, TRUNK, rows), F32),
                pltpu.VMEM((2, nb, 2 * SEGLEN, SEGLEN), F32),
                pltpu.VMEM((2, TRUNK, rows), BF),
            ],
        ),
        name="attend",
        **costs(30e9, 25e6),
    )(info, qn, qr, cosp, sinp, qlim[None, :], lat, up, upx)


def attend_back(nb, info, qn, qr, cosp, sinp, qlim, lat, kv, up, upx, do, att, stats, upper):
    rows, keys = qn.shape[0], TRUNK + 2 * nb * SEGLEN
    return pl.pallas_call(
        functools.partial(attend_back_kernel, nb),
        out_shape=(
            jax.ShapeDtypeStruct((rows, HEADS * NOPE), BF),
            jax.ShapeDtypeStruct((rows, HEADS * ROPE), BF),
            jax.ShapeDtypeStruct((128, HEADS * (NOPE + VDIM)), F32),
            jax.ShapeDtypeStruct((TREE, LATW), BF),
        ),
        grid_spec=pltpu.PrefetchScalarGridSpec(
            num_scalar_prefetch=1,
            grid=(HEADS // 2,),
            in_specs=[
                pair_spec(rows, 256),
                pair_spec(rows, 128),
                whole_spec((rows, 128)),
                whole_spec((rows, 128)),
                whole_spec((1, rows)),
                pl.BlockSpec((TREE, 128), lambda i, info: (0, KVR // 128)),
                pair_spec(keys, 512),
                pair_spec(KVR, 512),
                pair_spec(LATW - KVR, 512),
                pair_spec(rows, 256),
                pair_spec(rows, 256),
                lead_spec(8, rows),
                whole_spec((LATW - KVR, KVR)),
            ],
            out_specs=(
                pair_spec(rows, 256),
                pair_spec(rows, 128),
                pair_spec(128, 512),
                whole_spec((TREE, LATW)),
            ),
            scratch_shapes=[
                pltpu.VMEM((keys, 128), BF),
                pltpu.VMEM((2, keys, 128), BF),
                pltpu.VMEM((TRUNK, rows), F32),
                pltpu.VMEM((nb, 2 * SEGLEN, SEGLEN), F32),
                pltpu.VMEM((TRUNK, rows), BF),
                pltpu.VMEM((keys, 512), BF),
                pltpu.VMEM((keys, LATW), F32),
                pltpu.VMEM((keys, 128), F32),
                pltpu.VMEM((TREE, LATW), F32),
            ],
        ),
        name="attend_back",
        **costs(54e9, 30e6),
    )(info, qn, qr, cosp, sinp, qlim[None, :], lat, kv, up, upx, do, att, stats, upper)


def prepare_kernel(planes, query, down, router, shared, front, cut):
    wide = query[...].astype(F32)
    nope, rope = [], []
    for pair in range(HEADS // 2):
        starts = [(2 * pair + a) * (NOPE + ROPE) for a in range(2)]
        for at in starts:
            nope.append(wide[:, at : at + NOPE])
        for half in range(2):
            for at in starts:
                first = at + NOPE + half * HALF
                rope.append(wide[:, first : first + HALF])
    rest = [down[...].astype(F32), router[...].astype(F32)]
    front[...] = jnp.concatenate(nope + rope + rest, 1).astype(BF)
    whole = shared[...].astype(F32)
    groups, _, width = cut.shape
    hidden = whole.shape[1] // 2
    each = hidden // (planes * groups)
    blank = jnp.zeros((whole.shape[0], width // 2 - planes * each), F32)
    for j in range(groups):
        columns = []
        for part in range(2):
            for i in range(planes):
                at = part * hidden + (i * groups + j) * each
                columns.append(whole[:, at : at + each])
            columns.append(blank)
        cut[j] = jnp.concatenate(columns, 1).astype(BF)


def prepare(query, down, router, shared, planes, groups, padded):
    rows = query.shape[0]
    width = query.shape[1] + down.shape[1] + router.shape[1]
    return pl.pallas_call(
        functools.partial(prepare_kernel, planes),
        out_shape=(
            jax.ShapeDtypeStruct((rows, width), BF),
            jax.ShapeDtypeStruct((groups, rows, 2 * padded), BF),
        ),
        name="prepare",
        **costs(1e6, 3e6),
    )(query, down, router, shared)


def project_kernel(
    info, tokens, front, query_in, query_out, lower_in, lower_out, upper_in, mixer, gain, cos, sin,
    qn, qr, ext, raw, hidden, query_mid, lower_mid, acc,
):
    step = pl.program_id(0)

    @pl.when(step == 0)
    def _():
        hidden[...] = normed(tokens[...].astype(F32), mixer[...]).astype(BF)
        query_mid[...] = product_t(hidden[...], query_in[...]).astype(BF)
        lower_mid[...] = product_t(hidden[...], lower_in[...]).astype(BF)

    depth = front.shape[0]
    part = product(hidden[:, pl.ds(pl.multiple_of(step * depth, depth), depth)], front[...])

    @pl.when(step == 0)
    def _():
        acc[...] = part

    @pl.when(step > 0)
    def _():
        acc[...] += part

    @pl.when(step == pl.num_programs(0) - 1)
    def _():
        rows = hidden.shape[0]
        wide = HEADS * (NOPE + ROPE)
        middle = HEADS * NOPE
        here = pl.ds(pl.multiple_of(info[0], 16), rows)
        qn[...] = jnp.zeros_like(qn)
        qr[...] = jnp.zeros_like(qr)
        mid = query_mid[...]
        qn[here, :] = (acc[:, :middle] + product(mid, query_out[:, :middle])).astype(BF)
        qr[here, :] = acc[:, middle:wide] + product(mid, query_out[:, middle:])
        low = product(lower_mid[...], lower_out[...])
        latent = acc[:, wide : wide + KVR] + low[:, :KVR]
        raw[...] = latent
        norm = normed(latent, gain[...]).astype(BF)
        upper = product_t(norm, upper_in[...])
        key = acc[:, wide + KVR : wide + KVR + ROPE] + low[:, KVR:]
        first, second = key[:, :HALF], key[:, HALF:]
        c, s = cos[...], sin[...]
        ext[:, :KVR] = norm
        ext[:, KVR:] = jnp.concatenate(
            [
                first * c - second * s,
                upper,
                jnp.zeros((rows, HALF - upper.shape[1]), F32),
                second * c + first * s,
                jnp.zeros((rows, HALF), F32),
            ],
            1,
        ).astype(BF)


def fixed_at(value):
    return pl.BlockSpec(value.shape, lambda i, info: (0,) * value.ndim)


def whole_out(shape):
    return pl.BlockSpec(shape, lambda i, info: (0,) * len(shape))


def project(nb, shift, tokens, front, small):
    rows, depth = tokens.shape
    padded, step, rank = nb * SEGLEN, 512, small[0].shape[0]
    shapes = [
        ((padded, HEADS * NOPE), BF),
        ((padded, HEADS * ROPE), F32),
        ((rows, LATW), BF),
        ((rows, KVR), F32),
        ((rows, depth), BF),
        ((rows, rank), BF),
        ((rows, rank), BF),
    ]
    return pl.pallas_call(
        project_kernel,
        out_shape=[jax.ShapeDtypeStruct(shape, kind) for shape, kind in shapes],
        grid_spec=pltpu.PrefetchScalarGridSpec(
            num_scalar_prefetch=1,
            grid=(depth // step,),
            in_specs=[
                fixed_at(tokens),
                pl.BlockSpec((step, front.shape[1]), lambda i, info: (i, 0)),
                *[fixed_at(v) for v in small],
            ],
            out_specs=[whole_out(shape) for shape, _ in shapes],
            scratch_shapes=[pltpu.VMEM((rows, front.shape[1]), F32)],
        ),
        name="project",
        **costs(5e9, 20e6),
    )(shift, tokens, front, *small)


def mix_kernel(
    info, attended, tokens, matrix, router, out_in, out_out, gain,
    mixed, payload, probs, out_mid, acc,
):
    step = pl.program_id(0)
    rows = tokens.shape[0]
    here = pl.ds(pl.multiple_of(info[0], 16), rows)

    @pl.when(step == 0)
    def _():
        out_mid[...] = product_t(attended[here, :], out_in[...]).astype(BF)

    depth = matrix.shape[0]
    columns = pl.ds(pl.multiple_of(step * depth, depth), depth)
    part = product(attended[here, columns], matrix[...])

    @pl.when(step == 0)
    def _():
        acc[...] = part

    @pl.when(step > 0)
    def _():
        acc[...] += part

    @pl.when(step == pl.num_programs(0) - 1)
    def _():
        state = tokens[...].astype(F32) + (acc[...] + product(out_mid[...], out_out[...]))
        mixed[...] = state
        feed = normed(state, gain[...]).astype(BF)
        experts = probs.shape[1]
        logits = product(feed, router[...])[:, 128 - experts :]
        powers = jnp.exp(logits - jnp.max(logits, axis=1, keepdims=True))
        chance = powers / jnp.sum(powers, axis=1, keepdims=True)
        probs[...] = chance
        high = chance.astype(BF).astype(F32)
        payload[:, :D] = feed
        payload[:, D:] = jnp.concatenate([high, chance - high], 1).astype(BF)


def mix(shift, attended, tokens, matrix, front, out_in, out_out, gain, experts):
    rows = tokens.shape[0]
    step, rank = 512, out_in.shape[0]
    last = front.shape[1] // 128 - 1
    shapes = [((rows, D), F32), ((rows, D + 128), BF), ((rows, experts), F32), ((rows, rank), BF)]
    return pl.pallas_call(
        mix_kernel,
        out_shape=[jax.ShapeDtypeStruct(shape, kind) for shape, kind in shapes],
        grid_spec=pltpu.PrefetchScalarGridSpec(
            num_scalar_prefetch=1,
            grid=(D // step,),
            in_specs=[
                fixed_at(attended),
                fixed_at(tokens),
                pl.BlockSpec((step, D), lambda i, info: (i, 0)),
                pl.BlockSpec((D, 128), lambda i, info: (0, last)),
                fixed_at(out_in),
                fixed_at(out_out),
                fixed_at(gain),
            ],
            out_specs=[whole_out(shape) for shape, _ in shapes],
            scratch_shapes=[pltpu.VMEM((rows, D), F32)],
        ),
        name="mix",
        **costs(3e9, 14e6),
    )(shift, attended, tokens, matrix, front, out_in, out_out, gain)


def turn_kernel(
    info, sums, probs, mixed, cotangent, gain, router, out_in, out_out, matrix,
    grad_mixed, out_mid, do, low,
):
    rows = mixed.shape[0]

    @pl.when(pl.program_id(0) == 0)
    def _():
        experts = probs.shape[1]
        both = sums[:, D:].astype(F32)
        direct = both[:, :experts] + both[:, experts:]
        chance = probs[...]
        logits = chance * (direct - jnp.sum(chance * direct, axis=1, keepdims=True))
        spread = jnp.concatenate([jnp.zeros((rows, 128 - experts), F32), logits], 1).astype(BF)
        keep = jnp.where(lane_iota(router.shape) >= 128 - experts, router[...].astype(F32), 0.0)
        feed = sums[:, :D].astype(F32) + product_t(spread, keep.astype(BF))
        state = mixed[...]
        inverse = lax.rsqrt(jnp.mean(state * state, axis=-1, keepdims=True) + 1e-06)
        scaled = feed * gain[...]
        along = jnp.mean(scaled * state, axis=-1, keepdims=True)
        back = inverse * scaled - state * (inverse * inverse * inverse * along)
        total = cotangent[...].astype(F32) + back
        grad_mixed[...] = total
        low[...] = total.astype(BF)
        out_mid[...] = product_t(low[...], out_out[...]).astype(BF)

    here = pl.ds(pl.multiple_of(info[0], 16), rows)
    do[...] = jnp.zeros_like(do)
    do[here, :] = (
        product_t(low[...], matrix[...]) + product(out_mid[...], out_in[...])
    ).astype(BF)


def turn(nb, shift, sums, probs, mixed, cotangent, gain, front, out_in, out_out, matrix):
    rows, experts = probs.shape
    step, rank = 512, out_in.shape[0]
    last = front.shape[1] // 128 - 1
    padded = nb * SEGLEN
    return pl.pallas_call(
        turn_kernel,
        out_shape=[
            jax.ShapeDtypeStruct((rows, D), F32),
            jax.ShapeDtypeStruct((rows, rank), BF),
            jax.ShapeDtypeStruct((padded, D), BF),
        ],
        grid_spec=pltpu.PrefetchScalarGridSpec(
            num_scalar_prefetch=1,
            grid=(D // step,),
            in_specs=[
                fixed_at(sums),
                fixed_at(probs),
                fixed_at(mixed),
                fixed_at(cotangent),
                fixed_at(gain),
                pl.BlockSpec((D, 128), lambda i, info: (0, last)),
                pl.BlockSpec((rank, step), lambda i, info: (0, i)),
                fixed_at(out_out),
                pl.BlockSpec((step, D), lambda i, info: (i, 0)),
            ],
            out_specs=[
                whole_out((rows, D)),
                whole_out((rows, rank)),
                pl.BlockSpec((padded, step), lambda i, info: (0, i)),
            ],
            scratch_shapes=[pltpu.VMEM((rows, D), BF)],
        ),
        name="turn",
        **costs(3e9, 18e6),
    )(shift, sums, probs, mixed, cotangent, gain, front, out_in, out_out, matrix)


def join_kernel(
    offsets, info, dqn, dqr, query_out, query_mid, hidden, sums, raw, gain, cos, sin, lower_out,
    lower_mid, tree, lat, upper_exit, out_mid, mixed, grad_out_mid, attended,
    grads, joined, grad_query_mid, grad_lower_mid,
):
    rows = hidden.shape[0]
    here = pl.ds(pl.multiple_of(info[0], 16), rows)
    nope, rope = dqn[here, :], dqr[here, :]
    middle, wide = HEADS * NOPE, HEADS * (NOPE + ROPE)
    values = raw[...]
    inverse = lax.rsqrt(jnp.mean(values * values, axis=-1, keepdims=True) + 1e-06)
    scaled = sums[:, :KVR] * gain[...]
    along = jnp.mean(scaled * values, axis=-1, keepdims=True)
    latent = inverse * scaled - values * (inverse * inverse * inverse * along)
    first = sums[:, KVR : KVR + HALF]
    second = sums[:, KVR + ROPE : KVR + ROPE + HALF]
    c, s = cos[...], sin[...]
    key = jnp.concatenate(
        [first * c + second * s, second * c - first * s, jnp.zeros((rows, ROPE), F32)], 1
    )
    low = jnp.concatenate([latent, key], 1).astype(BF)
    grads[:, :middle] = nope
    grads[:, middle:wide] = rope
    grads[:, wide:] = low
    back_low = product_t(low[:, : KVR + ROPE], lower_out[...]).astype(BF)
    back_query = (
        product_t(nope, query_out[:, :middle]) + product_t(rope, query_out[:, middle:])
    ).astype(BF)
    grad_lower_mid[...] = back_low
    grad_query_mid[...] = back_query
    exit_nope = product_left(query_mid[...], nope)
    exit_rope = product_left(query_mid[...], rope)
    heads = []
    for head in range(HEADS):
        at = (head // 2) * 128 + (head % 2) * HALF
        heads += [
            exit_nope[:, head * NOPE : (head + 1) * NOPE],
            exit_rope[:, at : at + HALF],
            exit_rope[:, at + ROPE : at + ROPE + HALF],
        ]
    rank = back_low.shape[1]
    pieces = (
        product_left(back_query, hidden[...]),
        jnp.concatenate(heads, 1),
        product_left(back_low, hidden[...]),
        product_left(lower_mid[...], low),
        product_left(tree[:, KVR:], lat[:, :KVR])[HALF : HALF + rank],
        upper_exit[HALF : HALF + rank, :],
        product_left(grad_out_mid[...], attended[here, :]),
        product_left(out_mid[...], mixed[...].astype(BF)),
    )
    end = 0
    for (at, _), piece in zip(offsets, pieces):
        end = at + piece.shape[1]
        joined[:, at:end] = piece.astype(BF)
    joined[:, end:] = jnp.zeros((rank, joined.shape[1] - end), BF)


def join(offsets, total, shift, operands):
    hidden, query_mid = operands[4], operands[3]
    rows, rank = query_mid.shape
    wide = HEADS * (NOPE + ROPE) + KVR + 2 * ROPE
    shapes = [((rows, wide), BF), ((rank, total), BF), ((rows, rank), BF), ((rows, rank), BF)]
    return pl.pallas_call(
        functools.partial(join_kernel, offsets),
        out_shape=[jax.ShapeDtypeStruct(shape, kind) for shape, kind in shapes],
        grid_spec=pltpu.PrefetchScalarGridSpec(
            num_scalar_prefetch=1,
            grid=(1,),
            in_specs=[fixed_at(v) for v in operands],
            out_specs=[whole_out(shape) for shape, _ in shapes],
        ),
        name="join",
        **costs(3e9, 25e6),
    )(shift, *operands)


def gated_parts(gate, up):
    sig = 1.0 / (1.0 + jnp.exp(-gate))
    swish = gate * sig
    return swish * up, swish, up * (sig * (1.0 + gate * (1.0 - sig)))


def slot_matrix(slots, owned, cap, rows):
    wanted = row_iota((cap, rows)) + 1
    return [slots[e : e + 1, :] == wanted for e in range(owned)]


def spread_grad_kernel(owned, cap, pay, slots, sh_out, perm, gsh):
    rows = pay.shape[0]
    pick = slot_matrix(slots[0].astype(jnp.int32), owned, cap, rows)
    hot = jnp.concatenate([p.astype(F32) for p in pick], 0).astype(BF)
    values = pay[:, :D]
    got = product(hot, values)
    for e in range(owned):
        perm[e, 0] = got[e * cap : (e + 1) * cap].astype(BF)
    gsh[...] = product_t(values, sh_out[...])


def spread_feed_kernel(owned, cap, pay, slots, probs, gsh, sh_in, perm, gates, inner, gact):
    rows = pay.shape[0]
    pick = slot_matrix(slots[0].astype(jnp.int32), owned, cap, rows)
    hot = jnp.concatenate([p.astype(F32) for p in pick], 0).astype(BF)
    values = pay[:, :D]
    got = product(hot, values)
    for e in range(owned):
        perm[e, 0] = got[e * cap : (e + 1) * cap].astype(BF)
        gate = jnp.sum(jnp.where(pick[e], probs[0, e : e + 1, :], 0.0), axis=1, keepdims=True)
        gates[e, 0] = jnp.broadcast_to(gate, (cap, 128))
    width = gsh.shape[1]
    act = product(values, sh_in[...])
    value, by_up, by_gate = gated_parts(act[:, :width], act[:, width:])
    inner[...] = value.astype(BF)
    gact[:, :width] = (gsh[...] * by_gate).astype(BF)
    gact[:, width:] = (gsh[...] * by_up).astype(BF)


def expert_grad_kernel(g, w_out, back):
    hidden = w_out.shape[1]
    for at in range(0, hidden, 256):
        width = min(256, hidden - at)
        back[0, :, at : at + width] = product_t(g[0], w_out[0, at : at + width, :]).astype(BF)


def expert_kernel(experts, first, x, back, gates, w_in, slot_out, inner, ggu):
    hidden = back.shape[2]
    x_here = x[0]
    gate_here = gates[0][:, :1]
    total = jnp.zeros((x_here.shape[0], 1), F32)
    for at in range(0, hidden, 256):
        width = min(256, hidden - at)
        gate = product(x_here, w_in[0, :, at : at + width])
        up = product(x_here, w_in[0, :, hidden + at : hidden + at + width])
        value, by_up, by_gate = gated_parts(gate, up)
        low = value.astype(BF)
        inner[0, :, at : at + width] = low
        here = back[0, :, at : at + width].astype(F32)
        scaled = here * gate_here
        ggu[:, at : at + width] = (scaled * by_gate).astype(BF)
        ggu[:, hidden + at : hidden + at + width] = (scaled * by_up).astype(BF)
        total = total + jnp.sum(low.astype(F32) * here, axis=1, keepdims=True)
    for at in range(0, D, 256):
        slot_out[0, :, at : at + 256] = product_t(ggu[...], w_in[0, at : at + 256, :]).astype(BF)
    high = total.astype(BF).astype(F32)
    mine = first[0] + pl.program_id(0)
    lane = lane_iota((x_here.shape[0], slot_out.shape[2] - D))
    extra = jnp.where(lane == mine, high, jnp.where(lane == experts + mine, total - high, 0.0))
    slot_out[0, :, D:] = extra.astype(BF)


def expert_rows_kernel(inner, gates, w_out, rows_out):
    gate_here = gates[0][:, :1]
    for at in range(0, D, 256):
        rows = product(inner[0], w_out[0, :, at : at + 256]) * gate_here
        rows_out[0, :, at : at + 256] = rows.astype(BF)


def collect_kernel(owned, cap, rows_perm, slots, inner, weight, out, *, transposed):
    rows = out.shape[0]
    spread = (
        lane_iota((128, owned * cap)) // cap == row_iota((128, owned * cap))
    ).astype(F32).astype(BF)
    named = product(slots[...], spread)
    wanted = (lane_iota((rows, owned * cap)) % cap + 1).astype(F32)
    hot = (named == wanted).astype(F32).astype(BF)
    values = jnp.concatenate([rows_perm[e, 0].astype(F32) for e in range(owned)], 0).astype(BF)
    if transposed:
        shared = product_t(inner[...], weight[...])
    else:
        shared = product(inner[...], weight[...])
    out[:, :D] = (product(hot, values[:, :D]) + shared).astype(BF)
    if out.shape[1] > D:
        out[:, D:] = product(hot, values[:, D:]).astype(BF)


def row_block(rows, width):
    return pl.BlockSpec((rows, width), lambda b: (b, 0))


def fixed(shape):
    return pl.BlockSpec(shape, lambda b: (0,) * len(shape))


def token_block(owned, rows):
    return pl.BlockSpec((1, owned, rows), lambda b: (b, 0, 0))


def perm_block(owned, cap, width):
    return pl.BlockSpec((owned, 1, cap, width), lambda b: (0, b, 0, 0))


def costs(flops, moved):
    return dict(
        compiler_params=pltpu.CompilerParams(
            vmem_limit_bytes=VMEM_LIMIT
        ),
        cost_estimate=pl.CostEstimate(
            flops=int(flops), bytes_accessed=int(moved), transcendentals=0
        ),
    )


def spread_grad(payload, slots, sh_out, cap):
    groups, owned, rows = slots.shape
    width = sh_out.shape[0]
    return pl.pallas_call(
        functools.partial(spread_grad_kernel, owned, cap),
        grid=(groups,),
        out_shape=(
            jax.ShapeDtypeStruct((owned, groups, cap, D), BF),
            jax.ShapeDtypeStruct((groups * rows, width), F32),
        ),
        in_specs=[
            row_block(rows, payload.shape[1]),
            token_block(owned, rows),
            fixed(sh_out.shape),
        ],
        out_specs=(perm_block(owned, cap, D), row_block(rows, width)),
        name="spread_grad",
        **costs(12e9, 28e6),
    )(payload, slots, sh_out)


def spread_feed(payload, slots, probs, gsh, sh_in, cap):
    groups, owned, rows = slots.shape
    width = gsh.shape[1]
    return pl.pallas_call(
        functools.partial(spread_feed_kernel, owned, cap),
        grid=(groups,),
        out_shape=(
            jax.ShapeDtypeStruct((owned, groups, cap, D), BF),
            jax.ShapeDtypeStruct((owned, groups, cap, 128), F32),
            jax.ShapeDtypeStruct((groups * rows, width), BF),
            jax.ShapeDtypeStruct((groups * rows, 2 * width), BF),
        ),
        in_specs=[
            row_block(rows, payload.shape[1]),
            token_block(owned, rows),
            token_block(owned, rows),
            row_block(rows, width),
            fixed(sh_in.shape),
        ],
        out_specs=(
            perm_block(owned, cap, D),
            perm_block(owned, cap, 128),
            row_block(rows, width),
            row_block(rows, 2 * width),
        ),
        name="spread_feed",
        **costs(14e9, 28e6),
    )(payload, slots, probs, gsh, sh_in)


def row_chunk(rows):
    count = 1
    while rows // count > 384 or rows % count or rows // count % 8:
        count += 1
    return rows // count


def expert_specs(owned, rows):
    chunk = row_chunk(rows)

    def at(width):
        return pl.BlockSpec((1, chunk, width), lambda e, i, *_: (e, i, 0))

    def weight(shape):
        return pl.BlockSpec((1,) + shape, lambda e, i, *_: (e, 0, 0))

    return (owned, rows // chunk), chunk, at, weight


def expert_grads(g, w_out):
    owned, rows, _ = g.shape
    hidden = w_out.shape[1]
    grid, _, at, weight = expert_specs(owned, rows)
    return pl.pallas_call(
        expert_grad_kernel,
        out_shape=jax.ShapeDtypeStruct((owned, rows, hidden), BF),
        grid=grid,
        in_specs=[at(D), weight((hidden, D))],
        out_specs=at(hidden),
        name="expert_grads",
        **costs(2 * owned * rows * D * hidden, owned * (D * hidden * 2 + rows * D * 4)),
    )(g, w_out)


def run_experts(first, x, back, gates, w_in, experts):
    owned, rows, _ = x.shape
    hidden = back.shape[2]
    grid, chunk, at, weight = expert_specs(owned, rows)
    return pl.pallas_call(
        functools.partial(expert_kernel, experts),
        out_shape=(
            jax.ShapeDtypeStruct((owned, rows, D + 128), BF),
            jax.ShapeDtypeStruct((owned, rows, hidden), BF),
        ),
        grid_spec=pltpu.PrefetchScalarGridSpec(
            num_scalar_prefetch=1,
            grid=grid,
            in_specs=[at(D), at(hidden), at(128), weight((D, 2 * hidden))],
            out_specs=(at(D + 128), at(hidden)),
            scratch_shapes=[pltpu.VMEM((chunk, 2 * hidden), BF)],
        ),
        name="experts",
        **costs(8 * owned * rows * D * hidden, owned * D * hidden * 4),
    )(first, x, back, gates, w_in)


def expert_rows(inner, gates, w_out):
    owned, rows, hidden = inner.shape
    grid, _, at, weight = expert_specs(owned, rows)
    return pl.pallas_call(
        expert_rows_kernel,
        out_shape=jax.ShapeDtypeStruct((owned, rows, D), BF),
        grid=grid,
        in_specs=[at(hidden), at(128), weight((hidden, D))],
        out_specs=at(D),
        name="expert_rows",
        **costs(2 * owned * rows * D * hidden, owned * (D * hidden * 2 + rows * D * 4)),
    )(inner, gates, w_out)


def collect(rows_perm, slots, inner, weight, transposed):
    owned, groups, cap, width = rows_perm.shape
    rows = slots.shape[0] // groups
    return pl.pallas_call(
        functools.partial(collect_kernel, owned, cap, transposed=transposed),
        grid=(groups,),
        out_shape=jax.ShapeDtypeStruct((groups * rows, width), BF),
        in_specs=[
            perm_block(owned, cap, width),
            row_block(rows, 128),
            row_block(rows, inner.shape[1]),
            fixed(weight.shape),
        ],
        out_specs=row_block(rows, width),
        name="collect_grad" if transposed else "collect_rows",
        **costs(14e9, 28e6),
    )(rows_perm, slots, inner, weight)


MESH = pl.DeviceIdType.MESH
PLANE = 8


def neighbours():
    e = lax.axis_index("expert")
    core, x, y = e % 2, (e // 2) % 2, e // 4
    return e, 1 - 2 * core, 2 - 4 * x, 4 - 8 * y


def remote(src, dst, send_sem, recv_sem, **where):
    return pltpu.make_async_remote_copy(
        src_ref=src,
        dst_ref=dst,
        send_sem=send_sem,
        recv_sem=recv_sem,
        device_id=where,
        device_id_type=MESH,
    )


def greet(plane, levels):
    barrier = pltpu.get_barrier_semaphore()
    for who in plane:
        pl.semaphore_signal(barrier, inc=1, device_id={"expert": who}, device_id_type=MESH)
    for level in levels:
        pl.semaphore_signal(barrier, inc=1, device_id={"dp": level}, device_id_type=MESH)
    pl.semaphore_wait(barrier, len(plane) + len(levels))


class Mail:
    def __init__(self):
        self.sent = []

    def start(self, src, dst, pair, index, **where):
        copy = remote(src, dst, pair[0].at[index], pair[1].at[index], **where)
        copy.start()
        self.sent.append((None, copy))

    def arrived(self, dst, pair, index):
        here = neighbours()[0]
        remote(dst, dst, pair[0].at[index], pair[1].at[index], expert=here).wait_recv()

    def along(self, level, planes, src, dst, pair, index):
        z = lax.axis_index("dp")
        for way, fits, ahead in (
            (0, (level <= z) & (z < planes - 1), z + 1),
            (1, (level >= z) & (z > 0), z - 1),
        ):
            copy = remote(src, dst, pair[0].at[(way, *index)], pair[1].at[index], dp=ahead)
            pl.when(fits)(copy.start)
            self.sent.append((fits, copy))

    def line_arrived(self, dst, pair, index):
        here = neighbours()[0]
        remote(dst, dst, pair[0].at[(0, *index)], pair[1].at[index], expert=here).wait_recv()

    def drain(self):
        for fits, copy in self.sent:
            if fits is None:
                copy.wait_send()
            else:
                pl.when(fits)(copy.wait_send)


def nearest_levels(planes):
    if planes == 1:
        return [0]
    z = lax.axis_index("dp")
    power = 1 + 3 * z + 9 * (z * (z - 1) // 2) + 27 * (z * (z - 1) * (z - 2) // 6)
    order = ((1, 2, 3), (0, 2, 3), (1, 3, 0), (2, 1, 0))
    packed = [sum(order[at][m] * 4**at for at in range(4)) for m in range(3)]
    return [z] + [(code // power) % 4 for code in packed]


def spread_pieces(planes, count, source, place, mail, sems, meanwhile=None):
    line, by_x, by_y, by_far, by_core = [sems[2 * n : 2 * n + 2] for n in range(5)]
    e, to_core, to_x, to_y = neighbours()
    levels = nearest_levels(planes)
    partner, xn, yn, dg = e + to_core, e + to_x, e + to_y, e + to_x + to_y

    def at(k, who, i):
        return place(levels[k], who, i)

    def stage_a(k):
        for i in range(count):
            here = at(k, e, i)
            src = source(i) if k == 0 else here
            if k:
                mail.line_arrived(here, line, (levels[k], i))
            if planes > 1:
                mail.along(levels[k], planes, src, here, line, (levels[k], i))
            if i % 2 == 0:
                mail.start(src, here, by_x, (k, i), expert=xn)
                mail.start(src, here, by_y, (k, i), expert=yn)
            else:
                mail.start(src, here, by_y, (k, i), expert=yn)
                mail.start(src, here, by_x, (k, i), expert=xn)
            mail.start(src, here, by_core, (0, k, i), expert=partner)

    def stage_b(k):
        for i in range(count):
            left, up = at(k, xn, i), at(k, yn, i)
            mail.arrived(left, by_x, (k, i))
            if i % 2 == 0:
                mail.start(left, left, by_far, (k, i), expert=yn)
            mail.start(left, left, by_core, (1, k, i), expert=partner)
            mail.arrived(up, by_y, (k, i))
            if i % 2:
                mail.start(up, up, by_far, (k, i), expert=xn)
            mail.start(up, up, by_core, (2, k, i), expert=partner)

    def stage_c(k):
        for i in range(count):
            here = at(k, dg, i)
            mail.arrived(here, by_far, (k, i))
            mail.start(here, here, by_core, (3, k, i), expert=partner)

    for s in range(planes + 2):
        if s < planes:
            stage_a(s)
        if meanwhile is not None:
            meanwhile(s)
        if 0 <= s - 1 < planes:
            stage_b(s - 1)
        if 0 <= s - 2:
            stage_c(s - 2)
    for k in range(planes):
        for n, who in enumerate((e, xn, yn, dg)):
            for i in range(count):
                mail.arrived(at(k, who + to_core, i), by_core, (n, k, i))


def spread_sems(planes, count):
    dma = pltpu.SemaphoreType.DMA
    each, core = dma((planes, count)), dma((4, planes, count))
    return [dma((2, planes, count)), *([each] * 7), core, core]


def plane_peers(swaps):
    e, to_core, to_x, to_y = neighbours()
    if swaps:
        return [(e + j) % PLANE for j in range(1, PLANE)]
    return [e + to_core, e + to_x, e + to_y]


def other_levels(planes):
    if planes == 1:
        return []
    z = lax.axis_index("dp")
    return [(z + k) % planes for k in range(1, planes)]


def swap_out(mail, src, landing, pair, n):
    e = neighbours()[0]
    for j in range(1, PLANE):
        who = (e + j) % PLANE
        mail.start(src(who), landing(e), pair, (n, j - 1), expert=who)


def swap_in(mail, landing, pair, n):
    e = neighbours()[0]
    for j in range(1, PLANE):
        mail.arrived(landing((e + PLANE - j) % PLANE), pair, (n, j - 1))


def gather_kernel(planes, depth, pieces, count, swaps, lines, *refs):
    total = count + swaps + lines
    shards, outs = refs[:total], refs[total : 2 * total]
    sems = refs[2 * total :]
    own_sem, swap, line = sems[10], sems[11:13], sems[13:15]
    e = neighbours()[0]
    levels = nearest_levels(depth)
    z = levels[0]
    mail = Mail()
    greet(plane_peers(swaps), other_levels(depth))
    home = z if planes > 1 else 0

    def place(level, who, i):
        array, first, rows = pieces[i]
        return outs[array].at[level, who, pl.ds(first, rows)]

    def source(i):
        array, first, rows = pieces[i]
        return shards[array].at[pl.ds(first, rows)]

    mine = [pltpu.make_async_copy(shards[a], outs[a].at[home, e], own_sem.at[a]) for a in range(count)]
    for a in range(count, count + swaps):
        mine.append(pltpu.make_async_copy(shards[a].at[e], outs[a].at[z, e], own_sem.at[a]))
    for a in range(count + swaps, total):
        mine.append(pltpu.make_async_copy(shards[a], outs[a].at[z], own_sem.at[a]))
    for copy in mine:
        copy.start()
    for n in range(swaps):
        a = count + n
        swap_out(
            mail, lambda who: shards[a].at[who], lambda who: outs[a].at[z, who], swap, n
        )
    cuts = []
    for a in range(count, total):
        size = outs[a].shape[1]
        half = size // 2
        cuts += [(a, pl.ds(0, half)), (a, pl.ds(half, size - half))]

    def line_step(k):
        for i, (a, rows) in enumerate(cuts):
            here = outs[a].at[levels[k], rows]
            src = here if k or a < count + swaps else shards[a].at[rows]
            if k:
                mail.line_arrived(here, line, (levels[k], i))
            mail.along(levels[k], depth, src, here, line, (levels[k], i))

    first = 2 if planes > 1 else 0

    def meanwhile(s):
        if s == 1:
            for n in range(swaps):
                a = count + n
                swap_in(mail, lambda who: outs[a].at[z, who], swap, n)
                mine[a].wait()
        if 0 <= s - first < depth:
            line_step(s - first)

    spread_pieces(
        planes, len(pieces), source, place, mail, sems, meanwhile if cuts else None
    )
    if cuts:
        for k in range(planes + 2 - first, depth):
            line_step(k)
    for n, copy in enumerate(mine):
        if not count <= n < count + swaps:
            copy.wait()
    mail.drain()


def gather_blocks(shards, planes, cuts, ident, swaps=(), lines=(), depth=None):
    dma = pltpu.SemaphoreType.DMA
    depth = planes if depth is None else depth
    pieces = []
    for array, (shard, cut) in enumerate(zip(shards, cuts)):
        rows = shard.shape[0] // cut
        pieces += [(array, at * rows, rows) for at in range(cut)]
    count, total = len(shards), len(shards) + len(swaps) + len(lines)
    shapes = [jax.ShapeDtypeStruct((planes, PLANE) + s.shape, s.dtype) for s in shards]
    shapes += [jax.ShapeDtypeStruct((depth,) + s.shape, s.dtype) for s in [*swaps, *lines]]
    return pl.pallas_call(
        functools.partial(
            gather_kernel, planes, depth, pieces, count, len(swaps), len(lines)
        ),
        out_shape=shapes,
        in_specs=[pl.BlockSpec(memory_space=pl.ANY)] * total,
        out_specs=[pl.BlockSpec(memory_space=pl.ANY)] * total,
        scratch_shapes=[
            *spread_sems(planes, len(pieces)),
            dma((total,)),
            dma((max(1, len(swaps)), PLANE - 1)),
            dma((max(1, len(swaps)), PLANE - 1)),
            dma((2, depth, max(1, 2 * (total - count)))),
            dma((depth, max(1, 2 * (total - count)))),
        ],
        compiler_params=pltpu.CompilerParams(collective_id=ident, has_side_effects=True),
        name=f"gather{ident}",
    )(*shards, *swaps, *lines)


def bank_kernel(
    planes, wide, parts, front, grads, query_mid, lower_mid, query_in, lower_in, tokens, gain, mixed,
    out, result, landing, part, hold, back, hold_sem, *sems,
):
    e = neighbours()[0]
    z = lax.axis_index("dp")
    mail = Mail()
    swap = sems[10:12]
    step = hold.shape[1]
    steps = D // step

    def fetch(n):
        return pltpu.make_async_copy(
            front.at[pl.ds(n * step, step)], hold.at[n % 2], hold_sem.at[n % 2]
        )

    def multiply(n):
        fetch(n).wait()
        columns = slice(n * step, (n + 1) * step)
        back[:, columns] = (
            product_t(grads[...], hold[n % 2])
            + product(query_mid[...], query_in[:, columns])
            + product(lower_mid[...], lower_in[:, columns])
        )
        if n + 2 < steps:
            fetch(n + 2).start()

    def finish():
        values = tokens[...].astype(F32)
        inverse = lax.rsqrt(jnp.mean(values * values, axis=-1, keepdims=True) + 1e-06)
        scaled = back[...] * gain[...]
        along = jnp.mean(scaled * values, axis=-1, keepdims=True)
        change = inverse * scaled - values * (inverse * inverse * inverse * along)
        result[...] = (mixed[...] + change).astype(BF)

    for n in range(2):
        fetch(n).start()
    greet(plane_peers(1), other_levels(planes))

    def chunk(who):
        return pl.ds(pl.multiple_of(who * wide, 128), wide)

    swap_out(mail, lambda who: parts.at[:, chunk(who)], lambda who: landing.at[who], swap, 0)
    early = steps - planes
    for n in range(early):
        multiply(n)
    total = parts[:, chunk(e)].astype(F32)
    for j in range(1, PLANE):
        who = (e + PLANE - j) % PLANE
        mail.arrived(landing.at[who], swap, (0, j - 1))
        total = total + landing[who].astype(F32)
    low = total.astype(BF)
    part[...] = low
    out[z, e] = low

    def meanwhile(s):
        if s < planes:
            multiply(early + s)
        if s == planes:
            finish()

    spread_pieces(
        planes, 1, lambda i: part, lambda level, who, i: out.at[level, who], mail, sems, meanwhile
    )
    mail.drain()


def exchange_banks(joined, planes, ident, front, operands):
    rank, width = joined.shape
    wide = width // PLANE
    rows = operands[0].shape[0]
    dma = pltpu.SemaphoreType.DMA
    vmem = pl.BlockSpec(memory_space=pltpu.VMEM)
    return pl.pallas_call(
        functools.partial(bank_kernel, planes, wide),
        out_shape=[
            jax.ShapeDtypeStruct((planes, PLANE, rank, wide), BF),
            jax.ShapeDtypeStruct((rows, D), BF),
        ],
        in_specs=[vmem, pl.BlockSpec(memory_space=pl.ANY), *([vmem] * len(operands))],
        out_specs=[vmem, vmem],
        scratch_shapes=[
            pltpu.VMEM((PLANE, rank, wide), BF),
            pltpu.VMEM((rank, wide), BF),
            pltpu.VMEM((2, 256, front.shape[1]), BF),
            pltpu.VMEM((rows, D), F32),
            dma((2,)),
            *spread_sems(planes, 1),
            dma((1, PLANE - 1)),
            dma((1, PLANE - 1)),
        ],
        compiler_params=pltpu.CompilerParams(
            collective_id=ident, has_side_effects=True, vmem_limit_bytes=VMEM_LIMIT
        ),
        name=f"banks{ident}",
    )(joined, front, *operands)


def place_kernel(trees, offsets, chosen, full, *outs):
    slot = pl.program_id(0)
    wide = full.shape[3]
    for n, (at, width) in enumerate(offsets):
        total = jnp.zeros(outs[n].shape[1:], F32)
        for t in range(trees):
            pick = (chosen[t] == slot).astype(F32)
            columns = []
            while sum(c.shape[1] for c in columns) < width:
                here = at + sum(c.shape[1] for c in columns)
                first = here % wide
                upto = min(wide, first + at + width - here)
                columns.append(full[t, here // wide, :, first:upto].astype(F32))
            total = total + pick * jnp.concatenate(columns, 1)
        outs[n][0] = total


def place_banks(full, adapter_index, offsets, adapters):
    trees, _, rank, _ = full.shape
    return pl.pallas_call(
        functools.partial(place_kernel, trees, offsets),
        out_shape=[jax.ShapeDtypeStruct((adapters, rank, w), F32) for _, w in offsets],
        grid_spec=pltpu.PrefetchScalarGridSpec(
            num_scalar_prefetch=1,
            grid=(adapters,),
            in_specs=[pl.BlockSpec(full.shape, lambda a, chosen: (0, 0, 0, 0))],
            out_specs=[pl.BlockSpec((1, rank, w), lambda a, chosen: (a, 0, 0)) for _, w in offsets],
        ),
        name="place_banks",
        **costs(1e6, 11e6),
    )(adapter_index, full)


def scatter_kernel(parts, blocks, out, core_in, x_in, y_in, chip, total, sends, sems):
    e, to_core, to_x, to_y = neighbours()
    partner, xn, yn, dg = e + to_core, e + to_x, e + to_y, e + to_x + to_y
    rows = out.shape[0] // parts
    half = parts // 2
    greet((partner, xn, yn), [])
    mail, pair = Mail(), (sends, sems)

    def start(src, dst, index, **where):
        mail.start(src, dst, pair, index, **where)

    def arrived(dst, index):
        mail.arrived(dst, pair, index)

    def cut(p):
        return pl.ds(p * rows, rows)

    order = [p // 2 + (p % 2) * half for p in range(parts)]
    whose = (0, to_x, to_y, to_x + to_y)
    for p in order:
        for b in (3, 1, 2, 0):
            start(
                blocks.at[partner + whose[b], cut(p)],
                core_in.at[b, cut(p)],
                (b, p),
                expert=partner,
            )

    def add_chip(p):
        for b in (3, 1, 2, 0):
            arrived(core_in.at[b, cut(p)], (b, p))
            chip[b, cut(p), :] = (
                blocks[e + whose[b], cut(p), :].astype(F32) + core_in[b, cut(p), :].astype(F32)
            ).astype(BF)

    def first_hop(p):
        if p < half:
            start(chip.at[3, cut(p)], x_in.at[1, cut(p)], (5, p), expert=xn)
            start(chip.at[1, cut(p)], x_in.at[0, cut(p)], (4, p), expert=xn)
        else:
            start(chip.at[3, cut(p)], x_in.at[1, cut(p)], (5, p), expert=yn)
            start(chip.at[2, cut(p)], x_in.at[0, cut(p)], (4, p), expert=yn)

    def add_first(p):
        passed = 2 if p < half else 1
        arrived(x_in.at[1, cut(p)], (5, p))
        chip[passed, cut(p), :] = (
            chip[passed, cut(p), :].astype(F32) + x_in[1, cut(p), :].astype(F32)
        ).astype(BF)
        arrived(x_in.at[0, cut(p)], (4, p))
        total[cut(p), :] = chip[0, cut(p), :].astype(F32) + x_in[0, cut(p), :].astype(F32)

    def second_hop(p):
        if p < half:
            start(chip.at[2, cut(p)], y_in.at[cut(p)], (6, p), expert=yn)
        else:
            start(chip.at[1, cut(p)], y_in.at[cut(p)], (6, p), expert=xn)

    def finish(p):
        arrived(y_in.at[cut(p)], (6, p))
        out[cut(p), :] = (total[cut(p), :] + y_in[cut(p), :].astype(F32)).astype(out.dtype)

    for n, p in enumerate(order):
        add_chip(p)
        if n:
            first_hop(order[n - 1])
    first_hop(order[-1])
    for n, p in enumerate(order):
        add_first(p)
        if n:
            second_hop(order[n - 1])
    second_hop(order[-1])
    for p in order:
        finish(p)
    mail.drain()


def scatter_blocks(blocks, parts, ident, dtype):
    _, rows, width = blocks.shape
    dma = pltpu.SemaphoreType.DMA
    vmem = pl.BlockSpec(memory_space=pltpu.VMEM)
    return pl.pallas_call(
        functools.partial(scatter_kernel, parts),
        out_shape=jax.ShapeDtypeStruct((rows, width), dtype),
        in_specs=[vmem],
        out_specs=vmem,
        scratch_shapes=[
            pltpu.VMEM((4, rows, width), BF),
            pltpu.VMEM((2, rows, width), BF),
            pltpu.VMEM((rows, width), BF),
            pltpu.VMEM((4, rows, width), BF),
            pltpu.VMEM((rows, width), F32),
            dma((7, parts)),
            dma((7, parts)),
        ],
        compiler_params=pltpu.CompilerParams(
            collective_id=ident, has_side_effects=True, vmem_limit_bytes=VMEM_LIMIT
        ),
        name=f"scatter{ident}",
    )(blocks)


def gather_dp(shard):
    size = lax.axis_size("dp")
    me = lax.axis_index("dp")
    pieces = [shard]
    for k in range(1, size):
        pieces.append(lax.ppermute(shard, "dp", [(i, (i + k) % size) for i in range(size)]))
    stacked = jnp.stack(pieces)
    return jnp.concatenate(
        [lax.dynamic_index_in_dim(stacked, (me - s) % size, 0, keepdims=True) for s in range(size)], 0
    )


def gather_plane(value):
    groups = lax.axis_size("expert")
    spread = jnp.broadcast_to(value[None], (groups,) + value.shape)
    return lax.all_to_all(spread, "expert", split_axis=0, concat_axis=0, tiled=True)


def reduce_banks(gradients, local_tree, trees_here, adapter_index, adapters):
    groups = lax.axis_size("expert")
    rank = gradients[0].shape[0]
    widths = [g.shape[1] for g in gradients]
    joined = jnp.concatenate(gradients, 1).astype(BF)
    if trees_here > 1:
        joined = jnp.where(
            (jnp.arange(trees_here) == local_tree)[:, None, None], joined[None], 0.0
        ).astype(BF)
    joined = joined.reshape(groups, -1)
    parts = lax.all_to_all(joined, "expert", split_axis=0, concat_axis=0, tiled=True)
    part = jnp.sum(parts.astype(F32), axis=0).astype(BF)
    lanes = gather_dp(part)
    full = gather_plane(lanes)
    trees = lax.axis_size("dp") * trees_here
    full = full.transpose(1, 0, 2).reshape(trees, rank, sum(widths))
    outs, at = [], 0
    for width in widths:
        piece = full[:, :, at : at + width].astype(F32)
        at += width
        outs.append(
            sum(
                jnp.where(
                    (jnp.arange(adapters) == adapter_index[t])[:, None, None], piece[t][None], 0.0
                )
                for t in range(trees)
            )
        )
    return outs


def body(
    tokens_in,
    cotangent,
    segment_id,
    parent_id,
    adapter_index,
    routes,
    mixer_gain,
    latent_gain,
    feed_gain,
    query_matrix,
    latent_down,
    latent_up,
    output_matrix,
    router_matrix,
    shared_in,
    shared_out,
    expert_in,
    expert_out,
    query_entry,
    query_exit,
    lower_entry,
    lower_exit,
    upper_entry,
    upper_exit,
    output_entry,
    output_exit,
):
    rows_here = tokens_in.shape[0]
    groups = lax.axis_size("expert")
    planes = lax.axis_size("dp")
    group_pos = lax.axis_index("expert")
    trees_here = segment_id.shape[0] // TREE
    local_tree = group_pos * rows_here // TREE
    tree_offset = group_pos * rows_here - local_tree * TREE
    chosen = adapter_index[lax.axis_index("dp") * trees_here + local_tree]
    query_in = select_slot(query_entry, chosen)
    qn_out, qr_out = split_heads(select_slot(query_exit, chosen))
    lower_in = select_slot(lower_entry, chosen)
    lower_out = select_slot(lower_exit, chosen)
    upper_in = select_slot(upper_entry, chosen)
    upper_out = select_slot(upper_exit, chosen)
    output_in = select_slot(output_entry, chosen)
    output_out = select_slot(output_exit, chosen)
    experts_all = router_matrix.shape[1]
    owned = expert_in.shape[0]
    capacity = max(2, 4 * rows_here * TOPK // (3 * experts_all))
    cap = -(-capacity // 8) * 8
    hidden_shared = shared_out.shape[0]
    both = ("dp", "expert")
    fast = groups == PLANE and planes == 4 and groups * rows_here == TREE and hidden_shared % 8 == 0

    weight_rows = query_matrix.shape[0]
    padded_shared = -(-planes * hidden_shared // 128) * 128
    fill = padded_shared - planes * hidden_shared
    front, cut = prepare(
        query_matrix, latent_down, router_matrix, shared_in, planes, groups, padded_shared
    )
    if fast:
        front, mix_up, mix_out, sh_in = gather_blocks(
            [front, latent_up, output_matrix], planes, (4, 2, 2), 1, [cut]
        )
        front = front.reshape(D, -1)
        mix_up = mix_up.reshape(KVR, -1)
        mix_out = mix_out.reshape(-1, D)
    else:
        front = lax.all_gather(front, both, axis=0, tiled=True)
        mix_up = lax.all_gather(latent_up, both, axis=0, tiled=True)
        mix_out = lax.all_gather(output_matrix, both, axis=0, tiled=True)
        cut = lax.all_to_all(cut, "expert", split_axis=0, concat_axis=0, tiled=True)
        sh_in = gather_dp(cut.reshape(groups * weight_rows, -1))
    wide = HEADS * (NOPE + ROPE)
    feed_router = front[:, wide + KVR + ROPE :]

    seg_tree = lax.dynamic_slice_in_dim(segment_id, local_tree * TREE, TREE)
    par_tree = lax.dynamic_slice_in_dim(parent_id, local_tree * TREE, TREE)
    key_index = jnp.arange(TREE, dtype=jnp.int32)
    start_pos = jnp.where(par_tree == 0, TRUNK, TRUNK + SEGLEN)
    key_pos = jnp.where(seg_tree == 0, key_index, start_pos + key_index % SEGLEN)
    row_pos = lax.dynamic_slice_in_dim(key_pos, tree_offset, rows_here)
    row_seg = lax.dynamic_slice_in_dim(seg_tree, tree_offset, rows_here)
    step = 128
    while rows_here % step:
        step //= 2
    nb = -(-(rows_here - step) // SEGLEN) + 1
    first_block = tree_offset // SEGLEN
    shift = tree_offset - first_block * SEGLEN
    seg_blocks = seg_tree.reshape(TREE // SEGLEN, SEGLEN)[:, 0]
    par_blocks = par_tree.reshape(TREE // SEGLEN, SEGLEN)[:, 0]
    own = jnp.minimum(first_block + jnp.arange(nb, dtype=jnp.int32), TREE // SEGLEN - 1)
    own_seg = seg_blocks[own]
    own_par = par_blocks[own]
    is_leaf = ((own_seg != 0) & (own_par != 0)).astype(jnp.int32)
    match = (seg_blocks[None, :] == own_par[:, None]) & (is_leaf[:, None] > 0)
    par_block = jnp.sum(
        jnp.where(match, jnp.arange(TREE // SEGLEN, dtype=jnp.int32)[None, :], 0), axis=1
    )
    info = jnp.concatenate([own, par_block, (own_seg != 0).astype(jnp.int32), is_leaf])
    query_limit = jnp.where(
        row_seg == 0, tree_offset + jnp.arange(rows_here, dtype=jnp.int32), TRUNK - 1
    )

    def pad_rows(value):
        empty = jnp.zeros((nb * SEGLEN,) + value.shape[1:], value.dtype)
        return lax.dynamic_update_slice_in_dim(empty, value, shift, 0)

    def cut_rows(value):
        return lax.dynamic_slice_in_dim(value, shift, rows_here, 0)

    inverse = 10000.0 ** (-(jnp.arange(HALF, dtype=F32) * 2.0 / ROPE))
    angles = row_pos.astype(F32)[:, None] * inverse[None, :]
    cos_half, sin_half = jnp.cos(angles), jnp.sin(angles)
    cosine = jnp.concatenate([cos_half, cos_half], -1)
    sine = jnp.concatenate([sin_half, sin_half], -1)
    cos_pair = pad_rows(jnp.concatenate([cos_half] * 4, -1))
    sin_pair = pad_rows(jnp.concatenate([-sin_half, -sin_half, sin_half, sin_half], -1))
    limit_rows = pad_rows(query_limit)

    mask = jnp.sum(
        (routes[:, :, None] == jnp.arange(experts_all, dtype=jnp.int32)).astype(F32), axis=1
    )
    lower = (
        jnp.arange(rows_here)[:, None] >= jnp.arange(rows_here)[None, :]
    ).astype(BF)
    slots_here = product(lower, mask.astype(BF)) * mask

    offset = shift.astype(jnp.int32).reshape(1)
    q_nope, q_rope, latent_ext, latent_raw, hidden, query_mid, lower_mid = project(
        nb,
        offset,
        tokens_in,
        front,
        (
            query_in,
            jnp.concatenate([qn_out, qr_out], 1),
            lower_in,
            lower_out,
            upper_in,
            mixer_gain[None, :],
            latent_gain[None, :],
            cos_half,
            sin_half,
        ),
    )
    grad_payload = jnp.concatenate(
        [cotangent, slots_here.astype(BF), jnp.zeros((rows_here, 128 - experts_all), BF)], 1
    )
    grad_payload, latent_ext, out_rows = lax.optimization_barrier(
        (grad_payload, latent_ext, shared_out)
    )
    sh_out = gather_dp(out_rows).reshape(planes * hidden_shared, D)
    sh_out = jnp.pad(sh_out, ((0, fill), (0, 0)))
    all_grad = lax.all_gather(grad_payload, "expert", axis=0, tiled=True)
    rank = query_mid.shape[1]
    if fast:
        all_latent = gather_blocks([latent_ext], 1, (2,), 2)[0].reshape(TREE, LATW)
    else:
        all_latent = lax.all_gather(latent_ext, "expert", axis=0, tiled=True)
    tree_latent = lax.dynamic_slice_in_dim(all_latent, local_tree * TREE, TREE, 0)
    sh_in = sh_in.reshape(D, 2 * padded_shared)
    up_extra = jnp.concatenate(
        [
            jnp.zeros((HALF, mix_up.shape[1]), BF),
            upper_out,
            jnp.zeros((LATW - KVR - HALF - rank, mix_up.shape[1]), BF),
        ],
        0,
    )
    attended, level, keys_values = attend(
        nb, info, q_nope, q_rope, cos_pair, sin_pair, limit_rows, tree_latent, mix_up, up_extra
    )
    attended, sh_out = lax.optimization_barrier((attended, sh_out))
    mixed_state, feed_payload, router_probs, output_mid = mix(
        offset,
        attended,
        tokens_in,
        mix_out,
        front,
        output_in,
        output_out,
        feed_gain[None, :],
        experts_all,
    )

    my_slots = lax.dynamic_slice(all_grad, (0, D + group_pos * owned), (groups * rows_here, owned))
    slot_rows = jnp.pad(my_slots, ((0, 0), (0, 128 - owned)))
    slot_cols = my_slots.reshape(groups, rows_here, owned).transpose(0, 2, 1).astype(F32)
    grad_perm, grad_shared = spread_grad(all_grad, slot_cols, sh_out, cap)
    flat = (owned, groups * cap)
    grad_inner = expert_grads(grad_perm.reshape(*flat, D), expert_out)

    all_feed = lax.all_gather(feed_payload, "expert", axis=0, tiled=True)

    all_feed, grad_inner = lax.optimization_barrier((all_feed, grad_inner))

    def my_columns(start):
        return lax.dynamic_slice(
            all_feed, (0, start + group_pos * owned), (groups * rows_here, owned)
        ).astype(F32)

    my_probs = my_columns(D) + my_columns(D + experts_all)
    prob_cols = my_probs.reshape(groups, rows_here, owned).transpose(0, 2, 1)
    feed_perm, gates, inner_shared, gact_shared = spread_feed(
        all_feed, slot_cols, prob_cols, grad_shared, sh_in, cap
    )
    gates = gates.reshape(*flat, 128)
    slot_perm, inner = run_experts(
        (group_pos * owned).astype(jnp.int32).reshape(1),
        feed_perm.reshape(*flat, D),
        grad_inner,
        gates,
        expert_in,
        experts_all,
    )
    grad_part = collect(
        slot_perm.reshape(owned, groups, cap, D + 128), slot_rows, gact_shared, sh_in, True
    )
    grad_sum = lax.psum_scatter(grad_part, "expert", scatter_dimension=0, tiled=True)
    inner, grad_part = lax.optimization_barrier((inner, grad_part))
    rows_perm = expert_rows(inner, gates, expert_out)
    row_part = collect(
        rows_perm.reshape(owned, groups, cap, D), slot_rows, inner_shared, sh_out, False
    )
    row_sum = lax.psum_scatter(row_part, "expert", scatter_dimension=0, tiled=True)

    grad_mixed, grad_output_mid, grad_attended = turn(
        nb,
        offset,
        grad_sum,
        router_probs,
        mixed_state,
        cotangent,
        feed_gain[None, :],
        front,
        output_in,
        output_out,
        mix_out,
    )

    dq_nope, dq_rope, grad_up, grad_tree = attend_back(
        nb,
        info,
        q_nope,
        q_rope,
        cos_pair,
        sin_pair,
        limit_rows,
        tree_latent,
        keys_values,
        mix_up,
        up_extra,
        grad_attended,
        attended,
        level,
        jnp.pad(upper_in, ((HALF, LATW - KVR - HALF - rank), (0, 0))),
    )
    own_tree = grad_tree
    if trees_here > 1:
        grad_tree = lax.dynamic_update_slice_in_dim(
            jnp.zeros((groups * rows_here, grad_tree.shape[1]), BF), grad_tree, local_tree * TREE, 0
        )
    if fast:
        grad_latent = scatter_blocks(grad_tree.reshape(groups, rows_here, -1), 4, 5, F32)
    else:
        grad_latent = lax.psum_scatter(
            grad_tree, "expert", scatter_dimension=0, tiled=True
        ).astype(F32)
    row_sum, grad_latent = lax.optimization_barrier((row_sum, grad_latent))
    block_output = (mixed_state + row_sum.astype(F32)).astype(BF)
    offsets, end = [], 0
    for width in (
        query_entry.shape[2],
        query_exit.shape[2],
        lower_entry.shape[2],
        lower_exit.shape[2],
        upper_entry.shape[2],
        upper_exit.shape[2],
        output_entry.shape[2],
        output_exit.shape[2],
    ):
        offsets.append((end, width))
        end += -(-width // 128) * 128
    total = -(-end // (128 * PLANE)) * 128 * PLANE
    grad_front, joined, grad_query_mid, grad_lower_mid = join(
        tuple(offsets),
        total,
        offset,
        [
            dq_nope,
            dq_rope,
            jnp.concatenate([qn_out, qr_out], 1),
            query_mid,
            hidden,
            grad_latent.astype(F32),
            latent_raw,
            latent_gain[None, :],
            cos_half,
            sin_half,
            lower_out,
            lower_mid,
            own_tree,
            tree_latent,
            grad_up,
            output_mid,
            grad_mixed,
            grad_output_mid,
            attended,
        ],
    )

    adapters = query_entry.shape[0]
    if fast:
        full, grad_input = exchange_banks(
            joined,
            planes,
            6,
            front,
            [
                grad_front,
                grad_query_mid,
                grad_lower_mid,
                query_in,
                lower_in,
                tokens_in,
                mixer_gain[None, :],
                grad_mixed,
            ],
        )
        banks = place_banks(full, adapter_index, tuple(offsets), adapters)
    else:
        grad_hidden = (
            product_t(grad_front, front)
            + product(grad_query_mid, query_in)
            + product(grad_lower_mid, lower_in)
        )
        inputs = tokens_in.astype(F32)
        _, norm_one_back = jax.vjp(lambda operand: normed(operand, mixer_gain), inputs)
        grad_input = (grad_mixed + norm_one_back(grad_hidden)[0]).astype(BF)
        gradients = [joined[:, at : at + width] for at, width in offsets]
        banks = reduce_banks(gradients, local_tree, trees_here, adapter_index, adapters)
    return (block_output, grad_input, *banks)


def solution(mesh):
    tokens = P(("dp", "expert"), None)
    in_specs = (
        tokens,
        tokens,
        P("dp"),
        P("dp"),
        P(),
        tokens,
        P(),
        P(),
        P(),
        *([tokens] * 7),
        P("expert", None, None),
        P("expert", None, None),
        *([P()] * 8),
    )
    out_specs = (tokens, tokens, *([P()] * 8))
    return jax.shard_map(body, mesh=mesh, in_specs=in_specs, out_specs=out_specs, check_vma=False)
```

```python
import functools

import jax
import jax.numpy as jnp
from jax import lax
from jax.experimental import pallas as pl
from jax.experimental.pallas import tpu as pltpu
from jax.sharding import PartitionSpec as P

D = 2048
HEADS = 16
NOPE = 128
ROPE = 64
VDIM = 128
KVR = 512
TOPK = 6
SEGLEN = 128
TRUNK = 1024
TREE = 2560
LATW = 640
HALF = ROPE // 2
VMEM_LIMIT = 66_000_000
BF = jnp.bfloat16
F32 = jnp.float32


def product(left, right):
    return jnp.dot(left, right, preferred_element_type=F32)


def product_t(left, right):
    return lax.dot_general(left, right, (((1,), (1,)), ((), ())), preferred_element_type=F32)


def product_left(left, right):
    return lax.dot_general(left, right, (((0,), (0,)), ((), ())), preferred_element_type=F32)


def normed(operand, gain):
    return operand * lax.rsqrt(jnp.mean(operand * operand, axis=-1, keepdims=True) + 1e-06) * gain


def rotate(operand, cosine, sine):
    half_width = operand.shape[-1] // 2
    turned = jnp.concatenate([-operand[..., half_width:], operand[..., :half_width]], -1)
    return operand * cosine + turned * sine


def lane_iota(shape):
    return lax.broadcasted_iota(jnp.int32, shape, len(shape) - 1)


def row_iota(shape):
    return lax.broadcasted_iota(jnp.int32, shape, len(shape) - 2)


LOG2E = 1.4426950408889634
SCALING = 1.0 / (NOPE + ROPE) ** 0.5


def place_keys(nb, info, lat, latsel):
    latsel[:TRUNK, :] = lat[:TRUNK, :]
    for m in range(nb):
        for side in range(2):
            start = pl.multiple_of(info[side * nb + m] * SEGLEN, SEGLEN)
            at = TRUNK + (2 * m + side) * SEGLEN
            latsel[at : at + SEGLEN, :] = lat[pl.ds(start, SEGLEN), :]


def rotary_keys(tail, kr):
    tail = tail.astype(F32)
    first = jnp.where(lane_iota(tail.shape) % ROPE < HALF, tail, 0.0)
    kr[0] = first.astype(BF)
    kr[1] = pltpu.roll(first, HALF, 1).astype(BF)


def local_limit(nb, info, m, key, row):
    return jnp.where(
        key < SEGLEN,
        (row + 1) * info[2 * nb + m] - 1,
        SEGLEN + SEGLEN * info[3 * nb + m] - 1,
    )


def attend_kernel(
    nb, info, qn, qr, cosp, sinp, qlim, lat, up, upx, out, lse, kv,
    latsel, kr, bias, near, st, sl, pt,
):
    rows_all = qn.shape[0]

    @pl.when(pl.program_id(0) == 0)
    def _():
        place_keys(nb, info, lat, latsel)
        rotary_keys(latsel[:, KVR:], kr)
        bias[...] = jnp.where(row_iota((TRUNK, rows_all)) <= qlim[...], 0.0, -1e30)
        key = row_iota((2 * SEGLEN, SEGLEN))
        row = lane_iota((2 * SEGLEN, SEGLEN))
        for m in range(nb):
            near[m] = jnp.where(key <= local_limit(nb, info, m, key, row), 0.0, -1e30)

    raw = qr[...]
    qrot = (raw * cosp[...] + pltpu.roll(raw, ROPE, 1) * sinp[...]).astype(BF)
    keys = latsel.shape[0]
    rows = keys // 2 if keys % 512 == 0 else keys
    for at in range(0, keys, rows):
        kv[at : at + rows, :] = (
            product(latsel[at : at + rows, :KVR], up[...])
            + product(latsel[at : at + rows, KVR:], upx[...])
        ).astype(BF)
    blocks = [slice(m * SEGLEN, (m + 1) * SEGLEN) for m in range(nb)]
    nears = [slice(TRUNK + 2 * m * SEGLEN, TRUNK + 2 * (m + 1) * SEGLEN) for m in range(nb)]
    chunks = [slice(at, at + 256) for at in range(0, TRUNK, 256)]
    peaks = []
    for a in range(2):
        q = jnp.concatenate([qn[:, a * 128 : a * 128 + 128], qrot], 1)
        k = jnp.concatenate([kv[:, a * 256 : a * 256 + 128], kr[a]], 1)
        peak = None
        for there in chunks:
            scores = product_t(k[there], q) + bias[there, :]
            st[a, there, :] = scores
            top = jnp.max(scores, axis=0, keepdims=True)
            peak = top if peak is None else jnp.maximum(peak, top)
        tops = []
        for m in range(nb):
            scores = product_t(k[nears[m]], q[blocks[m]]) + near[m]
            sl[a, m] = scores
            tops.append(jnp.max(scores, axis=0, keepdims=True))
        peak = jnp.maximum(peak, jnp.concatenate(tops, 1))
        peaks.append(peak * (SCALING * LOG2E))
    levels = []
    for a in range(2):
        v = kv[:, a * 256 + 128 : a * 256 + 256]
        total = None
        for there in chunks:
            e = jnp.exp2(st[a, there, :] * (SCALING * LOG2E) - peaks[a])
            part = jnp.sum(e, axis=0, keepdims=True)
            total = part if total is None else total + part
            pt[a, there, :] = e.astype(BF)
        parts, sums = [], []
        for m in range(nb):
            e = jnp.exp2(sl[a, m] * (SCALING * LOG2E) - peaks[a][:, blocks[m]])
            sums.append(jnp.sum(e, axis=0, keepdims=True))
            parts.append(product_left(e.astype(BF), v[nears[m]]))
        total = total + jnp.concatenate(sums, 1)
        got = product_left(pt[a], v[:TRUNK]) + jnp.concatenate(parts, 0)
        inverse = jnp.broadcast_to(1.0 / total, (128, rows_all)).T
        out[:, a * 128 : a * 128 + 128] = (got * inverse).astype(BF)
        levels.append(peaks[a] + jnp.log(total) * LOG2E)
    lse[0] = jnp.concatenate(levels + [jnp.zeros((6, rows_all), F32)], 0)


def chance_kernel(
    nb, info, qn, qr, cosp, sinp, qlim, tails, kv, stats, pt, pn, tail, kr, bias, near
):
    rows_all = qn.shape[0]

    @pl.when(pl.program_id(0) == 0)
    def _():
        place_keys(nb, info, tails, tail)
        rotary_keys(tail[...], kr)
        bias[...] = jnp.where(row_iota((TRUNK, rows_all)) <= qlim[...], 0.0, -1e30)
        key = row_iota((2 * SEGLEN, SEGLEN))
        row = lane_iota((2 * SEGLEN, SEGLEN))
        for m in range(nb):
            near[m] = jnp.where(key <= local_limit(nb, info, m, key, row), 0.0, -1e30)

    raw = qr[...]
    qrot = (raw * cosp[...] + pltpu.roll(raw, ROPE, 1) * sinp[...]).astype(BF)
    for a in range(2):
        q = jnp.concatenate([qn[:, a * 128 : a * 128 + 128], qrot], 1)
        k = jnp.concatenate([kv[:, a * 256 : a * 256 + 128], kr[a]], 1)
        level = stats[0, a : a + 1, :]
        for at in range(0, TRUNK, 256):
            there = slice(at, at + 256)
            scores = product_t(k[there], q) + bias[there, :]
            pt[0, a, there, :] = jnp.exp2(scores * (SCALING * LOG2E) - level).astype(BF)
        for m in range(nb):
            here = slice(m * SEGLEN, (m + 1) * SEGLEN)
            there = slice(TRUNK + 2 * m * SEGLEN, TRUNK + 2 * (m + 1) * SEGLEN)
            scores = product_t(k[there], q[here]) + near[m]
            pn[0, a, m] = jnp.exp2(scores * (SCALING * LOG2E) - level[:, here]).astype(BF)


def attend_back_kernel(
    nb, info, qn, qr, cosp, sinp, tails, kv, up, upx, do, att, pt, pn, upper,
    dqn, dqr, gup, dlow, tail, kr, dss, dkv, acc, dkr, dlat,
):
    step = pl.program_id(0)
    rows_all = qn.shape[0]

    @pl.when(step == 0)
    def _():
        place_keys(nb, info, tails, tail)
        rotary_keys(tail[...], kr)
        acc[...] = jnp.zeros_like(acc)
        dkr[...] = jnp.zeros_like(dkr)

    raw = qr[...]
    qrot = (raw * cosp[...] + pltpu.roll(raw, ROPE, 1) * sinp[...]).astype(BF)
    dq_rope = None
    for a in range(2):
        q = jnp.concatenate([qn[:, a * 128 : a * 128 + 128], qrot], 1)
        k = jnp.concatenate([kv[:, a * 256 : a * 256 + 128], kr[a]], 1)
        v = kv[:, a * 256 + 128 : a * 256 + 256]
        g = do[:, a * 128 : a * 128 + 128]
        shares = g.astype(F32) * att[:, a * 128 : a * 128 + 128].astype(F32)
        main = shares.astype(BF)
        ones = jnp.ones((8, 128), BF)
        delta = product_t(ones, main) + product_t(ones, (shares - main.astype(F32)).astype(BF))
        delta = delta[:1]
        mine = lane_iota((1, 128)) % ROPE
        mine = (mine < HALF) if a == 0 else (mine >= HALF)

        def block(there, here, p):
            dp = product_t(v[there], g[here])
            ds = (p.astype(F32) * (dp - delta[:, here])).astype(BF)
            dk = product(ds, q[here]) * SCALING
            dkv[there, a * 256 : a * 256 + 128] = dk[:, :128].astype(BF)
            dkv[there, a * 256 + 128 : a * 256 + 256] = product(p, g[here]).astype(BF)
            dkr[there, :] += jnp.where(mine, dk[:, 128:], 0.0)
            return ds

        for at in range(0, TRUNK, 256):
            there = slice(at, at + 256)
            dss[there, :] = block(there, slice(0, rows_all), pt[0, a, there, :])
        parts = []
        for m in range(nb):
            here = slice(m * SEGLEN, (m + 1) * SEGLEN)
            there = slice(TRUNK + 2 * m * SEGLEN, TRUNK + 2 * (m + 1) * SEGLEN)
            parts.append(product_left(block(there, here, pn[0, a, m]), k[there]))
        dq = (product_left(dss[...], k[:TRUNK]) + jnp.concatenate(parts, 0)) * SCALING
        dqn[:, a * 128 : a * 128 + 128] = dq[:, :128].astype(BF)
        dq_rope = dq[:, 128:] if dq_rope is None else dq_rope + dq[:, 128:]
    dqr[...] = (dq_rope * cosp[...] + pltpu.roll(dq_rope * sinp[...], ROPE, 1)).astype(BF)
    gup[...] = product_left(tail[...], dkv[...])
    for at in range(0, tail.shape[0], 256):
        acc[at : at + 256, :KVR] += product_t(dkv[at : at + 256, :], up[...])
        acc[at : at + 256, KVR:] += product_t(dkv[at : at + 256, :], upx[...])

    @pl.when(step == pl.num_programs(0) - 1)
    def _():
        rope = dkr[...]
        folded = rope + pltpu.roll(rope, 128 - HALF, 1)
        keep = lane_iota(rope.shape) % ROPE < HALF
        acc[:, KVR:] += jnp.where(keep, folded, 0.0)
        dlat[:TRUNK, :] = acc[:TRUNK, :]
        dlat[TRUNK:, :] = jnp.zeros((TREE - TRUNK, LATW), F32)
        for m in range(nb):
            for side in range(2):
                start = pl.multiple_of(info[side * nb + m] * SEGLEN, SEGLEN)
                at = TRUNK + (2 * m + side) * SEGLEN
                dlat[pl.ds(start, SEGLEN), :] += acc[at : at + SEGLEN, :]
        low = dlat[:, KVR:].astype(BF)
        dlow[:, KVR:] = low
        dlow[:, :KVR] = (dlat[:, :KVR] + product(low, upper[...])).astype(BF)


def pair_spec(rows, width):
    return pl.BlockSpec((rows, width), lambda i, info: (0, i))


def lead_spec(rows, width):
    return pl.BlockSpec((1, rows, width), lambda i, info: (i, 0, 0))


def whole_spec(shape):
    return pl.BlockSpec(shape, lambda i, info: (0, 0))


def attend(nb, info, qn, qr, cosp, sinp, qlim, lat, up, upx):
    rows, keys = qn.shape[0], TRUNK + 2 * nb * SEGLEN
    return pl.pallas_call(
        functools.partial(attend_kernel, nb),
        out_shape=(
            jax.ShapeDtypeStruct((rows, HEADS * VDIM), BF),
            jax.ShapeDtypeStruct((HEADS // 2, 8, rows), F32),
            jax.ShapeDtypeStruct((keys, HEADS * (NOPE + VDIM)), BF),
        ),
        grid_spec=pltpu.PrefetchScalarGridSpec(
            num_scalar_prefetch=1,
            grid=(HEADS // 2,),
            in_specs=[
                pair_spec(rows, 256),
                pair_spec(rows, 128),
                whole_spec((rows, 128)),
                whole_spec((rows, 128)),
                whole_spec((1, rows)),
                whole_spec((TREE, LATW)),
                pair_spec(KVR, 512),
                pair_spec(LATW - KVR, 512),
            ],
            out_specs=(pair_spec(rows, 256), lead_spec(8, rows), pair_spec(keys, 512)),
            scratch_shapes=[
                pltpu.VMEM((keys, LATW), BF),
                pltpu.VMEM((2, keys, 128), BF),
                pltpu.VMEM((TRUNK, rows), F32),
                pltpu.VMEM((nb, 2 * SEGLEN, SEGLEN), F32),
                pltpu.VMEM((2, TRUNK, rows), F32),
                pltpu.VMEM((2, nb, 2 * SEGLEN, SEGLEN), F32),
                pltpu.VMEM((2, TRUNK, rows), BF),
            ],
        ),
        name="attend",
        **costs(30e9, 25e6),
    )(info, qn, qr, cosp, sinp, qlim[None, :], lat, up, upx)


def far_spec(keys, rows):
    return pl.BlockSpec((1, 2, keys, rows), lambda i, info: (i, 0, 0, 0))


def near_spec(nb):
    return pl.BlockSpec((1, 2, nb, 2 * SEGLEN, SEGLEN), lambda i, info: (i, 0, 0, 0, 0))


def chances(nb, info, qn, qr, cosp, sinp, qlim, lat, kv, stats):
    rows, keys = qn.shape[0], TRUNK + 2 * nb * SEGLEN
    return pl.pallas_call(
        functools.partial(chance_kernel, nb),
        out_shape=(
            jax.ShapeDtypeStruct((HEADS // 2, 2, TRUNK, rows), BF),
            jax.ShapeDtypeStruct((HEADS // 2, 2, nb, 2 * SEGLEN, SEGLEN), BF),
        ),
        grid_spec=pltpu.PrefetchScalarGridSpec(
            num_scalar_prefetch=1,
            grid=(HEADS // 2,),
            in_specs=[
                pair_spec(rows, 256),
                pair_spec(rows, 128),
                whole_spec((rows, 128)),
                whole_spec((rows, 128)),
                whole_spec((1, rows)),
                pl.BlockSpec((TREE, 128), lambda i, info: (0, KVR // 128)),
                pair_spec(keys, 512),
                lead_spec(8, rows),
            ],
            out_specs=(far_spec(TRUNK, rows), near_spec(nb)),
            scratch_shapes=[
                pltpu.VMEM((keys, 128), BF),
                pltpu.VMEM((2, keys, 128), BF),
                pltpu.VMEM((TRUNK, rows), F32),
                pltpu.VMEM((nb, 2 * SEGLEN, SEGLEN), F32),
            ],
        ),
        name="chances",
        **costs(6e9, 32e6),
    )(info, qn, qr, cosp, sinp, qlim[None, :], lat, kv, stats)


def attend_back(nb, info, qn, qr, cosp, sinp, lat, kv, up, upx, do, att, pt, pn, upper):
    rows, keys = qn.shape[0], TRUNK + 2 * nb * SEGLEN
    return pl.pallas_call(
        functools.partial(attend_back_kernel, nb),
        out_shape=(
            jax.ShapeDtypeStruct((rows, HEADS * NOPE), BF),
            jax.ShapeDtypeStruct((rows, HEADS * ROPE), BF),
            jax.ShapeDtypeStruct((128, HEADS * (NOPE + VDIM)), F32),
            jax.ShapeDtypeStruct((TREE, LATW), BF),
        ),
        grid_spec=pltpu.PrefetchScalarGridSpec(
            num_scalar_prefetch=1,
            grid=(HEADS // 2,),
            in_specs=[
                pair_spec(rows, 256),
                pair_spec(rows, 128),
                whole_spec((rows, 128)),
                whole_spec((rows, 128)),
                pl.BlockSpec((TREE, 128), lambda i, info: (0, KVR // 128)),
                pair_spec(keys, 512),
                pair_spec(KVR, 512),
                pair_spec(LATW - KVR, 512),
                pair_spec(rows, 256),
                pair_spec(rows, 256),
                far_spec(TRUNK, rows),
                near_spec(nb),
                whole_spec((LATW - KVR, KVR)),
            ],
            out_specs=(
                pair_spec(rows, 256),
                pair_spec(rows, 128),
                pair_spec(128, 512),
                whole_spec((TREE, LATW)),
            ),
            scratch_shapes=[
                pltpu.VMEM((keys, 128), BF),
                pltpu.VMEM((2, keys, 128), BF),
                pltpu.VMEM((TRUNK, rows), BF),
                pltpu.VMEM((keys, 512), BF),
                pltpu.VMEM((keys, LATW), F32),
                pltpu.VMEM((keys, 128), F32),
                pltpu.VMEM((TREE, LATW), F32),
            ],
        ),
        name="attend_back",
        **costs(54e9, 30e6),
    )(info, qn, qr, cosp, sinp, lat, kv, up, upx, do, att, pt, pn, upper)


def head_columns(wide):
    nope, rope = [], []
    for pair in range(HEADS // 2):
        starts = [(2 * pair + a) * (NOPE + ROPE) for a in range(2)]
        for at in starts:
            nope.append(wide[:, at : at + NOPE])
        for half in range(2):
            for at in starts:
                first = at + NOPE + half * HALF
                rope.append(wide[:, first : first + HALF])
    return nope + rope


def prepare_kernel(planes, picked, info, *refs):
    query, down, router, shared = refs[:4]
    banks, (front, cut), chosen = refs[4 : 4 + picked], refs[4 + picked : 6 + picked], refs[6 + picked :]
    rest = [down[...].astype(F32), router[...].astype(F32)]
    front[...] = jnp.concatenate(head_columns(query[...].astype(F32)) + rest, 1).astype(BF)
    whole = shared[...].astype(F32)
    groups, _, width = cut.shape
    hidden = whole.shape[1] // 2
    each = hidden // (planes * groups)
    blank = jnp.zeros((whole.shape[0], width // 2 - planes * each), F32)
    for j in range(groups):
        columns = []
        for part in range(2):
            for i in range(planes):
                at = part * hidden + (i * groups + j) * each
                columns.append(whole[:, at : at + each])
            columns.append(blank)
        cut[j] = jnp.concatenate(columns, 1).astype(BF)
    rank = banks[0].shape[1]
    for n in range(picked):
        if n == 1:
            chosen[n][...] = jnp.concatenate(head_columns(banks[n][0].astype(F32)), 1).astype(BF)
        elif n in (4, 5):
            columns = banks[n].shape[2]
            chosen[n][...] = jnp.concatenate(
                [
                    jnp.zeros((HALF, columns), F32),
                    banks[n][0].astype(F32),
                    jnp.zeros((LATW - KVR - HALF - rank, columns), F32),
                ],
                0,
            ).astype(BF)
        else:
            chosen[n][...] = banks[n][0]
    chosen[picked][...] = banks[4][0]


def prepare(chosen, matrices, banks, planes, groups, padded):
    query, down, router, shared = matrices
    rows, rank = query.shape[0], banks[0].shape[1]
    width = query.shape[1] + down.shape[1] + router.shape[1]
    shapes = [(rows, width), (groups, rows, 2 * padded)]
    for n, bank in enumerate(banks):
        shapes.append((LATW - KVR if n in (4, 5) else rank, bank.shape[2]))
    shapes.append((rank, banks[4].shape[2]))
    return pl.pallas_call(
        functools.partial(prepare_kernel, planes, len(banks)),
        out_shape=[jax.ShapeDtypeStruct(shape, BF) for shape in shapes],
        grid_spec=pltpu.PrefetchScalarGridSpec(
            num_scalar_prefetch=1,
            grid=(1,),
            in_specs=[
                *[fixed_at(m) for m in matrices],
                *[
                    pl.BlockSpec((1, rank, bank.shape[2]), lambda i, info: (info[0], 0, 0))
                    for bank in banks
                ],
            ],
            out_specs=[whole_out(shape) for shape in shapes],
        ),
        name="prepare",
        **costs(1e6, 4e6),
    )(chosen.reshape(1), *matrices, *banks)


def project_kernel(
    info, tokens, front, query_in, query_out, lower_in, lower_out, upper_in, mixer, gain, cos, sin,
    qn, qr, ext, raw, hidden, query_mid, lower_mid, acc,
):
    step = pl.program_id(0)

    @pl.when(step == 0)
    def _():
        hidden[...] = normed(tokens[...].astype(F32), mixer[...]).astype(BF)
        query_mid[...] = product_t(hidden[...], query_in[...]).astype(BF)
        lower_mid[...] = product_t(hidden[...], lower_in[...]).astype(BF)

    depth = front.shape[0]
    part = product(hidden[:, pl.ds(pl.multiple_of(step * depth, depth), depth)], front[...])

    @pl.when(step == 0)
    def _():
        acc[...] = part

    @pl.when(step > 0)
    def _():
        acc[...] += part

    @pl.when(step == pl.num_programs(0) - 1)
    def _():
        rows = hidden.shape[0]
        wide = HEADS * (NOPE + ROPE)
        middle = HEADS * NOPE
        here = pl.ds(pl.multiple_of(info[0], 16), rows)
        qn[...] = jnp.zeros_like(qn)
        qr[...] = jnp.zeros_like(qr)
        mid = query_mid[...]
        qn[here, :] = (acc[:, :middle] + product(mid, query_out[:, :middle])).astype(BF)
        qr[here, :] = acc[:, middle:wide] + product(mid, query_out[:, middle:])
        low = product(lower_mid[...], lower_out[...])
        latent = acc[:, wide : wide + KVR] + low[:, :KVR]
        raw[...] = latent
        norm = normed(latent, gain[...]).astype(BF)
        upper = product_t(norm, upper_in[...])
        key = acc[:, wide + KVR : wide + KVR + ROPE] + low[:, KVR:]
        first, second = key[:, :HALF], key[:, HALF:]
        c, s = cos[...], sin[...]
        ext[:, :KVR] = norm
        ext[:, KVR:] = jnp.concatenate(
            [
                first * c - second * s,
                upper,
                jnp.zeros((rows, HALF - upper.shape[1]), F32),
                second * c + first * s,
                jnp.zeros((rows, HALF), F32),
            ],
            1,
        ).astype(BF)


def fixed_at(value):
    return pl.BlockSpec(value.shape, lambda i, info: (0,) * value.ndim)


def whole_out(shape):
    return pl.BlockSpec(shape, lambda i, info: (0,) * len(shape))


def project(nb, shift, tokens, front, small):
    rows, depth = tokens.shape
    padded, step, rank = nb * SEGLEN, 512, small[0].shape[0]
    shapes = [
        ((padded, HEADS * NOPE), BF),
        ((padded, HEADS * ROPE), F32),
        ((rows, LATW), BF),
        ((rows, KVR), F32),
        ((rows, depth), BF),
        ((rows, rank), BF),
        ((rows, rank), BF),
    ]
    return pl.pallas_call(
        project_kernel,
        out_shape=[jax.ShapeDtypeStruct(shape, kind) for shape, kind in shapes],
        grid_spec=pltpu.PrefetchScalarGridSpec(
            num_scalar_prefetch=1,
            grid=(depth // step,),
            in_specs=[
                fixed_at(tokens),
                pl.BlockSpec((step, front.shape[1]), lambda i, info: (i, 0)),
                *[fixed_at(v) for v in small],
            ],
            out_specs=[whole_out(shape) for shape, _ in shapes],
            scratch_shapes=[pltpu.VMEM((rows, front.shape[1]), F32)],
        ),
        name="project",
        **costs(5e9, 20e6),
    )(shift, tokens, front, *small)


def mix_kernel(
    info, attended, tokens, matrix, router, out_in, out_out, gain,
    mixed, payload, probs, out_mid, acc,
):
    step = pl.program_id(0)
    rows = tokens.shape[0]
    here = pl.ds(pl.multiple_of(info[0], 16), rows)

    @pl.when(step == 0)
    def _():
        out_mid[...] = product_t(attended[here, :], out_in[...]).astype(BF)

    depth = matrix.shape[0]
    columns = pl.ds(pl.multiple_of(step * depth, depth), depth)
    part = product(attended[here, columns], matrix[...])

    @pl.when(step == 0)
    def _():
        acc[...] = part

    @pl.when(step > 0)
    def _():
        acc[...] += part

    @pl.when(step == pl.num_programs(0) - 1)
    def _():
        state = tokens[...].astype(F32) + (acc[...] + product(out_mid[...], out_out[...]))
        mixed[...] = state
        feed = normed(state, gain[...]).astype(BF)
        experts = probs.shape[1]
        logits = product(feed, router[...])[:, 128 - experts :]
        powers = jnp.exp(logits - jnp.max(logits, axis=1, keepdims=True))
        chance = powers / jnp.sum(powers, axis=1, keepdims=True)
        probs[...] = chance
        high = chance.astype(BF).astype(F32)
        payload[:, :D] = feed
        payload[:, D:] = jnp.concatenate([high, chance - high], 1).astype(BF)


def mix(shift, attended, tokens, matrix, front, out_in, out_out, gain, experts):
    rows = tokens.shape[0]
    step, rank = 512, out_in.shape[0]
    last = front.shape[1] // 128 - 1
    shapes = [((rows, D), F32), ((rows, D + 128), BF), ((rows, experts), F32), ((rows, rank), BF)]
    return pl.pallas_call(
        mix_kernel,
        out_shape=[jax.ShapeDtypeStruct(shape, kind) for shape, kind in shapes],
        grid_spec=pltpu.PrefetchScalarGridSpec(
            num_scalar_prefetch=1,
            grid=(D // step,),
            in_specs=[
                fixed_at(attended),
                fixed_at(tokens),
                pl.BlockSpec((step, D), lambda i, info: (i, 0)),
                pl.BlockSpec((D, 128), lambda i, info: (0, last)),
                fixed_at(out_in),
                fixed_at(out_out),
                fixed_at(gain),
            ],
            out_specs=[whole_out(shape) for shape, _ in shapes],
            scratch_shapes=[pltpu.VMEM((rows, D), F32)],
        ),
        name="mix",
        **costs(3e9, 14e6),
    )(shift, attended, tokens, matrix, front, out_in, out_out, gain)


def turn_kernel(
    info, sums, probs, mixed, cotangent, gain, router, out_in, out_out, matrix,
    grad_mixed, out_mid, do, low,
):
    rows = mixed.shape[0]

    @pl.when(pl.program_id(0) == 0)
    def _():
        experts = probs.shape[1]
        both = sums[:, D:].astype(F32)
        direct = both[:, :experts] + both[:, experts:]
        chance = probs[...]
        logits = chance * (direct - jnp.sum(chance * direct, axis=1, keepdims=True))
        spread = jnp.concatenate([jnp.zeros((rows, 128 - experts), F32), logits], 1).astype(BF)
        keep = jnp.where(lane_iota(router.shape) >= 128 - experts, router[...].astype(F32), 0.0)
        feed = sums[:, :D].astype(F32) + product_t(spread, keep.astype(BF))
        state = mixed[...]
        inverse = lax.rsqrt(jnp.mean(state * state, axis=-1, keepdims=True) + 1e-06)
        scaled = feed * gain[...]
        along = jnp.mean(scaled * state, axis=-1, keepdims=True)
        back = inverse * scaled - state * (inverse * inverse * inverse * along)
        total = cotangent[...].astype(F32) + back
        grad_mixed[...] = total
        low[...] = total.astype(BF)
        out_mid[...] = product_t(low[...], out_out[...]).astype(BF)

    here = pl.ds(pl.multiple_of(info[0], 16), rows)
    do[...] = jnp.zeros_like(do)
    do[here, :] = (
        product_t(low[...], matrix[...]) + product(out_mid[...], out_in[...])
    ).astype(BF)


def turn(nb, shift, sums, probs, mixed, cotangent, gain, front, out_in, out_out, matrix):
    rows, experts = probs.shape
    step, rank = 512, out_in.shape[0]
    last = front.shape[1] // 128 - 1
    padded = nb * SEGLEN
    return pl.pallas_call(
        turn_kernel,
        out_shape=[
            jax.ShapeDtypeStruct((rows, D), F32),
            jax.ShapeDtypeStruct((rows, rank), BF),
            jax.ShapeDtypeStruct((padded, D), BF),
        ],
        grid_spec=pltpu.PrefetchScalarGridSpec(
            num_scalar_prefetch=1,
            grid=(D // step,),
            in_specs=[
                fixed_at(sums),
                fixed_at(probs),
                fixed_at(mixed),
                fixed_at(cotangent),
                fixed_at(gain),
                pl.BlockSpec((D, 128), lambda i, info: (0, last)),
                pl.BlockSpec((rank, step), lambda i, info: (0, i)),
                fixed_at(out_out),
                pl.BlockSpec((step, D), lambda i, info: (i, 0)),
            ],
            out_specs=[
                whole_out((rows, D)),
                whole_out((rows, rank)),
                pl.BlockSpec((padded, step), lambda i, info: (0, i)),
            ],
            scratch_shapes=[pltpu.VMEM((rows, D), BF)],
        ),
        name="turn",
        **costs(3e9, 18e6),
    )(shift, sums, probs, mixed, cotangent, gain, front, out_in, out_out, matrix)


def join_kernel(
    offsets, info, dqn, dqr, query_out, query_mid, hidden, sums, raw, gain, cos, sin, lower_out,
    lower_mid, tree, lat, upper_exit, out_mid, mixed, grad_out_mid, attended,
    grads, joined, grad_query_mid, grad_lower_mid,
):
    rows = hidden.shape[0]
    here = pl.ds(pl.multiple_of(info[0], 16), rows)
    nope, rope = dqn[here, :], dqr[here, :]
    middle, wide = HEADS * NOPE, HEADS * (NOPE + ROPE)
    values = raw[...]
    inverse = lax.rsqrt(jnp.mean(values * values, axis=-1, keepdims=True) + 1e-06)
    scaled = sums[:, :KVR] * gain[...]
    along = jnp.mean(scaled * values, axis=-1, keepdims=True)
    latent = inverse * scaled - values * (inverse * inverse * inverse * along)
    first = sums[:, KVR : KVR + HALF]
    second = sums[:, KVR + ROPE : KVR + ROPE + HALF]
    c, s = cos[...], sin[...]
    key = jnp.concatenate(
        [first * c + second * s, second * c - first * s, jnp.zeros((rows, ROPE), F32)], 1
    )
    low = jnp.concatenate([latent, key], 1).astype(BF)
    grads[:, :middle] = nope
    grads[:, middle:wide] = rope
    grads[:, wide:] = low
    back_low = product_t(low[:, : KVR + ROPE], lower_out[...]).astype(BF)
    back_query = (
        product_t(nope, query_out[:, :middle]) + product_t(rope, query_out[:, middle:])
    ).astype(BF)
    grad_lower_mid[...] = back_low
    grad_query_mid[...] = back_query
    exit_nope = product_left(query_mid[...], nope)
    exit_rope = product_left(query_mid[...], rope)
    heads = []
    for head in range(HEADS):
        at = (head // 2) * 128 + (head % 2) * HALF
        heads += [
            exit_nope[:, head * NOPE : (head + 1) * NOPE],
            exit_rope[:, at : at + HALF],
            exit_rope[:, at + ROPE : at + ROPE + HALF],
        ]
    rank = back_low.shape[1]
    pieces = (
        product_left(back_query, hidden[...]),
        jnp.concatenate(heads, 1),
        product_left(back_low, hidden[...]),
        product_left(lower_mid[...], low),
        product_left(tree[:, KVR:], lat[:, :KVR])[HALF : HALF + rank],
        upper_exit[HALF : HALF + rank, :],
        product_left(grad_out_mid[...], attended[here, :]),
        product_left(out_mid[...], mixed[...].astype(BF)),
    )
    end = 0
    for (at, _), piece in zip(offsets, pieces):
        end = at + piece.shape[1]
        joined[:, at:end] = piece.astype(BF)
    joined[:, end:] = jnp.zeros((rank, joined.shape[1] - end), BF)


def join(offsets, total, shift, operands):
    hidden, query_mid = operands[4], operands[3]
    rows, rank = query_mid.shape
    wide = HEADS * (NOPE + ROPE) + KVR + 2 * ROPE
    shapes = [((rows, wide), BF), ((rank, total), BF), ((rows, rank), BF), ((rows, rank), BF)]
    return pl.pallas_call(
        functools.partial(join_kernel, offsets),
        out_shape=[jax.ShapeDtypeStruct(shape, kind) for shape, kind in shapes],
        grid_spec=pltpu.PrefetchScalarGridSpec(
            num_scalar_prefetch=1,
            grid=(1,),
            in_specs=[fixed_at(v) for v in operands],
            out_specs=[whole_out(shape) for shape, _ in shapes],
        ),
        name="join",
        **costs(3e9, 25e6),
    )(shift, *operands)


def gated_parts(gate, up):
    sig = 1.0 / (1.0 + jnp.exp(-gate))
    swish = gate * sig
    return swish * up, swish, up * (sig * (1.0 + gate * (1.0 - sig)))


def slot_matrix(slots, owned, cap, rows):
    wanted = row_iota((cap, rows)) + 1
    return [slots[e : e + 1, :] == wanted for e in range(owned)]


def my_columns(first, extra, owned, offsets):
    shape = (max(8, owned), extra.shape[1])
    lane, row = lane_iota(shape), row_iota(shape) + first[0]
    pick = sum((lane == row + at).astype(F32) for at in offsets)
    return product_t(pick.astype(BF), extra)


def spread_grad_kernel(owned, cap, first, pay, sh_out, perm, gsh):
    rows = pay.shape[0]
    slots = my_columns(first, pay[:, D:], owned, (0,)).astype(jnp.int32)
    pick = slot_matrix(slots, owned, cap, rows)
    hot = jnp.concatenate([p.astype(F32) for p in pick], 0).astype(BF)
    values = pay[:, :D]
    got = product(hot, values)
    for e in range(owned):
        perm[e, 0] = got[e * cap : (e + 1) * cap].astype(BF)
    gsh[...] = product_t(values, sh_out[...])


def spread_feed_kernel(
    owned, cap, experts, first, pay, marks, gsh, sh_in, perm, gates, inner, gact
):
    rows = pay.shape[0]
    slots = my_columns(first, marks[...], owned, (0,)).astype(jnp.int32)
    probs = my_columns(first, pay[:, D:], owned, (0, experts))
    pick = slot_matrix(slots, owned, cap, rows)
    hot = jnp.concatenate([p.astype(F32) for p in pick], 0).astype(BF)
    values = pay[:, :D]
    got = product(hot, values)
    for e in range(owned):
        perm[e, 0] = got[e * cap : (e + 1) * cap].astype(BF)
        gate = jnp.sum(jnp.where(pick[e], probs[e : e + 1, :], 0.0), axis=1, keepdims=True)
        gates[e, 0] = jnp.broadcast_to(gate, (cap, 128))
    width = gsh.shape[1]
    act = product(values, sh_in[...])
    value, by_up, by_gate = gated_parts(act[:, :width], act[:, width:])
    inner[...] = value.astype(BF)
    gact[:, :width] = (gsh[...] * by_gate).astype(BF)
    gact[:, width:] = (gsh[...] * by_up).astype(BF)


def expert_grad_kernel(g, w_out, back):
    hidden = w_out.shape[1]
    for at in range(0, hidden, 256):
        width = min(256, hidden - at)
        back[0, :, at : at + width] = product_t(g[0], w_out[0, at : at + width, :]).astype(BF)


def expert_kernel(experts, first, x, back, gates, w_in, slot_out, inner, ggu):
    hidden = back.shape[2]
    x_here = x[0]
    gate_here = gates[0][:, :1]
    total = jnp.zeros((x_here.shape[0], 1), F32)
    for at in range(0, hidden, 256):
        width = min(256, hidden - at)
        gate = product(x_here, w_in[0, :, at : at + width])
        up = product(x_here, w_in[0, :, hidden + at : hidden + at + width])
        value, by_up, by_gate = gated_parts(gate, up)
        low = value.astype(BF)
        inner[0, :, at : at + width] = low
        here = back[0, :, at : at + width].astype(F32)
        scaled = here * gate_here
        ggu[:, at : at + width] = (scaled * by_gate).astype(BF)
        ggu[:, hidden + at : hidden + at + width] = (scaled * by_up).astype(BF)
        total = total + jnp.sum(low.astype(F32) * here, axis=1, keepdims=True)
    for at in range(0, D, 256):
        slot_out[0, :, at : at + 256] = product_t(ggu[...], w_in[0, at : at + 256, :]).astype(BF)
    high = total.astype(BF).astype(F32)
    mine = first[0] + pl.program_id(0)
    lane = lane_iota((x_here.shape[0], slot_out.shape[2] - D))
    extra = jnp.where(lane == mine, high, jnp.where(lane == experts + mine, total - high, 0.0))
    slot_out[0, :, D:] = extra.astype(BF)


def expert_rows_kernel(inner, gates, w_out, rows_out):
    gate_here = gates[0][:, :1]
    for at in range(0, D, 256):
        rows = product(inner[0], w_out[0, :, at : at + 256]) * gate_here
        rows_out[0, :, at : at + 256] = rows.astype(BF)


def collect_kernel(owned, cap, first, rows_perm, slots, inner, weight, *outs, transposed):
    rows = slots.shape[0]
    spread = (
        lane_iota((128, owned * cap)) // cap + first[0] == row_iota((128, owned * cap))
    ).astype(F32).astype(BF)
    named = product(slots[...], spread)
    wanted = (lane_iota((rows, owned * cap)) % cap + 1).astype(F32)
    hot = (named == wanted).astype(F32).astype(BF)
    values = jnp.concatenate([rows_perm[e, 0].astype(F32) for e in range(owned)], 0).astype(BF)
    if transposed:
        shared = product_t(inner[...], weight[...])
    else:
        shared = product(inner[...], weight[...])
    whole = (product(hot, values[:, :D]) + shared).astype(BF)
    if transposed:
        outs[0][:, :D] = whole
        outs[0][:, D:] = product(hot, values[:, D:]).astype(BF)
    else:
        at = 0
        for out in outs:
            out[...] = whole[:, at : at + out.shape[1]]
            at += out.shape[1]


def row_block(rows, width):
    return pl.BlockSpec((rows, width), lambda b, *_: (b, 0))


def fixed(shape):
    return pl.BlockSpec(shape, lambda b, *_: (0,) * len(shape))


def extra_block(rows):
    return pl.BlockSpec((rows, 128), lambda b, *_: (b, D // 128))


def perm_block(owned, cap, width):
    return pl.BlockSpec((owned, 1, cap, width), lambda b, *_: (0, b, 0, 0))


def costs(flops, moved):
    return dict(
        compiler_params=pltpu.CompilerParams(
            vmem_limit_bytes=VMEM_LIMIT
        ),
        cost_estimate=pl.CostEstimate(
            flops=int(flops), bytes_accessed=int(moved), transcendentals=0
        ),
    )


def spread_grad(first, payload, sh_out, groups, owned, cap):
    rows, width = payload.shape[0] // groups, sh_out.shape[0]
    return pl.pallas_call(
        functools.partial(spread_grad_kernel, owned, cap),
        out_shape=(
            jax.ShapeDtypeStruct((owned, groups, cap, D), BF),
            jax.ShapeDtypeStruct((groups * rows, width), F32),
        ),
        grid_spec=pltpu.PrefetchScalarGridSpec(
            num_scalar_prefetch=1,
            grid=(groups,),
            in_specs=[row_block(rows, payload.shape[1]), fixed(sh_out.shape)],
            out_specs=(perm_block(owned, cap, D), row_block(rows, width)),
        ),
        name="spread_grad",
        **costs(12e9, 28e6),
    )(first, payload, sh_out)


def spread_feed(first, payload, marks, gsh, sh_in, groups, owned, cap, experts):
    rows, width = payload.shape[0] // groups, gsh.shape[1]
    return pl.pallas_call(
        functools.partial(spread_feed_kernel, owned, cap, experts),
        out_shape=(
            jax.ShapeDtypeStruct((owned, groups, cap, D), BF),
            jax.ShapeDtypeStruct((owned, groups, cap, 128), F32),
            jax.ShapeDtypeStruct((groups * rows, width), BF),
            jax.ShapeDtypeStruct((groups * rows, 2 * width), BF),
        ),
        grid_spec=pltpu.PrefetchScalarGridSpec(
            num_scalar_prefetch=1,
            grid=(groups,),
            in_specs=[
                row_block(rows, payload.shape[1]),
                extra_block(rows),
                row_block(rows, width),
                fixed(sh_in.shape),
            ],
            out_specs=(
                perm_block(owned, cap, D),
                perm_block(owned, cap, 128),
                row_block(rows, width),
                row_block(rows, 2 * width),
            ),
        ),
        name="spread_feed",
        **costs(14e9, 28e6),
    )(first, payload, marks, gsh, sh_in)


def row_chunk(rows):
    count = 1
    while rows // count > 384 or rows % count or rows // count % 8:
        count += 1
    return rows // count


def expert_specs(owned, rows):
    chunk = row_chunk(rows)

    def at(width):
        return pl.BlockSpec((1, chunk, width), lambda e, i, *_: (e, i, 0))

    def weight(shape):
        return pl.BlockSpec((1,) + shape, lambda e, i, *_: (e, 0, 0))

    return (owned, rows // chunk), chunk, at, weight


def expert_grads(g, w_out):
    owned, rows, _ = g.shape
    hidden = w_out.shape[1]
    grid, _, at, weight = expert_specs(owned, rows)
    return pl.pallas_call(
        expert_grad_kernel,
        out_shape=jax.ShapeDtypeStruct((owned, rows, hidden), BF),
        grid=grid,
        in_specs=[at(D), weight((hidden, D))],
        out_specs=at(hidden),
        name="expert_grads",
        **costs(2 * owned * rows * D * hidden, owned * (D * hidden * 2 + rows * D * 4)),
    )(g, w_out)


def run_experts(first, x, back, gates, w_in, experts):
    owned, rows, _ = x.shape
    hidden = back.shape[2]
    grid, chunk, at, weight = expert_specs(owned, rows)
    return pl.pallas_call(
        functools.partial(expert_kernel, experts),
        out_shape=(
            jax.ShapeDtypeStruct((owned, rows, D + 128), BF),
            jax.ShapeDtypeStruct((owned, rows, hidden), BF),
        ),
        grid_spec=pltpu.PrefetchScalarGridSpec(
            num_scalar_prefetch=1,
            grid=grid,
            in_specs=[at(D), at(hidden), at(128), weight((D, 2 * hidden))],
            out_specs=(at(D + 128), at(hidden)),
            scratch_shapes=[pltpu.VMEM((chunk, 2 * hidden), BF)],
        ),
        name="experts",
        **costs(8 * owned * rows * D * hidden, owned * D * hidden * 4),
    )(first, x, back, gates, w_in)


def expert_rows(inner, gates, w_out):
    owned, rows, hidden = inner.shape
    grid, _, at, weight = expert_specs(owned, rows)
    return pl.pallas_call(
        expert_rows_kernel,
        out_shape=jax.ShapeDtypeStruct((owned, rows, D), BF),
        grid=grid,
        in_specs=[at(hidden), at(128), weight((hidden, D))],
        out_specs=at(D),
        name="expert_rows",
        **costs(2 * owned * rows * D * hidden, owned * (D * hidden * 2 + rows * D * 4)),
    )(inner, gates, w_out)


def collect(first, rows_perm, marks, inner, weight, widths, transposed):
    owned, groups, cap, width = rows_perm.shape
    rows = marks.shape[0] // groups
    return pl.pallas_call(
        functools.partial(collect_kernel, owned, cap, transposed=transposed),
        out_shape=[jax.ShapeDtypeStruct((groups * rows, w), BF) for w in widths],
        grid_spec=pltpu.PrefetchScalarGridSpec(
            num_scalar_prefetch=1,
            grid=(groups,),
            in_specs=[
                perm_block(owned, cap, width),
                extra_block(rows),
                row_block(rows, inner.shape[1]),
                fixed(weight.shape),
            ],
            out_specs=[row_block(rows, w) for w in widths],
        ),
        name="collect_grad" if transposed else "collect_rows",
        **costs(14e9, 28e6),
    )(first, rows_perm, marks, inner, weight)


MESH = pl.DeviceIdType.MESH
PLANE = 8


def neighbours():
    e = lax.axis_index("expert")
    core, x, y = e % 2, (e // 2) % 2, e // 4
    return e, 1 - 2 * core, 2 - 4 * x, 4 - 8 * y


def remote(src, dst, send_sem, recv_sem, **where):
    return pltpu.make_async_remote_copy(
        src_ref=src,
        dst_ref=dst,
        send_sem=send_sem,
        recv_sem=recv_sem,
        device_id=where,
        device_id_type=MESH,
    )


def greet(plane, levels):
    barrier = pltpu.get_barrier_semaphore()
    for who in plane:
        pl.semaphore_signal(barrier, inc=1, device_id={"expert": who}, device_id_type=MESH)
    for level in levels:
        pl.semaphore_signal(barrier, inc=1, device_id={"dp": level}, device_id_type=MESH)
    pl.semaphore_wait(barrier, len(plane) + len(levels))


class Mail:
    def __init__(self):
        self.sent = []

    def start(self, src, dst, pair, index, **where):
        copy = remote(src, dst, pair[0].at[index], pair[1].at[index], **where)
        copy.start()
        self.sent.append((None, copy))

    def arrived(self, dst, pair, index):
        here = neighbours()[0]
        remote(dst, dst, pair[0].at[index], pair[1].at[index], expert=here).wait_recv()

    def along(self, level, planes, src, dst, pair, index):
        z = lax.axis_index("dp")
        for way, fits, ahead in (
            (0, (level <= z) & (z < planes - 1), z + 1),
            (1, (level >= z) & (z > 0), z - 1),
        ):
            copy = remote(src, dst, pair[0].at[(way, *index)], pair[1].at[index], dp=ahead)
            pl.when(fits)(copy.start)
            self.sent.append((fits, copy))

    def line_arrived(self, dst, pair, index):
        here = neighbours()[0]
        remote(dst, dst, pair[0].at[(0, *index)], pair[1].at[index], expert=here).wait_recv()

    def drain(self):
        for fits, copy in self.sent:
            if fits is None:
                copy.wait_send()
            else:
                pl.when(fits)(copy.wait_send)


def nearest_levels(planes):
    if planes == 1:
        return [0]
    z = lax.axis_index("dp")
    power = 1 + 3 * z + 9 * (z * (z - 1) // 2) + 27 * (z * (z - 1) * (z - 2) // 6)
    order = ((1, 2, 3), (0, 2, 3), (1, 3, 0), (2, 1, 0))
    packed = [sum(order[at][m] * 4**at for at in range(4)) for m in range(3)]
    return [z] + [(code // power) % 4 for code in packed]


def spread_pieces(planes, count, source, place, mail, sems, meanwhile=None):
    line, by_x, by_y, by_far, by_core = [sems[2 * n : 2 * n + 2] for n in range(5)]
    e, to_core, to_x, to_y = neighbours()
    levels = nearest_levels(planes)
    partner, xn, yn, dg = e + to_core, e + to_x, e + to_y, e + to_x + to_y

    def at(k, who, i):
        return place(levels[k], who, i)

    def stage_a(k):
        for i in range(count):
            here = at(k, e, i)
            src = source(i) if k == 0 else here
            if k:
                mail.line_arrived(here, line, (levels[k], i))
            if planes > 1:
                mail.along(levels[k], planes, src, here, line, (levels[k], i))
            if i % 2 == 0:
                mail.start(src, here, by_x, (k, i), expert=xn)
                mail.start(src, here, by_y, (k, i), expert=yn)
            else:
                mail.start(src, here, by_y, (k, i), expert=yn)
                mail.start(src, here, by_x, (k, i), expert=xn)
            mail.start(src, here, by_core, (0, k, i), expert=partner)

    def stage_b(k):
        for i in range(count):
            left, up = at(k, xn, i), at(k, yn, i)
            mail.arrived(left, by_x, (k, i))
            if i % 2 == 0:
                mail.start(left, left, by_far, (k, i), expert=yn)
            mail.start(left, left, by_core, (1, k, i), expert=partner)
            mail.arrived(up, by_y, (k, i))
            if i % 2:
                mail.start(up, up, by_far, (k, i), expert=xn)
            mail.start(up, up, by_core, (2, k, i), expert=partner)

    def stage_c(k):
        for i in range(count):
            here = at(k, dg, i)
            mail.arrived(here, by_far, (k, i))
            mail.start(here, here, by_core, (3, k, i), expert=partner)

    for s in range(planes + 2):
        if s < planes:
            stage_a(s)
        if meanwhile is not None:
            meanwhile(s)
        if 0 <= s - 1 < planes:
            stage_b(s - 1)
        if 0 <= s - 2:
            stage_c(s - 2)
    for k in range(planes):
        for n, who in enumerate((e, xn, yn, dg)):
            for i in range(count):
                mail.arrived(at(k, who + to_core, i), by_core, (n, k, i))


def spread_sems(planes, count):
    dma = pltpu.SemaphoreType.DMA
    each, core = dma((planes, count)), dma((4, planes, count))
    return [dma((2, planes, count)), *([each] * 7), core, core]


def plane_peers(swaps):
    e, to_core, to_x, to_y = neighbours()
    if swaps:
        return [(e + j) % PLANE for j in range(1, PLANE)]
    return [e + to_core, e + to_x, e + to_y]


def other_levels(planes):
    if planes == 1:
        return []
    z = lax.axis_index("dp")
    return [(z + k) % planes for k in range(1, planes)]


def swap_out(mail, src, landing, pair, n):
    e = neighbours()[0]
    for j in range(1, PLANE):
        who = (e + j) % PLANE
        mail.start(src(who), landing(e), pair, (n, j - 1), expert=who)


def swap_in(mail, landing, pair, n):
    e = neighbours()[0]
    for j in range(1, PLANE):
        mail.arrived(landing((e + PLANE - j) % PLANE), pair, (n, j - 1))


def gather_kernel(planes, depth, pieces, count, swaps, lines, *refs):
    total = count + swaps + lines
    shards, outs = refs[:total], refs[total : 2 * total]
    sems = refs[2 * total :]
    own_sem, swap, line = sems[10], sems[11:13], sems[13:15]
    e = neighbours()[0]
    levels = nearest_levels(depth)
    z = levels[0]
    mail = Mail()
    greet(plane_peers(swaps), other_levels(depth))
    home = z if planes > 1 else 0

    def place(level, who, i):
        array, first, rows = pieces[i]
        return outs[array].at[level, who, pl.ds(first, rows)]

    def source(i):
        array, first, rows = pieces[i]
        return shards[array].at[pl.ds(first, rows)]

    mine = [pltpu.make_async_copy(shards[a], outs[a].at[home, e], own_sem.at[a]) for a in range(count)]
    for a in range(count, count + swaps):
        mine.append(pltpu.make_async_copy(shards[a].at[e], outs[a].at[z, e], own_sem.at[a]))
    for a in range(count + swaps, total):
        mine.append(pltpu.make_async_copy(shards[a], outs[a].at[z], own_sem.at[a]))
    for copy in mine:
        copy.start()
    for n in range(swaps):
        a = count + n
        swap_out(
            mail, lambda who: shards[a].at[who], lambda who: outs[a].at[z, who], swap, n
        )
    cuts = []
    for a in range(count, total):
        size = outs[a].shape[1]
        half = size // 2
        cuts += [(a, pl.ds(0, half)), (a, pl.ds(half, size - half))]

    def line_step(k):
        for i, (a, rows) in enumerate(cuts):
            here = outs[a].at[levels[k], rows]
            src = here if k or a < count + swaps else shards[a].at[rows]
            if k:
                mail.line_arrived(here, line, (levels[k], i))
            mail.along(levels[k], depth, src, here, line, (levels[k], i))

    first = 2 if planes > 1 else 0

    def meanwhile(s):
        if s == 1:
            for n in range(swaps):
                a = count + n
                swap_in(mail, lambda who: outs[a].at[z, who], swap, n)
                mine[a].wait()
        if 0 <= s - first < depth:
            line_step(s - first)

    spread_pieces(
        planes, len(pieces), source, place, mail, sems, meanwhile if cuts else None
    )
    if cuts:
        for k in range(planes + 2 - first, depth):
            line_step(k)
    for n, copy in enumerate(mine):
        if not count <= n < count + swaps:
            copy.wait()
    mail.drain()


def gather_blocks(shards, planes, cuts, ident, swaps=(), lines=(), depth=None):
    dma = pltpu.SemaphoreType.DMA
    depth = planes if depth is None else depth
    pieces = []
    for array, (shard, cut) in enumerate(zip(shards, cuts)):
        rows = shard.shape[0] // cut
        pieces += [(array, at * rows, rows) for at in range(cut)]
    count, total = len(shards), len(shards) + len(swaps) + len(lines)
    shapes = [jax.ShapeDtypeStruct((planes, PLANE) + s.shape, s.dtype) for s in shards]
    shapes += [jax.ShapeDtypeStruct((depth,) + s.shape, s.dtype) for s in [*swaps, *lines]]
    return pl.pallas_call(
        functools.partial(
            gather_kernel, planes, depth, pieces, count, len(swaps), len(lines)
        ),
        out_shape=shapes,
        in_specs=[pl.BlockSpec(memory_space=pl.ANY)] * total,
        out_specs=[pl.BlockSpec(memory_space=pl.ANY)] * total,
        scratch_shapes=[
            *spread_sems(planes, len(pieces)),
            dma((total,)),
            dma((max(1, len(swaps)), PLANE - 1)),
            dma((max(1, len(swaps)), PLANE - 1)),
            dma((2, depth, max(1, 2 * (total - count)))),
            dma((depth, max(1, 2 * (total - count)))),
        ],
        compiler_params=pltpu.CompilerParams(collective_id=ident, has_side_effects=True),
        name=f"gather{ident}",
    )(*shards, *swaps, *lines)


def bank_kernel(
    planes, wide, parts, front, grads, query_mid, lower_mid, query_in, lower_in, tokens, gain, mixed,
    out, result, landing, part, hold, back, hold_sem, *sems,
):
    e = neighbours()[0]
    z = lax.axis_index("dp")
    mail = Mail()
    swap = sems[10:12]
    step = hold.shape[1]
    steps = D // step

    def fetch(n):
        return pltpu.make_async_copy(
            front.at[pl.ds(n * step, step)], hold.at[n % 2], hold_sem.at[n % 2]
        )

    def multiply(n):
        fetch(n).wait()
        columns = slice(n * step, (n + 1) * step)
        back[:, columns] = (
            product_t(grads[...], hold[n % 2])
            + product(query_mid[...], query_in[:, columns])
            + product(lower_mid[...], lower_in[:, columns])
        )
        if n + 2 < steps:
            fetch(n + 2).start()

    def finish():
        values = tokens[...].astype(F32)
        inverse = lax.rsqrt(jnp.mean(values * values, axis=-1, keepdims=True) + 1e-06)
        scaled = back[...] * gain[...]
        along = jnp.mean(scaled * values, axis=-1, keepdims=True)
        change = inverse * scaled - values * (inverse * inverse * inverse * along)
        result[...] = (mixed[...] + change).astype(BF)

    for n in range(2):
        fetch(n).start()
    greet(plane_peers(1), other_levels(planes))

    def chunk(who):
        return pl.ds(pl.multiple_of(who * wide, 128), wide)

    swap_out(mail, lambda who: parts.at[:, chunk(who)], lambda who: landing.at[who], swap, 0)
    early = steps - planes
    for n in range(early):
        multiply(n)
    total = parts[:, chunk(e)].astype(F32)
    for j in range(1, PLANE):
        who = (e + PLANE - j) % PLANE
        mail.arrived(landing.at[who], swap, (0, j - 1))
        total = total + landing[who].astype(F32)
    low = total.astype(BF)
    part[...] = low
    out[z, e] = low

    def meanwhile(s):
        if s < planes:
            multiply(early + s)
        if s == planes:
            finish()

    spread_pieces(
        planes, 1, lambda i: part, lambda level, who, i: out.at[level, who], mail, sems, meanwhile
    )
    mail.drain()


def exchange_banks(joined, planes, ident, front, operands):
    rank, width = joined.shape
    wide = width // PLANE
    rows = operands[0].shape[0]
    dma = pltpu.SemaphoreType.DMA
    vmem = pl.BlockSpec(memory_space=pltpu.VMEM)
    return pl.pallas_call(
        functools.partial(bank_kernel, planes, wide),
        out_shape=[
            jax.ShapeDtypeStruct((planes, PLANE, rank, wide), BF),
            jax.ShapeDtypeStruct((rows, D), BF),
        ],
        in_specs=[vmem, pl.BlockSpec(memory_space=pl.ANY), *([vmem] * len(operands))],
        out_specs=[vmem, vmem],
        scratch_shapes=[
            pltpu.VMEM((PLANE, rank, wide), BF),
            pltpu.VMEM((rank, wide), BF),
            pltpu.VMEM((2, 256, front.shape[1]), BF),
            pltpu.VMEM((rows, D), F32),
            dma((2,)),
            *spread_sems(planes, 1),
            dma((1, PLANE - 1)),
            dma((1, PLANE - 1)),
        ],
        compiler_params=pltpu.CompilerParams(
            collective_id=ident, has_side_effects=True, vmem_limit_bytes=VMEM_LIMIT
        ),
        name=f"banks{ident}",
    )(joined, front, *operands)


def place_kernel(trees, offsets, chosen, full, *outs):
    slot = pl.program_id(0)
    wide = full.shape[3]
    for n, (at, width) in enumerate(offsets):
        total = jnp.zeros(outs[n].shape[1:], F32)
        for t in range(trees):
            pick = (chosen[t] == slot).astype(F32)
            columns = []
            while sum(c.shape[1] for c in columns) < width:
                here = at + sum(c.shape[1] for c in columns)
                first = here % wide
                upto = min(wide, first + at + width - here)
                columns.append(full[t, here // wide, :, first:upto].astype(F32))
            total = total + pick * jnp.concatenate(columns, 1)
        outs[n][0] = total


def place_banks(full, adapter_index, offsets, adapters):
    trees, _, rank, _ = full.shape
    return pl.pallas_call(
        functools.partial(place_kernel, trees, offsets),
        out_shape=[jax.ShapeDtypeStruct((adapters, rank, w), F32) for _, w in offsets],
        grid_spec=pltpu.PrefetchScalarGridSpec(
            num_scalar_prefetch=1,
            grid=(adapters,),
            in_specs=[pl.BlockSpec(full.shape, lambda a, chosen: (0, 0, 0, 0))],
            out_specs=[pl.BlockSpec((1, rank, w), lambda a, chosen: (a, 0, 0)) for _, w in offsets],
        ),
        name="place_banks",
        **costs(1e6, 11e6),
    )(adapter_index, full)


def scatter_kernel(parts, blocks, out, core_in, x_in, y_in, chip, total, sends, sems):
    e, to_core, to_x, to_y = neighbours()
    partner, xn, yn, dg = e + to_core, e + to_x, e + to_y, e + to_x + to_y
    rows = out.shape[0] // parts
    half = parts // 2
    greet((partner, xn, yn), [])
    mail, pair = Mail(), (sends, sems)

    def start(src, dst, index, **where):
        mail.start(src, dst, pair, index, **where)

    def arrived(dst, index):
        mail.arrived(dst, pair, index)

    def cut(p):
        return pl.ds(p * rows, rows)

    order = [p // 2 + (p % 2) * half for p in range(parts)]
    whose = (0, to_x, to_y, to_x + to_y)
    for p in order:
        for b in (3, 1, 2, 0):
            start(
                blocks.at[partner + whose[b], cut(p)],
                core_in.at[b, cut(p)],
                (b, p),
                expert=partner,
            )

    def add_chip(p):
        for b in (3, 1, 2, 0):
            arrived(core_in.at[b, cut(p)], (b, p))
            chip[b, cut(p), :] = (
                blocks[e + whose[b], cut(p), :].astype(F32) + core_in[b, cut(p), :].astype(F32)
            ).astype(BF)

    def first_hop(p):
        if p < half:
            start(chip.at[3, cut(p)], x_in.at[1, cut(p)], (5, p), expert=xn)
            start(chip.at[1, cut(p)], x_in.at[0, cut(p)], (4, p), expert=xn)
        else:
            start(chip.at[3, cut(p)], x_in.at[1, cut(p)], (5, p), expert=yn)
            start(chip.at[2, cut(p)], x_in.at[0, cut(p)], (4, p), expert=yn)

    def add_first(p):
        passed = 2 if p < half else 1
        arrived(x_in.at[1, cut(p)], (5, p))
        chip[passed, cut(p), :] = (
            chip[passed, cut(p), :].astype(F32) + x_in[1, cut(p), :].astype(F32)
        ).astype(BF)
        arrived(x_in.at[0, cut(p)], (4, p))
        total[cut(p), :] = chip[0, cut(p), :].astype(F32) + x_in[0, cut(p), :].astype(F32)

    def second_hop(p):
        if p < half:
            start(chip.at[2, cut(p)], y_in.at[cut(p)], (6, p), expert=yn)
        else:
            start(chip.at[1, cut(p)], y_in.at[cut(p)], (6, p), expert=xn)

    def finish(p):
        arrived(y_in.at[cut(p)], (6, p))
        out[cut(p), :] = (total[cut(p), :] + y_in[cut(p), :].astype(F32)).astype(out.dtype)

    for n, p in enumerate(order):
        add_chip(p)
        if n:
            first_hop(order[n - 1])
    first_hop(order[-1])
    for n, p in enumerate(order):
        add_first(p)
        if n:
            second_hop(order[n - 1])
    second_hop(order[-1])
    for p in order:
        finish(p)
    mail.drain()


def scatter_blocks(blocks, parts, ident, dtype):
    _, rows, width = blocks.shape
    dma = pltpu.SemaphoreType.DMA
    vmem = pl.BlockSpec(memory_space=pltpu.VMEM)
    return pl.pallas_call(
        functools.partial(scatter_kernel, parts),
        out_shape=jax.ShapeDtypeStruct((rows, width), dtype),
        in_specs=[vmem],
        out_specs=vmem,
        scratch_shapes=[
            pltpu.VMEM((4, rows, width), BF),
            pltpu.VMEM((2, rows, width), BF),
            pltpu.VMEM((rows, width), BF),
            pltpu.VMEM((4, rows, width), BF),
            pltpu.VMEM((rows, width), F32),
            dma((7, parts)),
            dma((7, parts)),
        ],
        compiler_params=pltpu.CompilerParams(
            collective_id=ident, has_side_effects=True, vmem_limit_bytes=VMEM_LIMIT
        ),
        name=f"scatter{ident}",
    )(blocks)


def gather_dp(shard):
    size = lax.axis_size("dp")
    me = lax.axis_index("dp")
    pieces = [shard]
    for k in range(1, size):
        pieces.append(lax.ppermute(shard, "dp", [(i, (i + k) % size) for i in range(size)]))
    stacked = jnp.stack(pieces)
    return jnp.concatenate(
        [lax.dynamic_index_in_dim(stacked, (me - s) % size, 0, keepdims=True) for s in range(size)], 0
    )


def gather_plane(value):
    groups = lax.axis_size("expert")
    spread = jnp.broadcast_to(value[None], (groups,) + value.shape)
    return lax.all_to_all(spread, "expert", split_axis=0, concat_axis=0, tiled=True)


def reduce_banks(gradients, local_tree, trees_here, adapter_index, adapters):
    groups = lax.axis_size("expert")
    rank = gradients[0].shape[0]
    widths = [g.shape[1] for g in gradients]
    joined = jnp.concatenate(gradients, 1).astype(BF)
    if trees_here > 1:
        joined = jnp.where(
            (jnp.arange(trees_here) == local_tree)[:, None, None], joined[None], 0.0
        ).astype(BF)
    joined = joined.reshape(groups, -1)
    parts = lax.all_to_all(joined, "expert", split_axis=0, concat_axis=0, tiled=True)
    part = jnp.sum(parts.astype(F32), axis=0).astype(BF)
    lanes = gather_dp(part)
    full = gather_plane(lanes)
    trees = lax.axis_size("dp") * trees_here
    full = full.transpose(1, 0, 2).reshape(trees, rank, sum(widths))
    outs, at = [], 0
    for width in widths:
        piece = full[:, :, at : at + width].astype(F32)
        at += width
        outs.append(
            sum(
                jnp.where(
                    (jnp.arange(adapters) == adapter_index[t])[:, None, None], piece[t][None], 0.0
                )
                for t in range(trees)
            )
        )
    return outs


def body(
    tokens_in,
    cotangent,
    segment_id,
    parent_id,
    adapter_index,
    routes,
    mixer_gain,
    latent_gain,
    feed_gain,
    query_matrix,
    latent_down,
    latent_up,
    output_matrix,
    router_matrix,
    shared_in,
    shared_out,
    expert_in,
    expert_out,
    query_entry,
    query_exit,
    lower_entry,
    lower_exit,
    upper_entry,
    upper_exit,
    output_entry,
    output_exit,
):
    rows_here = tokens_in.shape[0]
    groups = lax.axis_size("expert")
    planes = lax.axis_size("dp")
    group_pos = lax.axis_index("expert")
    trees_here = segment_id.shape[0] // TREE
    local_tree = group_pos * rows_here // TREE
    tree_offset = group_pos * rows_here - local_tree * TREE
    chosen = adapter_index[lax.axis_index("dp") * trees_here + local_tree]
    experts_all = router_matrix.shape[1]
    owned = expert_in.shape[0]
    capacity = max(2, 4 * rows_here * TOPK // (3 * experts_all))
    cap = -(-capacity // 8) * 8
    hidden_shared = shared_out.shape[0]
    both = ("dp", "expert")
    fast = groups == PLANE and planes == 4 and groups * rows_here == TREE and hidden_shared % 8 == 0

    weight_rows = query_matrix.shape[0]
    padded_shared = -(-planes * hidden_shared // 128) * 128
    fill = padded_shared - planes * hidden_shared
    (
        front,
        cut,
        query_in,
        query_out,
        lower_in,
        lower_out,
        upper_extra,
        up_extra,
        output_in,
        output_out,
        upper_in,
    ) = prepare(
        chosen,
        (query_matrix, latent_down, router_matrix, shared_in),
        (
            query_entry,
            query_exit,
            lower_entry,
            lower_exit,
            upper_entry,
            upper_exit,
            output_entry,
            output_exit,
        ),
        planes,
        groups,
        padded_shared,
    )
    if fast:
        front, mix_up, mix_out, sh_in = gather_blocks(
            [front, latent_up, output_matrix], planes, (4, 2, 2), 1, [cut]
        )
        front = front.reshape(D, -1)
        mix_up = mix_up.reshape(KVR, -1)
        mix_out = mix_out.reshape(-1, D)
    else:
        front = lax.all_gather(front, both, axis=0, tiled=True)
        mix_up = lax.all_gather(latent_up, both, axis=0, tiled=True)
        mix_out = lax.all_gather(output_matrix, both, axis=0, tiled=True)
        cut = lax.all_to_all(cut, "expert", split_axis=0, concat_axis=0, tiled=True)
        sh_in = gather_dp(cut.reshape(groups * weight_rows, -1))
    wide = HEADS * (NOPE + ROPE)
    feed_router = front[:, wide + KVR + ROPE :]

    seg_tree = lax.dynamic_slice_in_dim(segment_id, local_tree * TREE, TREE)
    par_tree = lax.dynamic_slice_in_dim(parent_id, local_tree * TREE, TREE)
    key_index = jnp.arange(TREE, dtype=jnp.int32)
    start_pos = jnp.where(par_tree == 0, TRUNK, TRUNK + SEGLEN)
    key_pos = jnp.where(seg_tree == 0, key_index, start_pos + key_index % SEGLEN)
    row_pos = lax.dynamic_slice_in_dim(key_pos, tree_offset, rows_here)
    row_seg = lax.dynamic_slice_in_dim(seg_tree, tree_offset, rows_here)
    step = 128
    while rows_here % step:
        step //= 2
    nb = -(-(rows_here - step) // SEGLEN) + 1
    first_block = tree_offset // SEGLEN
    shift = tree_offset - first_block * SEGLEN
    seg_blocks = seg_tree.reshape(TREE // SEGLEN, SEGLEN)[:, 0]
    par_blocks = par_tree.reshape(TREE // SEGLEN, SEGLEN)[:, 0]
    own = jnp.minimum(first_block + jnp.arange(nb, dtype=jnp.int32), TREE // SEGLEN - 1)
    own_seg = seg_blocks[own]
    own_par = par_blocks[own]
    is_leaf = ((own_seg != 0) & (own_par != 0)).astype(jnp.int32)
    match = (seg_blocks[None, :] == own_par[:, None]) & (is_leaf[:, None] > 0)
    par_block = jnp.sum(
        jnp.where(match, jnp.arange(TREE // SEGLEN, dtype=jnp.int32)[None, :], 0), axis=1
    )
    info = jnp.concatenate([own, par_block, (own_seg != 0).astype(jnp.int32), is_leaf])
    query_limit = jnp.where(
        row_seg == 0, tree_offset + jnp.arange(rows_here, dtype=jnp.int32), TRUNK - 1
    )

    def pad_rows(value):
        empty = jnp.zeros((nb * SEGLEN,) + value.shape[1:], value.dtype)
        return lax.dynamic_update_slice_in_dim(empty, value, shift, 0)

    def cut_rows(value):
        return lax.dynamic_slice_in_dim(value, shift, rows_here, 0)

    inverse = 10000.0 ** (-(jnp.arange(HALF, dtype=F32) * 2.0 / ROPE))
    angles = row_pos.astype(F32)[:, None] * inverse[None, :]
    cos_half, sin_half = jnp.cos(angles), jnp.sin(angles)
    cosine = jnp.concatenate([cos_half, cos_half], -1)
    sine = jnp.concatenate([sin_half, sin_half], -1)
    cos_pair = pad_rows(jnp.concatenate([cos_half] * 4, -1))
    sin_pair = pad_rows(jnp.concatenate([-sin_half, -sin_half, sin_half, sin_half], -1))
    limit_rows = pad_rows(query_limit)

    mask = jnp.sum(
        (routes[:, :, None] == jnp.arange(experts_all, dtype=jnp.int32)).astype(F32), axis=1
    )
    lower = (
        jnp.arange(rows_here)[:, None] >= jnp.arange(rows_here)[None, :]
    ).astype(BF)
    slots_here = product(lower, mask.astype(BF)) * mask

    offset = shift.astype(jnp.int32).reshape(1)
    q_nope, q_rope, latent_ext, latent_raw, hidden, query_mid, lower_mid = project(
        nb,
        offset,
        tokens_in,
        front,
        (
            query_in,
            query_out,
            lower_in,
            lower_out,
            upper_in,
            mixer_gain[None, :],
            latent_gain[None, :],
            cos_half,
            sin_half,
        ),
    )
    grad_payload = jnp.concatenate(
        [cotangent, slots_here.astype(BF), jnp.zeros((rows_here, 128 - experts_all), BF)], 1
    )
    grad_payload, latent_ext, out_rows = lax.optimization_barrier(
        (grad_payload, latent_ext, shared_out)
    )
    sh_out = gather_dp(out_rows).reshape(planes * hidden_shared, D)
    sh_out = jnp.pad(sh_out, ((0, fill), (0, 0)))
    all_grad = lax.all_gather(grad_payload, "expert", axis=0, tiled=True)
    rank = query_mid.shape[1]
    if fast:
        all_latent = gather_blocks([latent_ext], 1, (2,), 2)[0].reshape(TREE, LATW)
    else:
        all_latent = lax.all_gather(latent_ext, "expert", axis=0, tiled=True)
    tree_latent = lax.dynamic_slice_in_dim(all_latent, local_tree * TREE, TREE, 0)
    sh_in = sh_in.reshape(D, 2 * padded_shared)
    attended, level, keys_values = attend(
        nb, info, q_nope, q_rope, cos_pair, sin_pair, limit_rows, tree_latent, mix_up, up_extra
    )
    attended, sh_out = lax.optimization_barrier((attended, sh_out))
    mixed_state, feed_payload, router_probs, output_mid = mix(
        offset,
        attended,
        tokens_in,
        mix_out,
        front,
        output_in,
        output_out,
        feed_gain[None, :],
        experts_all,
    )

    first_expert = (group_pos * owned).astype(jnp.int32).reshape(1)
    grad_perm, grad_shared = spread_grad(first_expert, all_grad, sh_out, groups, owned, cap)
    flat = (owned, groups * cap)
    grad_inner = expert_grads(grad_perm.reshape(*flat, D), expert_out)

    all_feed = lax.all_gather(feed_payload, "expert", axis=0, tiled=True)

    all_feed, grad_inner = lax.optimization_barrier((all_feed, grad_inner))

    feed_perm, gates, inner_shared, gact_shared = spread_feed(
        first_expert, all_feed, all_grad, grad_shared, sh_in, groups, owned, cap, experts_all
    )
    gates = gates.reshape(*flat, 128)
    slot_perm, inner = run_experts(
        first_expert,
        feed_perm.reshape(*flat, D),
        grad_inner,
        gates,
        expert_in,
        experts_all,
    )
    grad_part = collect(
        first_expert,
        slot_perm.reshape(owned, groups, cap, D + 128),
        all_grad,
        gact_shared,
        sh_in,
        (D + 128,),
        True,
    )[0]
    grad_sum = lax.psum_scatter(grad_part, "expert", scatter_dimension=0, tiled=True)
    inner, grad_part = lax.optimization_barrier((inner, grad_part))
    rows_perm = expert_rows(inner, gates, expert_out)
    row_part, late_part = collect(
        first_expert,
        rows_perm.reshape(owned, groups, cap, D),
        all_grad,
        inner_shared,
        sh_out,
        (1280, D - 1280),
        False,
    )

    level, grad_part = lax.optimization_barrier((level, grad_part))
    far, near = chances(
        nb, info, q_nope, q_rope, cos_pair, sin_pair, limit_rows, tree_latent, keys_values, level
    )
    grad_sum, far, row_part = lax.optimization_barrier((grad_sum, far, row_part))
    row_sum = lax.psum_scatter(row_part, "expert", scatter_dimension=0, tiled=True)
    grad_mixed, grad_output_mid, grad_attended = turn(
        nb,
        offset,
        grad_sum,
        router_probs,
        mixed_state,
        cotangent,
        feed_gain[None, :],
        front,
        output_in,
        output_out,
        mix_out,
    )

    dq_nope, dq_rope, grad_up, grad_tree = attend_back(
        nb,
        info,
        q_nope,
        q_rope,
        cos_pair,
        sin_pair,
        tree_latent,
        keys_values,
        mix_up,
        up_extra,
        grad_attended,
        attended,
        far,
        near,
        upper_extra,
    )
    own_tree = grad_tree
    if trees_here > 1:
        grad_tree = lax.dynamic_update_slice_in_dim(
            jnp.zeros((groups * rows_here, grad_tree.shape[1]), BF), grad_tree, local_tree * TREE, 0
        )
    if fast:
        grad_latent = scatter_blocks(grad_tree.reshape(groups, rows_here, -1), 4, 5, F32)
    else:
        grad_latent = lax.psum_scatter(
            grad_tree, "expert", scatter_dimension=0, tiled=True
        ).astype(F32)
    row_sum, late_part, grad_latent = lax.optimization_barrier((row_sum, late_part, grad_latent))
    late_sum = lax.psum_scatter(late_part, "expert", scatter_dimension=0, tiled=True)
    offsets, end = [], 0
    for width in (
        query_entry.shape[2],
        query_exit.shape[2],
        lower_entry.shape[2],
        lower_exit.shape[2],
        upper_entry.shape[2],
        upper_exit.shape[2],
        output_entry.shape[2],
        output_exit.shape[2],
    ):
        offsets.append((end, width))
        end += -(-width // 128) * 128
    total = -(-end // (128 * PLANE)) * 128 * PLANE
    grad_front, joined, grad_query_mid, grad_lower_mid = join(
        tuple(offsets),
        total,
        offset,
        [
            dq_nope,
            dq_rope,
            query_out,
            query_mid,
            hidden,
            grad_latent.astype(F32),
            latent_raw,
            latent_gain[None, :],
            cos_half,
            sin_half,
            lower_out,
            lower_mid,
            own_tree,
            tree_latent,
            grad_up,
            output_mid,
            grad_mixed,
            grad_output_mid,
            attended,
        ],
    )

    adapters = query_entry.shape[0]
    if fast:
        full, grad_input = exchange_banks(
            joined,
            planes,
            6,
            front,
            [
                grad_front,
                grad_query_mid,
                grad_lower_mid,
                query_in,
                lower_in,
                tokens_in,
                mixer_gain[None, :],
                grad_mixed,
            ],
        )
        banks = place_banks(full, adapter_index, tuple(offsets), adapters)
    else:
        grad_hidden = (
            product_t(grad_front, front)
            + product(grad_query_mid, query_in)
            + product(grad_lower_mid, lower_in)
        )
        inputs = tokens_in.astype(F32)
        _, norm_one_back = jax.vjp(lambda operand: normed(operand, mixer_gain), inputs)
        grad_input = (grad_mixed + norm_one_back(grad_hidden)[0]).astype(BF)
        gradients = [joined[:, at : at + width] for at, width in offsets]
        banks = reduce_banks(gradients, local_tree, trees_here, adapter_index, adapters)
    late_sum, grad_input = lax.optimization_barrier((late_sum, grad_input))
    row_sum = jnp.concatenate([row_sum, late_sum], 1).astype(F32)
    block_output = (mixed_state + row_sum).astype(BF)
    return (block_output, grad_input, *banks)


def solution(mesh):
    tokens = P(("dp", "expert"), None)
    in_specs = (
        tokens,
        tokens,
        P("dp"),
        P("dp"),
        P(),
        tokens,
        P(),
        P(),
        P(),
        *([tokens] * 7),
        P("expert", None, None),
        P("expert", None, None),
        *([P()] * 8),
    )
    out_specs = (tokens, tokens, *([P()] * 8))
    return jax.shard_map(body, mesh=mesh, in_specs=in_specs, out_specs=out_specs, check_vma=False)
```

```python
import functools

import jax
import jax.numpy as jnp
from jax import lax
from jax.experimental import pallas as pl
from jax.experimental.pallas import tpu as pltpu
from jax.sharding import PartitionSpec as P

D = 2048
HEADS = 16
NOPE = 128
ROPE = 64
VDIM = 128
KVR = 512
TOPK = 6
SEGLEN = 128
TRUNK = 1024
TREE = 2560
LATW = 640
HALF = ROPE // 2
VMEM_LIMIT = 66_000_000
BF = jnp.bfloat16
F32 = jnp.float32


def product(left, right):
    return jnp.dot(left, right, preferred_element_type=F32)


def product_t(left, right):
    return lax.dot_general(left, right, (((1,), (1,)), ((), ())), preferred_element_type=F32)


def product_left(left, right):
    return lax.dot_general(left, right, (((0,), (0,)), ((), ())), preferred_element_type=F32)


def normed(operand, gain):
    return operand * lax.rsqrt(jnp.mean(operand * operand, axis=-1, keepdims=True) + 1e-06) * gain


def rotate(operand, cosine, sine):
    half_width = operand.shape[-1] // 2
    turned = jnp.concatenate([-operand[..., half_width:], operand[..., :half_width]], -1)
    return operand * cosine + turned * sine


def lane_iota(shape):
    return lax.broadcasted_iota(jnp.int32, shape, len(shape) - 1)


def row_iota(shape):
    return lax.broadcasted_iota(jnp.int32, shape, len(shape) - 2)


LOG2E = 1.4426950408889634
SCALING = 1.0 / (NOPE + ROPE) ** 0.5


def place_keys(nb, info, lat, latsel):
    latsel[:TRUNK, :] = lat[:TRUNK, :]
    for m in range(nb):
        for side in range(2):
            start = pl.multiple_of(info[side * nb + m] * SEGLEN, SEGLEN)
            at = TRUNK + (2 * m + side) * SEGLEN
            latsel[at : at + SEGLEN, :] = lat[pl.ds(start, SEGLEN), :]


def rotary_keys(tail, kr):
    tail = tail.astype(F32)
    first = jnp.where(lane_iota(tail.shape) % ROPE < HALF, tail, 0.0)
    kr[0] = first.astype(BF)
    kr[1] = pltpu.roll(first, HALF, 1).astype(BF)


def local_limit(nb, info, m, key, row):
    return jnp.where(
        key < SEGLEN,
        (row + 1) * info[2 * nb + m] - 1,
        SEGLEN + SEGLEN * info[3 * nb + m] - 1,
    )


def attend_kernel(
    nb, info, qn, qr, cosp, sinp, qlim, lat, up, upx, out, lse, kv,
    latsel, kr, bias, near, st, sl, pt,
):
    rows_all = qn.shape[0]

    @pl.when(pl.program_id(0) == 0)
    def _():
        place_keys(nb, info, lat, latsel)
        rotary_keys(latsel[:, KVR:], kr)
        bias[...] = jnp.where(row_iota((TRUNK, rows_all)) <= qlim[...], 0.0, -1e30)
        key = row_iota((2 * SEGLEN, SEGLEN))
        row = lane_iota((2 * SEGLEN, SEGLEN))
        for m in range(nb):
            near[m] = jnp.where(key <= local_limit(nb, info, m, key, row), 0.0, -1e30)

    raw = qr[...]
    qrot = (raw * cosp[...] + pltpu.roll(raw, ROPE, 1) * sinp[...]).astype(BF)
    keys = latsel.shape[0]
    rows = keys // 2 if keys % 512 == 0 else keys
    for at in range(0, keys, rows):
        kv[at : at + rows, :] = (
            product(latsel[at : at + rows, :KVR], up[...])
            + product(latsel[at : at + rows, KVR:], upx[...])
        ).astype(BF)
    blocks = [slice(m * SEGLEN, (m + 1) * SEGLEN) for m in range(nb)]
    nears = [slice(TRUNK + 2 * m * SEGLEN, TRUNK + 2 * (m + 1) * SEGLEN) for m in range(nb)]
    chunks = [slice(at, at + 256) for at in range(0, TRUNK, 256)]
    peaks = []
    for a in range(2):
        q = jnp.concatenate([qn[:, a * 128 : a * 128 + 128], qrot], 1)
        k = jnp.concatenate([kv[:, a * 256 : a * 256 + 128], kr[a]], 1)
        peak = None
        for there in chunks:
            scores = product_t(k[there], q) + bias[there, :]
            st[a, there, :] = scores
            top = jnp.max(scores, axis=0, keepdims=True)
            peak = top if peak is None else jnp.maximum(peak, top)
        tops = []
        for m in range(nb):
            scores = product_t(k[nears[m]], q[blocks[m]]) + near[m]
            sl[a, m] = scores
            tops.append(jnp.max(scores, axis=0, keepdims=True))
        peak = jnp.maximum(peak, jnp.concatenate(tops, 1))
        peaks.append(peak * (SCALING * LOG2E))
    levels = []
    for a in range(2):
        v = kv[:, a * 256 + 128 : a * 256 + 256]
        total = None
        for there in chunks:
            e = jnp.exp2(st[a, there, :] * (SCALING * LOG2E) - peaks[a])
            part = jnp.sum(e, axis=0, keepdims=True)
            total = part if total is None else total + part
            pt[a, there, :] = e.astype(BF)
        parts, sums = [], []
        for m in range(nb):
            e = jnp.exp2(sl[a, m] * (SCALING * LOG2E) - peaks[a][:, blocks[m]])
            sums.append(jnp.sum(e, axis=0, keepdims=True))
            parts.append(product_left(e.astype(BF), v[nears[m]]))
        total = total + jnp.concatenate(sums, 1)
        got = product_left(pt[a], v[:TRUNK]) + jnp.concatenate(parts, 0)
        inverse = jnp.broadcast_to(1.0 / total, (128, rows_all)).T
        out[:, a * 128 : a * 128 + 128] = (got * inverse).astype(BF)
        levels.append(peaks[a] + jnp.log(total) * LOG2E)
    lse[0] = jnp.concatenate(levels + [jnp.zeros((6, rows_all), F32)], 0)


def chance_kernel(
    nb, info, qn, qr, cosp, sinp, qlim, tails, kv, stats, pt, pn, tail, kr, bias, near
):
    rows_all = qn.shape[0]

    @pl.when(pl.program_id(0) == 0)
    def _():
        place_keys(nb, info, tails, tail)
        rotary_keys(tail[...], kr)
        bias[...] = jnp.where(row_iota((TRUNK, rows_all)) <= qlim[...], 0.0, -1e30)
        key = row_iota((2 * SEGLEN, SEGLEN))
        row = lane_iota((2 * SEGLEN, SEGLEN))
        for m in range(nb):
            near[m] = jnp.where(key <= local_limit(nb, info, m, key, row), 0.0, -1e30)

    raw = qr[...]
    qrot = (raw * cosp[...] + pltpu.roll(raw, ROPE, 1) * sinp[...]).astype(BF)
    for a in range(2):
        q = jnp.concatenate([qn[:, a * 128 : a * 128 + 128], qrot], 1)
        k = jnp.concatenate([kv[:, a * 256 : a * 256 + 128], kr[a]], 1)
        level = stats[0, a : a + 1, :]
        for at in range(0, TRUNK, 256):
            there = slice(at, at + 256)
            scores = product_t(k[there], q) + bias[there, :]
            pt[0, a, there, :] = jnp.exp2(scores * (SCALING * LOG2E) - level).astype(BF)
        for m in range(nb):
            here = slice(m * SEGLEN, (m + 1) * SEGLEN)
            there = slice(TRUNK + 2 * m * SEGLEN, TRUNK + 2 * (m + 1) * SEGLEN)
            scores = product_t(k[there], q[here]) + near[m]
            pn[0, a, m] = jnp.exp2(scores * (SCALING * LOG2E) - level[:, here]).astype(BF)


def attend_back_kernel(
    nb, info, qn, qr, cosp, sinp, tails, kv, up, upx, do, att, pt, pn, upper,
    dqn, dqr, gup, dlow, tail, kr, dss, dkv, acc, dkr, dlat,
):
    step = pl.program_id(0)
    rows_all = qn.shape[0]

    @pl.when(step == 0)
    def _():
        place_keys(nb, info, tails, tail)
        rotary_keys(tail[...], kr)
        acc[...] = jnp.zeros_like(acc)
        dkr[...] = jnp.zeros_like(dkr)

    raw = qr[...]
    qrot = (raw * cosp[...] + pltpu.roll(raw, ROPE, 1) * sinp[...]).astype(BF)
    dq_rope = None
    for a in range(2):
        q = jnp.concatenate([qn[:, a * 128 : a * 128 + 128], qrot], 1)
        k = jnp.concatenate([kv[:, a * 256 : a * 256 + 128], kr[a]], 1)
        v = kv[:, a * 256 + 128 : a * 256 + 256]
        g = do[:, a * 128 : a * 128 + 128]
        shares = g.astype(F32) * att[:, a * 128 : a * 128 + 128].astype(F32)
        main = shares.astype(BF)
        ones = jnp.ones((8, 128), BF)
        delta = product_t(ones, main) + product_t(ones, (shares - main.astype(F32)).astype(BF))
        delta = delta[:1]
        mine = lane_iota((1, 128)) % ROPE
        mine = (mine < HALF) if a == 0 else (mine >= HALF)

        def block(there, here, p):
            dp = product_t(v[there], g[here])
            ds = (p.astype(F32) * (dp - delta[:, here])).astype(BF)
            dk = product(ds, q[here]) * SCALING
            dkv[there, a * 256 : a * 256 + 128] = dk[:, :128].astype(BF)
            dkv[there, a * 256 + 128 : a * 256 + 256] = product(p, g[here]).astype(BF)
            dkr[there, :] += jnp.where(mine, dk[:, 128:], 0.0)
            return ds

        for at in range(0, TRUNK, 256):
            there = slice(at, at + 256)
            dss[there, :] = block(there, slice(0, rows_all), pt[0, a, there, :])
        parts = []
        for m in range(nb):
            here = slice(m * SEGLEN, (m + 1) * SEGLEN)
            there = slice(TRUNK + 2 * m * SEGLEN, TRUNK + 2 * (m + 1) * SEGLEN)
            parts.append(product_left(block(there, here, pn[0, a, m]), k[there]))
        dq = (product_left(dss[...], k[:TRUNK]) + jnp.concatenate(parts, 0)) * SCALING
        dqn[:, a * 128 : a * 128 + 128] = dq[:, :128].astype(BF)
        dq_rope = dq[:, 128:] if dq_rope is None else dq_rope + dq[:, 128:]
    dqr[...] = (dq_rope * cosp[...] + pltpu.roll(dq_rope * sinp[...], ROPE, 1)).astype(BF)
    gup[...] = product_left(tail[...], dkv[...])[HALF : HALF + gup.shape[0]]
    for at in range(0, tail.shape[0], 256):
        acc[at : at + 256, :KVR] += product_t(dkv[at : at + 256, :], up[...])
        acc[at : at + 256, KVR:] += product_t(dkv[at : at + 256, :], upx[...])

    @pl.when(step == pl.num_programs(0) - 1)
    def _():
        rope = dkr[...]
        folded = rope + pltpu.roll(rope, 128 - HALF, 1)
        keep = lane_iota(rope.shape) % ROPE < HALF
        acc[:, KVR:] += jnp.where(keep, folded, 0.0)
        dlat[:TRUNK, :] = acc[:TRUNK, :]
        dlat[TRUNK:, :] = jnp.zeros((TREE - TRUNK, LATW), F32)
        for m in range(nb):
            for side in range(2):
                start = pl.multiple_of(info[side * nb + m] * SEGLEN, SEGLEN)
                at = TRUNK + (2 * m + side) * SEGLEN
                dlat[pl.ds(start, SEGLEN), :] += acc[at : at + SEGLEN, :]
        low = dlat[:, KVR:].astype(BF)
        dlow[:, KVR:] = low
        dlow[:, :KVR] = (dlat[:, :KVR] + product(low, upper[...])).astype(BF)


def pair_spec(rows, width):
    return pl.BlockSpec((rows, width), lambda i, info: (0, i))


def lead_spec(rows, width):
    return pl.BlockSpec((1, rows, width), lambda i, info: (i, 0, 0))


def whole_spec(shape):
    return pl.BlockSpec(shape, lambda i, info: (0, 0))


def attend(nb, info, qn, qr, cosp, sinp, qlim, lat, up, upx):
    rows, keys = qn.shape[0], TRUNK + 2 * nb * SEGLEN
    return pl.pallas_call(
        functools.partial(attend_kernel, nb),
        out_shape=(
            jax.ShapeDtypeStruct((rows, HEADS * VDIM), BF),
            jax.ShapeDtypeStruct((HEADS // 2, 8, rows), F32),
            jax.ShapeDtypeStruct((keys, HEADS * (NOPE + VDIM)), BF),
        ),
        grid_spec=pltpu.PrefetchScalarGridSpec(
            num_scalar_prefetch=1,
            grid=(HEADS // 2,),
            in_specs=[
                pair_spec(rows, 256),
                pair_spec(rows, 128),
                whole_spec((rows, 128)),
                whole_spec((rows, 128)),
                whole_spec((1, rows)),
                whole_spec((TREE, LATW)),
                pair_spec(KVR, 512),
                pair_spec(LATW - KVR, 512),
            ],
            out_specs=(pair_spec(rows, 256), lead_spec(8, rows), pair_spec(keys, 512)),
            scratch_shapes=[
                pltpu.VMEM((keys, LATW), BF),
                pltpu.VMEM((2, keys, 128), BF),
                pltpu.VMEM((TRUNK, rows), F32),
                pltpu.VMEM((nb, 2 * SEGLEN, SEGLEN), F32),
                pltpu.VMEM((2, TRUNK, rows), F32),
                pltpu.VMEM((2, nb, 2 * SEGLEN, SEGLEN), F32),
                pltpu.VMEM((2, TRUNK, rows), BF),
            ],
        ),
        name="attend",
        **costs(30e9, 25e6),
    )(info, qn, qr, cosp, sinp, qlim[None, :], lat, up, upx)


def far_spec(keys, rows):
    return pl.BlockSpec((1, 2, keys, rows), lambda i, info: (i, 0, 0, 0))


def near_spec(nb):
    return pl.BlockSpec((1, 2, nb, 2 * SEGLEN, SEGLEN), lambda i, info: (i, 0, 0, 0, 0))


def chances(nb, info, qn, qr, cosp, sinp, qlim, lat, kv, stats):
    rows, keys = qn.shape[0], TRUNK + 2 * nb * SEGLEN
    return pl.pallas_call(
        functools.partial(chance_kernel, nb),
        out_shape=(
            jax.ShapeDtypeStruct((HEADS // 2, 2, TRUNK, rows), BF),
            jax.ShapeDtypeStruct((HEADS // 2, 2, nb, 2 * SEGLEN, SEGLEN), BF),
        ),
        grid_spec=pltpu.PrefetchScalarGridSpec(
            num_scalar_prefetch=1,
            grid=(HEADS // 2,),
            in_specs=[
                pair_spec(rows, 256),
                pair_spec(rows, 128),
                whole_spec((rows, 128)),
                whole_spec((rows, 128)),
                whole_spec((1, rows)),
                pl.BlockSpec((TREE, 128), lambda i, info: (0, KVR // 128)),
                pair_spec(keys, 512),
                lead_spec(8, rows),
            ],
            out_specs=(far_spec(TRUNK, rows), near_spec(nb)),
            scratch_shapes=[
                pltpu.VMEM((keys, 128), BF),
                pltpu.VMEM((2, keys, 128), BF),
                pltpu.VMEM((TRUNK, rows), F32),
                pltpu.VMEM((nb, 2 * SEGLEN, SEGLEN), F32),
            ],
        ),
        name="chances",
        **costs(6e9, 32e6),
    )(info, qn, qr, cosp, sinp, qlim[None, :], lat, kv, stats)


def attend_back(nb, info, qn, qr, cosp, sinp, lat, kv, up, upx, do, att, pt, pn, upper, rank):
    rows, keys = qn.shape[0], TRUNK + 2 * nb * SEGLEN
    return pl.pallas_call(
        functools.partial(attend_back_kernel, nb),
        out_shape=(
            jax.ShapeDtypeStruct((rows, HEADS * NOPE), BF),
            jax.ShapeDtypeStruct((rows, HEADS * ROPE), BF),
            jax.ShapeDtypeStruct((rank, HEADS * (NOPE + VDIM)), F32),
            jax.ShapeDtypeStruct((TREE, LATW), BF),
        ),
        grid_spec=pltpu.PrefetchScalarGridSpec(
            num_scalar_prefetch=1,
            grid=(HEADS // 2,),
            in_specs=[
                pair_spec(rows, 256),
                pair_spec(rows, 128),
                whole_spec((rows, 128)),
                whole_spec((rows, 128)),
                pl.BlockSpec((TREE, 128), lambda i, info: (0, KVR // 128)),
                pair_spec(keys, 512),
                pair_spec(KVR, 512),
                pair_spec(LATW - KVR, 512),
                pair_spec(rows, 256),
                pair_spec(rows, 256),
                far_spec(TRUNK, rows),
                near_spec(nb),
                whole_spec((LATW - KVR, KVR)),
            ],
            out_specs=(
                pair_spec(rows, 256),
                pair_spec(rows, 128),
                pair_spec(rank, 512),
                whole_spec((TREE, LATW)),
            ),
            scratch_shapes=[
                pltpu.VMEM((keys, 128), BF),
                pltpu.VMEM((2, keys, 128), BF),
                pltpu.VMEM((TRUNK, rows), BF),
                pltpu.VMEM((keys, 512), BF),
                pltpu.VMEM((keys, LATW), F32),
                pltpu.VMEM((keys, 128), F32),
                pltpu.VMEM((TREE, LATW), F32),
            ],
        ),
        name="attend_back",
        **costs(54e9, 30e6),
    )(info, qn, qr, cosp, sinp, lat, kv, up, upx, do, att, pt, pn, upper)


def head_columns(wide):
    nope, rope = [], []
    for pair in range(HEADS // 2):
        starts = [(2 * pair + a) * (NOPE + ROPE) for a in range(2)]
        for at in starts:
            nope.append(wide[:, at : at + NOPE])
        for half in range(2):
            for at in starts:
                first = at + NOPE + half * HALF
                rope.append(wide[:, first : first + HALF])
    return nope + rope


def prepare_kernel(planes, picked, info, *refs):
    query, down, router, shared = refs[:4]
    cotangent, slots, banks = refs[4], refs[5], refs[6 : 6 + picked]
    front, cut, payload = refs[6 + picked : 9 + picked]
    chosen = refs[9 + picked :]
    payload[:, :D] = cotangent[...]
    marks = slots[...]
    blank = jnp.zeros((marks.shape[0], 128 - marks.shape[1]), F32)
    payload[:, D:] = jnp.concatenate([marks, blank], 1).astype(BF)
    rest = [down[...].astype(F32), router[...].astype(F32)]
    front[...] = jnp.concatenate(head_columns(query[...].astype(F32)) + rest, 1).astype(BF)
    whole = shared[...].astype(F32)
    groups, _, width = cut.shape
    hidden = whole.shape[1] // 2
    each = hidden // (planes * groups)
    blank = jnp.zeros((whole.shape[0], width // 2 - planes * each), F32)
    for j in range(groups):
        columns = []
        for part in range(2):
            for i in range(planes):
                at = part * hidden + (i * groups + j) * each
                columns.append(whole[:, at : at + each])
            columns.append(blank)
        cut[j] = jnp.concatenate(columns, 1).astype(BF)
    rank = banks[0].shape[1]
    for n in range(picked):
        if n == 1:
            chosen[n][...] = jnp.concatenate(head_columns(banks[n][0].astype(F32)), 1).astype(BF)
        elif n in (4, 5):
            columns = banks[n].shape[2]
            chosen[n][...] = jnp.concatenate(
                [
                    jnp.zeros((HALF, columns), F32),
                    banks[n][0].astype(F32),
                    jnp.zeros((LATW - KVR - HALF - rank, columns), F32),
                ],
                0,
            ).astype(BF)
        else:
            chosen[n][...] = banks[n][0]
    chosen[picked][...] = banks[4][0]


def prepare(chosen, matrices, banks, planes, groups, padded):
    query, down, router, shared, cotangent, _ = matrices
    rows, rank = query.shape[0], banks[0].shape[1]
    width = query.shape[1] + down.shape[1] + router.shape[1]
    shapes = [
        (rows, width),
        (groups, rows, 2 * padded),
        (cotangent.shape[0], D + 128),
    ]
    for n, bank in enumerate(banks):
        shapes.append((LATW - KVR if n in (4, 5) else rank, bank.shape[2]))
    shapes.append((rank, banks[4].shape[2]))
    return pl.pallas_call(
        functools.partial(prepare_kernel, planes, len(banks)),
        out_shape=[jax.ShapeDtypeStruct(shape, BF) for shape in shapes],
        grid_spec=pltpu.PrefetchScalarGridSpec(
            num_scalar_prefetch=1,
            grid=(1,),
            in_specs=[
                *[fixed_at(m) for m in matrices],
                *[
                    pl.BlockSpec((1, rank, bank.shape[2]), lambda i, info: (info[0], 0, 0))
                    for bank in banks
                ],
            ],
            out_specs=[whole_out(shape) for shape in shapes],
        ),
        name="prepare",
        **costs(1e6, 4e6),
    )(chosen.reshape(1), *matrices, *banks)


def project_kernel(
    info, tokens, front, query_in, query_out, lower_in, lower_out, upper_in, mixer, gain, cos, sin,
    qn, qr, ext, raw, hidden, query_mid, lower_mid, acc,
):
    step = pl.program_id(0)

    @pl.when(step == 0)
    def _():
        hidden[...] = normed(tokens[...].astype(F32), mixer[...]).astype(BF)
        query_mid[...] = product_t(hidden[...], query_in[...]).astype(BF)
        lower_mid[...] = product_t(hidden[...], lower_in[...]).astype(BF)

    depth = front.shape[0]
    part = product(hidden[:, pl.ds(pl.multiple_of(step * depth, depth), depth)], front[...])

    @pl.when(step == 0)
    def _():
        acc[...] = part

    @pl.when(step > 0)
    def _():
        acc[...] += part

    @pl.when(step == pl.num_programs(0) - 1)
    def _():
        rows = hidden.shape[0]
        wide = HEADS * (NOPE + ROPE)
        middle = HEADS * NOPE
        here = pl.ds(pl.multiple_of(info[0], 16), rows)
        qn[...] = jnp.zeros_like(qn)
        qr[...] = jnp.zeros_like(qr)
        mid = query_mid[...]
        qn[here, :] = (acc[:, :middle] + product(mid, query_out[:, :middle])).astype(BF)
        qr[here, :] = acc[:, middle:wide] + product(mid, query_out[:, middle:])
        low = product(lower_mid[...], lower_out[...])
        latent = acc[:, wide : wide + KVR] + low[:, :KVR]
        raw[...] = latent
        norm = normed(latent, gain[...]).astype(BF)
        upper = product_t(norm, upper_in[...])
        key = acc[:, wide + KVR : wide + KVR + ROPE] + low[:, KVR:]
        first, second = key[:, :HALF], key[:, HALF:]
        c, s = cos[...], sin[...]
        ext[:, :KVR] = norm
        ext[:, KVR:] = jnp.concatenate(
            [
                first * c - second * s,
                upper,
                jnp.zeros((rows, HALF - upper.shape[1]), F32),
                second * c + first * s,
                jnp.zeros((rows, HALF), F32),
            ],
            1,
        ).astype(BF)


def fixed_at(value):
    return pl.BlockSpec(value.shape, lambda i, info: (0,) * value.ndim)


def whole_out(shape):
    return pl.BlockSpec(shape, lambda i, info: (0,) * len(shape))


def project(nb, shift, tokens, front, small):
    rows, depth = tokens.shape
    padded, step, rank = nb * SEGLEN, 512, small[0].shape[0]
    shapes = [
        ((padded, HEADS * NOPE), BF),
        ((padded, HEADS * ROPE), F32),
        ((rows, LATW), BF),
        ((rows, KVR), F32),
        ((rows, depth), BF),
        ((rows, rank), BF),
        ((rows, rank), BF),
    ]
    return pl.pallas_call(
        project_kernel,
        out_shape=[jax.ShapeDtypeStruct(shape, kind) for shape, kind in shapes],
        grid_spec=pltpu.PrefetchScalarGridSpec(
            num_scalar_prefetch=1,
            grid=(depth // step,),
            in_specs=[
                fixed_at(tokens),
                pl.BlockSpec((step, front.shape[1]), lambda i, info: (i, 0)),
                *[fixed_at(v) for v in small],
            ],
            out_specs=[whole_out(shape) for shape, _ in shapes],
            scratch_shapes=[pltpu.VMEM((rows, front.shape[1]), F32)],
        ),
        name="project",
        **costs(5e9, 20e6),
    )(shift, tokens, front, *small)


def mix_kernel(
    info, attended, tokens, matrix, router, out_in, out_out, gain,
    mixed, payload, probs, out_mid, acc,
):
    step = pl.program_id(0)
    rows = tokens.shape[0]
    here = pl.ds(pl.multiple_of(info[0], 16), rows)

    @pl.when(step == 0)
    def _():
        out_mid[...] = product_t(attended[here, :], out_in[...]).astype(BF)

    depth = matrix.shape[0]
    columns = pl.ds(pl.multiple_of(step * depth, depth), depth)
    part = product(attended[here, columns], matrix[...])

    @pl.when(step == 0)
    def _():
        acc[...] = part

    @pl.when(step > 0)
    def _():
        acc[...] += part

    @pl.when(step == pl.num_programs(0) - 1)
    def _():
        state = tokens[...].astype(F32) + (acc[...] + product(out_mid[...], out_out[...]))
        mixed[...] = state
        feed = normed(state, gain[...]).astype(BF)
        experts = probs.shape[1]
        logits = product(feed, router[...])[:, 128 - experts :]
        powers = jnp.exp(logits - jnp.max(logits, axis=1, keepdims=True))
        chance = powers / jnp.sum(powers, axis=1, keepdims=True)
        probs[...] = chance
        high = chance.astype(BF).astype(F32)
        payload[:, :D] = feed
        payload[:, D:] = jnp.concatenate([high, chance - high], 1).astype(BF)


def mix(shift, attended, tokens, matrix, front, out_in, out_out, gain, experts):
    rows = tokens.shape[0]
    step, rank = 512, out_in.shape[0]
    last = front.shape[1] // 128 - 1
    shapes = [((rows, D), F32), ((rows, D + 128), BF), ((rows, experts), F32), ((rows, rank), BF)]
    return pl.pallas_call(
        mix_kernel,
        out_shape=[jax.ShapeDtypeStruct(shape, kind) for shape, kind in shapes],
        grid_spec=pltpu.PrefetchScalarGridSpec(
            num_scalar_prefetch=1,
            grid=(D // step,),
            in_specs=[
                fixed_at(attended),
                fixed_at(tokens),
                pl.BlockSpec((step, D), lambda i, info: (i, 0)),
                pl.BlockSpec((D, 128), lambda i, info: (0, last)),
                fixed_at(out_in),
                fixed_at(out_out),
                fixed_at(gain),
            ],
            out_specs=[whole_out(shape) for shape, _ in shapes],
            scratch_shapes=[pltpu.VMEM((rows, D), F32)],
        ),
        name="mix",
        **costs(3e9, 14e6),
    )(shift, attended, tokens, matrix, front, out_in, out_out, gain)


def turn_kernel(
    info, sums, probs, mixed, cotangent, gain, router, out_in, out_out, matrix,
    grad_mixed, out_mid, do, low,
):
    rows = mixed.shape[0]

    @pl.when(pl.program_id(0) == 0)
    def _():
        experts = probs.shape[1]
        both = sums[:, D:].astype(F32)
        direct = both[:, :experts] + both[:, experts:]
        chance = probs[...]
        logits = chance * (direct - jnp.sum(chance * direct, axis=1, keepdims=True))
        spread = jnp.concatenate([jnp.zeros((rows, 128 - experts), F32), logits], 1).astype(BF)
        keep = jnp.where(lane_iota(router.shape) >= 128 - experts, router[...].astype(F32), 0.0)
        feed = sums[:, :D].astype(F32) + product_t(spread, keep.astype(BF))
        state = mixed[...]
        inverse = lax.rsqrt(jnp.mean(state * state, axis=-1, keepdims=True) + 1e-06)
        scaled = feed * gain[...]
        along = jnp.mean(scaled * state, axis=-1, keepdims=True)
        back = inverse * scaled - state * (inverse * inverse * inverse * along)
        total = cotangent[...].astype(F32) + back
        grad_mixed[...] = total
        low[...] = total.astype(BF)
        out_mid[...] = product_t(low[...], out_out[...]).astype(BF)

    here = pl.ds(pl.multiple_of(info[0], 16), rows)
    do[...] = jnp.zeros_like(do)
    do[here, :] = (
        product_t(low[...], matrix[...]) + product(out_mid[...], out_in[...])
    ).astype(BF)


def turn(nb, shift, sums, probs, mixed, cotangent, gain, front, out_in, out_out, matrix):
    rows, experts = probs.shape
    step, rank = 512, out_in.shape[0]
    last = front.shape[1] // 128 - 1
    padded = nb * SEGLEN
    return pl.pallas_call(
        turn_kernel,
        out_shape=[
            jax.ShapeDtypeStruct((rows, D), F32),
            jax.ShapeDtypeStruct((rows, rank), BF),
            jax.ShapeDtypeStruct((padded, D), BF),
        ],
        grid_spec=pltpu.PrefetchScalarGridSpec(
            num_scalar_prefetch=1,
            grid=(D // step,),
            in_specs=[
                fixed_at(sums),
                fixed_at(probs),
                fixed_at(mixed),
                fixed_at(cotangent),
                fixed_at(gain),
                pl.BlockSpec((D, 128), lambda i, info: (0, last)),
                pl.BlockSpec((rank, step), lambda i, info: (0, i)),
                fixed_at(out_out),
                pl.BlockSpec((step, D), lambda i, info: (i, 0)),
            ],
            out_specs=[
                whole_out((rows, D)),
                whole_out((rows, rank)),
                pl.BlockSpec((padded, step), lambda i, info: (0, i)),
            ],
            scratch_shapes=[pltpu.VMEM((rows, D), BF)],
        ),
        name="turn",
        **costs(3e9, 18e6),
    )(shift, sums, probs, mixed, cotangent, gain, front, out_in, out_out, matrix)


def join_kernel(
    offsets, info, dqn, dqr, query_out, query_mid, hidden, sums, raw, gain, cos, sin, lower_out,
    lower_mid, tree, lat, upper_exit, out_mid, mixed, grad_out_mid, attended,
    grads, joined, grad_query_mid, grad_lower_mid,
):
    rows = hidden.shape[0]
    here = pl.ds(pl.multiple_of(info[0], 16), rows)
    nope, rope = dqn[here, :], dqr[here, :]
    middle, wide = HEADS * NOPE, HEADS * (NOPE + ROPE)
    values = raw[...]
    inverse = lax.rsqrt(jnp.mean(values * values, axis=-1, keepdims=True) + 1e-06)
    scaled = sums[:, :KVR] * gain[...]
    along = jnp.mean(scaled * values, axis=-1, keepdims=True)
    latent = inverse * scaled - values * (inverse * inverse * inverse * along)
    first = sums[:, KVR : KVR + HALF]
    second = sums[:, KVR + ROPE : KVR + ROPE + HALF]
    c, s = cos[...], sin[...]
    key = jnp.concatenate(
        [first * c + second * s, second * c - first * s, jnp.zeros((rows, ROPE), F32)], 1
    )
    low = jnp.concatenate([latent, key], 1).astype(BF)
    grads[:, :middle] = nope
    grads[:, middle:wide] = rope
    grads[:, wide:] = low
    back_low = product_t(low[:, : KVR + ROPE], lower_out[...]).astype(BF)
    back_query = (
        product_t(nope, query_out[:, :middle]) + product_t(rope, query_out[:, middle:])
    ).astype(BF)
    grad_lower_mid[...] = back_low
    grad_query_mid[...] = back_query
    exit_nope = product_left(query_mid[...], nope)
    exit_rope = product_left(query_mid[...], rope)
    heads = []
    for head in range(HEADS):
        at = (head // 2) * 128 + (head % 2) * HALF
        heads += [
            exit_nope[:, head * NOPE : (head + 1) * NOPE],
            exit_rope[:, at : at + HALF],
            exit_rope[:, at + ROPE : at + ROPE + HALF],
        ]
    rank = back_low.shape[1]
    pieces = (
        product_left(back_query, hidden[...]),
        jnp.concatenate(heads, 1),
        product_left(back_low, hidden[...]),
        product_left(lower_mid[...], low),
        product_left(tree[...], lat[...])[HALF : HALF + rank],
        upper_exit[...],
        product_left(grad_out_mid[...], attended[here, :]),
        product_left(out_mid[...], mixed[...].astype(BF)),
    )
    end = 0
    for (at, _), piece in zip(offsets, pieces):
        end = at + piece.shape[1]
        joined[:, at:end] = piece.astype(BF)
    joined[:, end:] = jnp.zeros((rank, joined.shape[1] - end), BF)


def join(offsets, total, shift, operands):
    hidden, query_mid = operands[4], operands[3]
    rows, rank = query_mid.shape
    wide = HEADS * (NOPE + ROPE) + KVR + 2 * ROPE
    shapes = [((rows, wide), BF), ((rank, total), BF), ((rows, rank), BF), ((rows, rank), BF)]
    return pl.pallas_call(
        functools.partial(join_kernel, offsets),
        out_shape=[jax.ShapeDtypeStruct(shape, kind) for shape, kind in shapes],
        grid_spec=pltpu.PrefetchScalarGridSpec(
            num_scalar_prefetch=1,
            grid=(1,),
            in_specs=[
                *[fixed_at(v) for v in operands[:12]],
                pl.BlockSpec((TREE, LATW - KVR), lambda i, info: (0, KVR // (LATW - KVR))),
                pl.BlockSpec((TREE, KVR), lambda i, info: (0, 0)),
                *[fixed_at(v) for v in operands[14:]],
            ],
            out_specs=[whole_out(shape) for shape, _ in shapes],
        ),
        name="join",
        **costs(3e9, 25e6),
    )(shift, *operands)


def gated_parts(gate, up):
    sig = 1.0 / (1.0 + jnp.exp(-gate))
    swish = gate * sig
    return swish * up, swish, up * (sig * (1.0 + gate * (1.0 - sig)))


def slot_matrix(slots, owned, cap, rows):
    wanted = row_iota((cap, rows)) + 1
    return [slots[e : e + 1, :] == wanted for e in range(owned)]


def my_columns(first, extra, owned, offsets):
    shape = (max(8, owned), extra.shape[1])
    lane, row = lane_iota(shape), row_iota(shape) + first[0]
    pick = sum((lane == row + at).astype(F32) for at in offsets)
    return product_t(pick.astype(BF), extra)


def spread_grad_kernel(owned, cap, first, pay, sh_out, perm, gsh):
    rows = pay.shape[0]
    slots = my_columns(first, pay[:, D:], owned, (0,)).astype(jnp.int32)
    pick = slot_matrix(slots, owned, cap, rows)
    hot = jnp.concatenate([p.astype(F32) for p in pick], 0).astype(BF)
    values = pay[:, :D]
    got = product(hot, values)
    for e in range(owned):
        perm[e, 0] = got[e * cap : (e + 1) * cap].astype(BF)
    gsh[...] = product_t(values, sh_out[...])


def spread_feed_kernel(
    owned, cap, experts, first, pay, marks, gsh, sh_in, perm, gates, inner, gact
):
    rows = pay.shape[0]
    slots = my_columns(first, marks[...], owned, (0,)).astype(jnp.int32)
    probs = my_columns(first, pay[:, D:], owned, (0, experts))
    pick = slot_matrix(slots, owned, cap, rows)
    hot = jnp.concatenate([p.astype(F32) for p in pick], 0).astype(BF)
    values = pay[:, :D]
    got = product(hot, values)
    for e in range(owned):
        perm[e, 0] = got[e * cap : (e + 1) * cap].astype(BF)
        gate = jnp.sum(jnp.where(pick[e], probs[e : e + 1, :], 0.0), axis=1, keepdims=True)
        gates[e, 0] = jnp.broadcast_to(gate, (cap, 128))
    width = gsh.shape[1]
    act = product(values, sh_in[...])
    value, by_up, by_gate = gated_parts(act[:, :width], act[:, width:])
    inner[...] = value.astype(BF)
    gact[:, :width] = (gsh[...] * by_gate).astype(BF)
    gact[:, width:] = (gsh[...] * by_up).astype(BF)


def expert_grad_kernel(g, w_out, back):
    hidden = w_out.shape[1]
    for at in range(0, hidden, 256):
        width = min(256, hidden - at)
        back[0, :, at : at + width] = product_t(g[0], w_out[0, at : at + width, :]).astype(BF)


def expert_kernel(experts, first, x, back, gates, w_in, slot_out, inner, ggu):
    hidden = back.shape[2]
    x_here = x[0]
    gate_here = gates[0][:, :1]
    total = jnp.zeros((x_here.shape[0], 1), F32)
    for at in range(0, hidden, 256):
        width = min(256, hidden - at)
        gate = product(x_here, w_in[0, :, at : at + width])
        up = product(x_here, w_in[0, :, hidden + at : hidden + at + width])
        value, by_up, by_gate = gated_parts(gate, up)
        low = value.astype(BF)
        inner[0, :, at : at + width] = low
        here = back[0, :, at : at + width].astype(F32)
        scaled = here * gate_here
        ggu[:, at : at + width] = (scaled * by_gate).astype(BF)
        ggu[:, hidden + at : hidden + at + width] = (scaled * by_up).astype(BF)
        total = total + jnp.sum(low.astype(F32) * here, axis=1, keepdims=True)
    for at in range(0, D, 256):
        slot_out[0, :, at : at + 256] = product_t(ggu[...], w_in[0, at : at + 256, :]).astype(BF)
    high = total.astype(BF).astype(F32)
    mine = first[0] + pl.program_id(0)
    lane = lane_iota((x_here.shape[0], slot_out.shape[2] - D))
    extra = jnp.where(lane == mine, high, jnp.where(lane == experts + mine, total - high, 0.0))
    slot_out[0, :, D:] = extra.astype(BF)


def expert_rows_kernel(inner, gates, w_out, rows_out):
    gate_here = gates[0][:, :1]
    for at in range(0, D, 256):
        rows = product(inner[0], w_out[0, :, at : at + 256]) * gate_here
        rows_out[0, :, at : at + 256] = rows.astype(BF)


def collect_kernel(owned, cap, first, rows_perm, slots, inner, weight, *outs, transposed):
    rows = slots.shape[0]
    spread = (
        lane_iota((128, owned * cap)) // cap + first[0] == row_iota((128, owned * cap))
    ).astype(F32).astype(BF)
    named = product(slots[...], spread)
    wanted = (lane_iota((rows, owned * cap)) % cap + 1).astype(F32)
    hot = (named == wanted).astype(F32).astype(BF)
    values = jnp.concatenate([rows_perm[e, 0].astype(F32) for e in range(owned)], 0).astype(BF)
    if transposed:
        shared = product_t(inner[...], weight[...])
    else:
        shared = product(inner[...], weight[...])
    whole = (product(hot, values[:, :D]) + shared).astype(BF)
    if transposed:
        outs[0][:, :D] = whole
        outs[0][:, D:] = product(hot, values[:, D:]).astype(BF)
    else:
        at = 0
        for out in outs:
            out[...] = whole[:, at : at + out.shape[1]]
            at += out.shape[1]


def row_block(rows, width):
    return pl.BlockSpec((rows, width), lambda b, *_: (b, 0))


def fixed(shape):
    return pl.BlockSpec(shape, lambda b, *_: (0,) * len(shape))


def extra_block(rows):
    return pl.BlockSpec((rows, 128), lambda b, *_: (b, D // 128))


def perm_block(owned, cap, width):
    return pl.BlockSpec((owned, 1, cap, width), lambda b, *_: (0, b, 0, 0))


def costs(flops, moved):
    return dict(
        compiler_params=pltpu.CompilerParams(
            vmem_limit_bytes=VMEM_LIMIT
        ),
        cost_estimate=pl.CostEstimate(
            flops=int(flops), bytes_accessed=int(moved), transcendentals=0
        ),
    )


def spread_grad(first, payload, sh_out, groups, owned, cap):
    rows, width = payload.shape[0] // groups, sh_out.shape[0]
    return pl.pallas_call(
        functools.partial(spread_grad_kernel, owned, cap),
        out_shape=(
            jax.ShapeDtypeStruct((owned, groups, cap, D), BF),
            jax.ShapeDtypeStruct((groups * rows, width), F32),
        ),
        grid_spec=pltpu.PrefetchScalarGridSpec(
            num_scalar_prefetch=1,
            grid=(groups,),
            in_specs=[row_block(rows, payload.shape[1]), fixed(sh_out.shape)],
            out_specs=(perm_block(owned, cap, D), row_block(rows, width)),
        ),
        name="spread_grad",
        **costs(12e9, 28e6),
    )(first, payload, sh_out)


def spread_feed(first, payload, marks, gsh, sh_in, groups, owned, cap, experts):
    rows, width = payload.shape[0] // groups, gsh.shape[1]
    return pl.pallas_call(
        functools.partial(spread_feed_kernel, owned, cap, experts),
        out_shape=(
            jax.ShapeDtypeStruct((owned, groups, cap, D), BF),
            jax.ShapeDtypeStruct((owned, groups, cap, 128), F32),
            jax.ShapeDtypeStruct((groups * rows, width), BF),
            jax.ShapeDtypeStruct((groups * rows, 2 * width), BF),
        ),
        grid_spec=pltpu.PrefetchScalarGridSpec(
            num_scalar_prefetch=1,
            grid=(groups,),
            in_specs=[
                row_block(rows, payload.shape[1]),
                extra_block(rows),
                row_block(rows, width),
                fixed(sh_in.shape),
            ],
            out_specs=(
                perm_block(owned, cap, D),
                perm_block(owned, cap, 128),
                row_block(rows, width),
                row_block(rows, 2 * width),
            ),
        ),
        name="spread_feed",
        **costs(14e9, 28e6),
    )(first, payload, marks, gsh, sh_in)


def row_chunk(rows):
    count = 1
    while rows // count > 384 or rows % count or rows // count % 8:
        count += 1
    return rows // count


def expert_specs(owned, rows):
    chunk = row_chunk(rows)

    def at(width):
        return pl.BlockSpec((1, chunk, width), lambda e, i, *_: (e, i, 0))

    def weight(shape):
        return pl.BlockSpec((1,) + shape, lambda e, i, *_: (e, 0, 0))

    return (owned, rows // chunk), chunk, at, weight


def expert_grads(g, w_out):
    owned, rows, _ = g.shape
    hidden = w_out.shape[1]
    grid, _, at, weight = expert_specs(owned, rows)
    return pl.pallas_call(
        expert_grad_kernel,
        out_shape=jax.ShapeDtypeStruct((owned, rows, hidden), BF),
        grid=grid,
        in_specs=[at(D), weight((hidden, D))],
        out_specs=at(hidden),
        name="expert_grads",
        **costs(2 * owned * rows * D * hidden, owned * (D * hidden * 2 + rows * D * 4)),
    )(g, w_out)


def run_experts(first, x, back, gates, w_in, experts):
    owned, rows, _ = x.shape
    hidden = back.shape[2]
    grid, chunk, at, weight = expert_specs(owned, rows)
    return pl.pallas_call(
        functools.partial(expert_kernel, experts),
        out_shape=(
            jax.ShapeDtypeStruct((owned, rows, D + 128), BF),
            jax.ShapeDtypeStruct((owned, rows, hidden), BF),
        ),
        grid_spec=pltpu.PrefetchScalarGridSpec(
            num_scalar_prefetch=1,
            grid=grid,
            in_specs=[at(D), at(hidden), at(128), weight((D, 2 * hidden))],
            out_specs=(at(D + 128), at(hidden)),
            scratch_shapes=[pltpu.VMEM((chunk, 2 * hidden), BF)],
        ),
        name="experts",
        **costs(8 * owned * rows * D * hidden, owned * D * hidden * 4),
    )(first, x, back, gates, w_in)


def expert_rows(inner, gates, w_out):
    owned, rows, hidden = inner.shape
    grid, _, at, weight = expert_specs(owned, rows)
    return pl.pallas_call(
        expert_rows_kernel,
        out_shape=jax.ShapeDtypeStruct((owned, rows, D), BF),
        grid=grid,
        in_specs=[at(hidden), at(128), weight((hidden, D))],
        out_specs=at(D),
        name="expert_rows",
        **costs(2 * owned * rows * D * hidden, owned * (D * hidden * 2 + rows * D * 4)),
    )(inner, gates, w_out)


def collect(first, rows_perm, marks, inner, weight, widths, transposed):
    owned, groups, cap, width = rows_perm.shape
    rows = marks.shape[0] // groups
    return pl.pallas_call(
        functools.partial(collect_kernel, owned, cap, transposed=transposed),
        out_shape=[jax.ShapeDtypeStruct((groups * rows, w), BF) for w in widths],
        grid_spec=pltpu.PrefetchScalarGridSpec(
            num_scalar_prefetch=1,
            grid=(groups,),
            in_specs=[
                perm_block(owned, cap, width),
                extra_block(rows),
                row_block(rows, inner.shape[1]),
                fixed(weight.shape),
            ],
            out_specs=[row_block(rows, w) for w in widths],
        ),
        name="collect_grad" if transposed else "collect_rows",
        **costs(14e9, 28e6),
    )(first, rows_perm, marks, inner, weight)


MESH = pl.DeviceIdType.MESH
PLANE = 8


def neighbours():
    e = lax.axis_index("expert")
    core, x, y = e % 2, (e // 2) % 2, e // 4
    return e, 1 - 2 * core, 2 - 4 * x, 4 - 8 * y


def remote(src, dst, send_sem, recv_sem, **where):
    return pltpu.make_async_remote_copy(
        src_ref=src,
        dst_ref=dst,
        send_sem=send_sem,
        recv_sem=recv_sem,
        device_id=where,
        device_id_type=MESH,
    )


def greet(plane, levels):
    barrier = pltpu.get_barrier_semaphore()
    for who in plane:
        pl.semaphore_signal(barrier, inc=1, device_id={"expert": who}, device_id_type=MESH)
    for level in levels:
        pl.semaphore_signal(barrier, inc=1, device_id={"dp": level}, device_id_type=MESH)
    pl.semaphore_wait(barrier, len(plane) + len(levels))


class Mail:
    def __init__(self):
        self.sent = []

    def start(self, src, dst, pair, index, **where):
        copy = remote(src, dst, pair[0].at[index], pair[1].at[index], **where)
        copy.start()
        self.sent.append((None, copy))

    def arrived(self, dst, pair, index):
        here = neighbours()[0]
        remote(dst, dst, pair[0].at[index], pair[1].at[index], expert=here).wait_recv()

    def along(self, level, planes, src, dst, pair, index):
        z = lax.axis_index("dp")
        for way, fits, ahead in (
            (0, (level <= z) & (z < planes - 1), z + 1),
            (1, (level >= z) & (z > 0), z - 1),
        ):
            copy = remote(src, dst, pair[0].at[(way, *index)], pair[1].at[index], dp=ahead)
            pl.when(fits)(copy.start)
            self.sent.append((fits, copy))

    def line_arrived(self, dst, pair, index):
        here = neighbours()[0]
        remote(dst, dst, pair[0].at[(0, *index)], pair[1].at[index], expert=here).wait_recv()

    def drain(self):
        for fits, copy in self.sent:
            if fits is None:
                copy.wait_send()
            else:
                pl.when(fits)(copy.wait_send)


def nearest_levels(planes):
    if planes == 1:
        return [0]
    z = lax.axis_index("dp")
    power = 1 + 3 * z + 9 * (z * (z - 1) // 2) + 27 * (z * (z - 1) * (z - 2) // 6)
    order = ((1, 2, 3), (0, 2, 3), (1, 3, 0), (2, 1, 0))
    packed = [sum(order[at][m] * 4**at for at in range(4)) for m in range(3)]
    return [z] + [(code // power) % 4 for code in packed]


def spread_pieces(planes, count, source, place, mail, sems, meanwhile=None):
    line, by_x, by_y, by_far, by_core = [sems[2 * n : 2 * n + 2] for n in range(5)]
    e, to_core, to_x, to_y = neighbours()
    levels = nearest_levels(planes)
    partner, xn, yn, dg = e + to_core, e + to_x, e + to_y, e + to_x + to_y

    def at(k, who, i):
        return place(levels[k], who, i)

    def stage_a(k):
        for i in range(count):
            here = at(k, e, i)
            src = source(i) if k == 0 else here
            if k:
                mail.line_arrived(here, line, (levels[k], i))
            if planes > 1:
                mail.along(levels[k], planes, src, here, line, (levels[k], i))
            if i % 2 == 0:
                mail.start(src, here, by_x, (k, i), expert=xn)
                mail.start(src, here, by_y, (k, i), expert=yn)
            else:
                mail.start(src, here, by_y, (k, i), expert=yn)
                mail.start(src, here, by_x, (k, i), expert=xn)
            mail.start(src, here, by_core, (0, k, i), expert=partner)

    def stage_b(k):
        for i in range(count):
            left, up = at(k, xn, i), at(k, yn, i)
            mail.arrived(left, by_x, (k, i))
            if i % 2 == 0:
                mail.start(left, left, by_far, (k, i), expert=yn)
            mail.start(left, left, by_core, (1, k, i), expert=partner)
            mail.arrived(up, by_y, (k, i))
            if i % 2:
                mail.start(up, up, by_far, (k, i), expert=xn)
            mail.start(up, up, by_core, (2, k, i), expert=partner)

    def stage_c(k):
        for i in range(count):
            here = at(k, dg, i)
            mail.arrived(here, by_far, (k, i))
            mail.start(here, here, by_core, (3, k, i), expert=partner)

    for s in range(planes + 2):
        if s < planes:
            stage_a(s)
        if meanwhile is not None:
            meanwhile(s)
        if 0 <= s - 1 < planes:
            stage_b(s - 1)
        if 0 <= s - 2:
            stage_c(s - 2)
    for k in range(planes):
        for n, who in enumerate((e, xn, yn, dg)):
            for i in range(count):
                mail.arrived(at(k, who + to_core, i), by_core, (n, k, i))


def spread_sems(planes, count):
    dma = pltpu.SemaphoreType.DMA
    each, core = dma((planes, count)), dma((4, planes, count))
    return [dma((2, planes, count)), *([each] * 7), core, core]


def plane_peers(swaps):
    e, to_core, to_x, to_y = neighbours()
    if swaps:
        return [(e + j) % PLANE for j in range(1, PLANE)]
    return [e + to_core, e + to_x, e + to_y]


def other_levels(planes):
    if planes == 1:
        return []
    z = lax.axis_index("dp")
    return [(z + k) % planes for k in range(1, planes)]


def swap_out(mail, src, landing, pair, n):
    e = neighbours()[0]
    for j in range(1, PLANE):
        who = (e + j) % PLANE
        mail.start(src(who), landing(e), pair, (n, j - 1), expert=who)


def swap_in(mail, landing, pair, n):
    e = neighbours()[0]
    for j in range(1, PLANE):
        mail.arrived(landing((e + PLANE - j) % PLANE), pair, (n, j - 1))


def gather_kernel(planes, depth, pieces, count, swaps, lines, *refs):
    total = count + swaps + lines
    shards, outs = refs[:total], refs[total : 2 * total]
    sems = refs[2 * total :]
    own_sem, swap, line = sems[10], sems[11:13], sems[13:15]
    e = neighbours()[0]
    levels = nearest_levels(depth)
    z = levels[0]
    mail = Mail()
    greet(plane_peers(swaps), other_levels(depth))
    home = z if planes > 1 else 0

    def place(level, who, i):
        array, first, rows = pieces[i]
        return outs[array].at[level, who, pl.ds(first, rows)]

    def source(i):
        array, first, rows = pieces[i]
        return shards[array].at[pl.ds(first, rows)]

    mine = [pltpu.make_async_copy(shards[a], outs[a].at[home, e], own_sem.at[a]) for a in range(count)]
    for a in range(count, count + swaps):
        mine.append(pltpu.make_async_copy(shards[a].at[e], outs[a].at[z, e], own_sem.at[a]))
    for a in range(count + swaps, total):
        mine.append(pltpu.make_async_copy(shards[a], outs[a].at[z], own_sem.at[a]))
    for copy in mine:
        copy.start()
    for n in range(swaps):
        a = count + n
        swap_out(
            mail, lambda who: shards[a].at[who], lambda who: outs[a].at[z, who], swap, n
        )
    cuts = []
    for a in range(count, total):
        size = outs[a].shape[1]
        half = size // 2
        cuts += [(a, pl.ds(0, half)), (a, pl.ds(half, size - half))]

    def line_step(k):
        for i, (a, rows) in enumerate(cuts):
            here = outs[a].at[levels[k], rows]
            src = here if k or a < count + swaps else shards[a].at[rows]
            if k:
                mail.line_arrived(here, line, (levels[k], i))
            mail.along(levels[k], depth, src, here, line, (levels[k], i))

    first = 2 if planes > 1 else 0

    def meanwhile(s):
        if s == 1:
            for n in range(swaps):
                a = count + n
                swap_in(mail, lambda who: outs[a].at[z, who], swap, n)
                mine[a].wait()
        if 0 <= s - first < depth:
            line_step(s - first)

    spread_pieces(
        planes, len(pieces), source, place, mail, sems, meanwhile if cuts else None
    )
    if cuts:
        for k in range(planes + 2 - first, depth):
            line_step(k)
    for n, copy in enumerate(mine):
        if not count <= n < count + swaps:
            copy.wait()
    mail.drain()


def gather_blocks(shards, planes, cuts, ident, swaps=(), lines=(), depth=None):
    dma = pltpu.SemaphoreType.DMA
    depth = planes if depth is None else depth
    pieces = []
    for array, (shard, cut) in enumerate(zip(shards, cuts)):
        rows = shard.shape[0] // cut
        pieces += [(array, at * rows, rows) for at in range(cut)]
    count, total = len(shards), len(shards) + len(swaps) + len(lines)
    shapes = [jax.ShapeDtypeStruct((planes, PLANE) + s.shape, s.dtype) for s in shards]
    shapes += [jax.ShapeDtypeStruct((depth,) + s.shape, s.dtype) for s in [*swaps, *lines]]
    return pl.pallas_call(
        functools.partial(
            gather_kernel, planes, depth, pieces, count, len(swaps), len(lines)
        ),
        out_shape=shapes,
        in_specs=[pl.BlockSpec(memory_space=pl.ANY)] * total,
        out_specs=[pl.BlockSpec(memory_space=pl.ANY)] * total,
        scratch_shapes=[
            *spread_sems(planes, len(pieces)),
            dma((total,)),
            dma((max(1, len(swaps)), PLANE - 1)),
            dma((max(1, len(swaps)), PLANE - 1)),
            dma((2, depth, max(1, 2 * (total - count)))),
            dma((depth, max(1, 2 * (total - count)))),
        ],
        compiler_params=pltpu.CompilerParams(collective_id=ident, has_side_effects=True),
        name=f"gather{ident}",
    )(*shards, *swaps, *lines)


def bank_kernel(
    planes, wide, parts, front, grads, query_mid, lower_mid, query_in, lower_in, tokens, gain, mixed,
    out, result, landing, part, hold, back, hold_sem, *sems,
):
    e = neighbours()[0]
    z = lax.axis_index("dp")
    mail = Mail()
    swap = sems[10:12]
    step = hold.shape[1]
    steps = D // step

    def fetch(n):
        return pltpu.make_async_copy(
            front.at[pl.ds(n * step, step)], hold.at[n % 2], hold_sem.at[n % 2]
        )

    def multiply(n):
        fetch(n).wait()
        columns = slice(n * step, (n + 1) * step)
        back[:, columns] = (
            product_t(grads[...], hold[n % 2])
            + product(query_mid[...], query_in[:, columns])
            + product(lower_mid[...], lower_in[:, columns])
        )
        if n + 2 < steps:
            fetch(n + 2).start()

    def finish():
        values = tokens[...].astype(F32)
        inverse = lax.rsqrt(jnp.mean(values * values, axis=-1, keepdims=True) + 1e-06)
        scaled = back[...] * gain[...]
        along = jnp.mean(scaled * values, axis=-1, keepdims=True)
        change = inverse * scaled - values * (inverse * inverse * inverse * along)
        result[...] = (mixed[...] + change).astype(BF)

    for n in range(2):
        fetch(n).start()
    greet(plane_peers(1), other_levels(planes))

    def chunk(who):
        return pl.ds(pl.multiple_of(who * wide, 128), wide)

    swap_out(mail, lambda who: parts.at[:, chunk(who)], lambda who: landing.at[who], swap, 0)
    early = steps - planes
    for n in range(early):
        multiply(n)
    total = parts[:, chunk(e)].astype(F32)
    for j in range(1, PLANE):
        who = (e + PLANE - j) % PLANE
        mail.arrived(landing.at[who], swap, (0, j - 1))
        total = total + landing[who].astype(F32)
    low = total.astype(BF)
    part[...] = low
    out[z, e] = low

    def meanwhile(s):
        if s < planes:
            multiply(early + s)
        if s == planes:
            finish()

    spread_pieces(
        planes, 1, lambda i: part, lambda level, who, i: out.at[level, who], mail, sems, meanwhile
    )
    mail.drain()


def exchange_banks(joined, planes, ident, front, operands):
    rank, width = joined.shape
    wide = width // PLANE
    rows = operands[0].shape[0]
    dma = pltpu.SemaphoreType.DMA
    vmem = pl.BlockSpec(memory_space=pltpu.VMEM)
    return pl.pallas_call(
        functools.partial(bank_kernel, planes, wide),
        out_shape=[
            jax.ShapeDtypeStruct((planes, PLANE, rank, wide), BF),
            jax.ShapeDtypeStruct((rows, D), BF),
        ],
        in_specs=[vmem, pl.BlockSpec(memory_space=pl.ANY), *([vmem] * len(operands))],
        out_specs=[vmem, vmem],
        scratch_shapes=[
            pltpu.VMEM((PLANE, rank, wide), BF),
            pltpu.VMEM((rank, wide), BF),
            pltpu.VMEM((2, 256, front.shape[1]), BF),
            pltpu.VMEM((rows, D), F32),
            dma((2,)),
            *spread_sems(planes, 1),
            dma((1, PLANE - 1)),
            dma((1, PLANE - 1)),
        ],
        compiler_params=pltpu.CompilerParams(
            collective_id=ident, has_side_effects=True, vmem_limit_bytes=VMEM_LIMIT
        ),
        name=f"banks{ident}",
    )(joined, front, *operands)


def place_kernel(trees, offsets, chosen, full, *outs):
    slot = pl.program_id(0)
    wide = full.shape[3]
    for n, (at, width) in enumerate(offsets):
        total = jnp.zeros(outs[n].shape[1:], F32)
        for t in range(trees):
            pick = (chosen[t] == slot).astype(F32)
            columns = []
            while sum(c.shape[1] for c in columns) < width:
                here = at + sum(c.shape[1] for c in columns)
                first = here % wide
                upto = min(wide, first + at + width - here)
                columns.append(full[t, here // wide, :, first:upto].astype(F32))
            total = total + pick * jnp.concatenate(columns, 1)
        outs[n][0] = total


def place_banks(full, adapter_index, offsets, adapters):
    trees, _, rank, _ = full.shape
    return pl.pallas_call(
        functools.partial(place_kernel, trees, offsets),
        out_shape=[jax.ShapeDtypeStruct((adapters, rank, w), F32) for _, w in offsets],
        grid_spec=pltpu.PrefetchScalarGridSpec(
            num_scalar_prefetch=1,
            grid=(adapters,),
            in_specs=[pl.BlockSpec(full.shape, lambda a, chosen: (0, 0, 0, 0))],
            out_specs=[pl.BlockSpec((1, rank, w), lambda a, chosen: (a, 0, 0)) for _, w in offsets],
        ),
        name="place_banks",
        **costs(1e6, 11e6),
    )(adapter_index, full)


def scatter_kernel(parts, blocks, out, core_in, x_in, y_in, chip, total, sends, sems):
    e, to_core, to_x, to_y = neighbours()
    partner, xn, yn, dg = e + to_core, e + to_x, e + to_y, e + to_x + to_y
    rows = out.shape[0] // parts
    half = parts // 2
    greet((partner, xn, yn), [])
    mail, pair = Mail(), (sends, sems)

    def start(src, dst, index, **where):
        mail.start(src, dst, pair, index, **where)

    def arrived(dst, index):
        mail.arrived(dst, pair, index)

    def cut(p):
        return pl.ds(p * rows, rows)

    order = [p // 2 + (p % 2) * half for p in range(parts)]
    whose = (0, to_x, to_y, to_x + to_y)
    for p in order:
        for b in (3, 1, 2, 0):
            start(
                blocks.at[partner + whose[b], cut(p)],
                core_in.at[b, cut(p)],
                (b, p),
                expert=partner,
            )

    def add_chip(p):
        for b in (3, 1, 2, 0):
            arrived(core_in.at[b, cut(p)], (b, p))
            chip[b, cut(p), :] = (
                blocks[e + whose[b], cut(p), :].astype(F32) + core_in[b, cut(p), :].astype(F32)
            ).astype(BF)

    def first_hop(p):
        if p < half:
            start(chip.at[3, cut(p)], x_in.at[1, cut(p)], (5, p), expert=xn)
            start(chip.at[1, cut(p)], x_in.at[0, cut(p)], (4, p), expert=xn)
        else:
            start(chip.at[3, cut(p)], x_in.at[1, cut(p)], (5, p), expert=yn)
            start(chip.at[2, cut(p)], x_in.at[0, cut(p)], (4, p), expert=yn)

    def add_first(p):
        passed = 2 if p < half else 1
        arrived(x_in.at[1, cut(p)], (5, p))
        chip[passed, cut(p), :] = (
            chip[passed, cut(p), :].astype(F32) + x_in[1, cut(p), :].astype(F32)
        ).astype(BF)
        arrived(x_in.at[0, cut(p)], (4, p))
        total[cut(p), :] = chip[0, cut(p), :].astype(F32) + x_in[0, cut(p), :].astype(F32)

    def second_hop(p):
        if p < half:
            start(chip.at[2, cut(p)], y_in.at[cut(p)], (6, p), expert=yn)
        else:
            start(chip.at[1, cut(p)], y_in.at[cut(p)], (6, p), expert=xn)

    def finish(p):
        arrived(y_in.at[cut(p)], (6, p))
        out[cut(p), :] = (total[cut(p), :] + y_in[cut(p), :].astype(F32)).astype(out.dtype)

    for n, p in enumerate(order):
        add_chip(p)
        if n:
            first_hop(order[n - 1])
    first_hop(order[-1])
    for n, p in enumerate(order):
        add_first(p)
        if n:
            second_hop(order[n - 1])
    second_hop(order[-1])
    for p in order:
        finish(p)
    mail.drain()


def scatter_blocks(blocks, parts, ident, dtype):
    _, rows, width = blocks.shape
    dma = pltpu.SemaphoreType.DMA
    vmem = pl.BlockSpec(memory_space=pltpu.VMEM)
    return pl.pallas_call(
        functools.partial(scatter_kernel, parts),
        out_shape=jax.ShapeDtypeStruct((rows, width), dtype),
        in_specs=[vmem],
        out_specs=vmem,
        scratch_shapes=[
            pltpu.VMEM((4, rows, width), BF),
            pltpu.VMEM((2, rows, width), BF),
            pltpu.VMEM((rows, width), BF),
            pltpu.VMEM((4, rows, width), BF),
            pltpu.VMEM((rows, width), F32),
            dma((7, parts)),
            dma((7, parts)),
        ],
        compiler_params=pltpu.CompilerParams(
            collective_id=ident, has_side_effects=True, vmem_limit_bytes=VMEM_LIMIT
        ),
        name=f"scatter{ident}",
    )(blocks)


def pieces_dp(shard):
    size = lax.axis_size("dp")
    pieces = [shard]
    for k in range(1, size):
        pieces.append(lax.ppermute(shard, "dp", [(i, (i + k) % size) for i in range(size)]))
    return pieces


def joined_dp(pieces):
    size, me = len(pieces), lax.axis_index("dp")
    stacked = jnp.stack(pieces)
    return jnp.concatenate(
        [lax.dynamic_index_in_dim(stacked, (me - s) % size, 0, keepdims=True) for s in range(size)], 0
    )


def gather_dp(shard):
    return joined_dp(pieces_dp(shard))


def gather_plane(value):
    groups = lax.axis_size("expert")
    spread = jnp.broadcast_to(value[None], (groups,) + value.shape)
    return lax.all_to_all(spread, "expert", split_axis=0, concat_axis=0, tiled=True)


def reduce_banks(gradients, local_tree, trees_here, adapter_index, adapters):
    groups = lax.axis_size("expert")
    rank = gradients[0].shape[0]
    widths = [g.shape[1] for g in gradients]
    joined = jnp.concatenate(gradients, 1).astype(BF)
    if trees_here > 1:
        joined = jnp.where(
            (jnp.arange(trees_here) == local_tree)[:, None, None], joined[None], 0.0
        ).astype(BF)
    joined = joined.reshape(groups, -1)
    parts = lax.all_to_all(joined, "expert", split_axis=0, concat_axis=0, tiled=True)
    part = jnp.sum(parts.astype(F32), axis=0).astype(BF)
    lanes = gather_dp(part)
    full = gather_plane(lanes)
    trees = lax.axis_size("dp") * trees_here
    full = full.transpose(1, 0, 2).reshape(trees, rank, sum(widths))
    outs, at = [], 0
    for width in widths:
        piece = full[:, :, at : at + width].astype(F32)
        at += width
        outs.append(
            sum(
                jnp.where(
                    (jnp.arange(adapters) == adapter_index[t])[:, None, None], piece[t][None], 0.0
                )
                for t in range(trees)
            )
        )
    return outs


def body(
    tokens_in,
    cotangent,
    segment_id,
    parent_id,
    adapter_index,
    routes,
    mixer_gain,
    latent_gain,
    feed_gain,
    query_matrix,
    latent_down,
    latent_up,
    output_matrix,
    router_matrix,
    shared_in,
    shared_out,
    expert_in,
    expert_out,
    query_entry,
    query_exit,
    lower_entry,
    lower_exit,
    upper_entry,
    upper_exit,
    output_entry,
    output_exit,
):
    rows_here = tokens_in.shape[0]
    groups = lax.axis_size("expert")
    planes = lax.axis_size("dp")
    group_pos = lax.axis_index("expert")
    trees_here = segment_id.shape[0] // TREE
    local_tree = group_pos * rows_here // TREE
    tree_offset = group_pos * rows_here - local_tree * TREE
    chosen = adapter_index[lax.axis_index("dp") * trees_here + local_tree]
    experts_all = router_matrix.shape[1]
    owned = expert_in.shape[0]
    capacity = max(2, 4 * rows_here * TOPK // (3 * experts_all))
    cap = -(-capacity // 8) * 8
    hidden_shared = shared_out.shape[0]
    both = ("dp", "expert")
    fast = groups == PLANE and planes == 4 and groups * rows_here == TREE and hidden_shared % 8 == 0

    mask = jnp.sum(
        (routes[:, :, None] == jnp.arange(experts_all, dtype=jnp.int32)).astype(F32), axis=1
    )
    lower = (
        jnp.arange(rows_here)[:, None] >= jnp.arange(rows_here)[None, :]
    ).astype(BF)
    slots_here = product(lower, mask.astype(BF)) * mask

    weight_rows = query_matrix.shape[0]
    padded_shared = -(-planes * hidden_shared // 128) * 128
    fill = padded_shared - planes * hidden_shared
    (
        front,
        cut,
        grad_payload,
        query_in,
        query_out,
        lower_in,
        lower_out,
        upper_extra,
        up_extra,
        output_in,
        output_out,
        upper_in,
    ) = prepare(
        chosen,
        (query_matrix, latent_down, router_matrix, shared_in, cotangent, slots_here),
        (
            query_entry,
            query_exit,
            lower_entry,
            lower_exit,
            upper_entry,
            upper_exit,
            output_entry,
            output_exit,
        ),
        planes,
        groups,
        padded_shared,
    )
    if fast:
        front, mix_up, mix_out, sh_in = gather_blocks(
            [front, latent_up, output_matrix], planes, (4, 2, 2), 1, [cut]
        )
        front = front.reshape(D, -1)
        mix_up = mix_up.reshape(KVR, -1)
        mix_out = mix_out.reshape(-1, D)
    else:
        front = lax.all_gather(front, both, axis=0, tiled=True)
        mix_up = lax.all_gather(latent_up, both, axis=0, tiled=True)
        mix_out = lax.all_gather(output_matrix, both, axis=0, tiled=True)
        cut = lax.all_to_all(cut, "expert", split_axis=0, concat_axis=0, tiled=True)
        sh_in = gather_dp(cut.reshape(groups * weight_rows, -1))
    wide = HEADS * (NOPE + ROPE)
    feed_router = front[:, wide + KVR + ROPE :]

    seg_tree = lax.dynamic_slice_in_dim(segment_id, local_tree * TREE, TREE)
    par_tree = lax.dynamic_slice_in_dim(parent_id, local_tree * TREE, TREE)
    key_index = jnp.arange(TREE, dtype=jnp.int32)
    start_pos = jnp.where(par_tree == 0, TRUNK, TRUNK + SEGLEN)
    key_pos = jnp.where(seg_tree == 0, key_index, start_pos + key_index % SEGLEN)
    row_pos = lax.dynamic_slice_in_dim(key_pos, tree_offset, rows_here)
    row_seg = lax.dynamic_slice_in_dim(seg_tree, tree_offset, rows_here)
    step = 128
    while rows_here % step:
        step //= 2
    nb = -(-(rows_here - step) // SEGLEN) + 1
    first_block = tree_offset // SEGLEN
    shift = tree_offset - first_block * SEGLEN
    seg_blocks = seg_tree.reshape(TREE // SEGLEN, SEGLEN)[:, 0]
    par_blocks = par_tree.reshape(TREE // SEGLEN, SEGLEN)[:, 0]
    own = jnp.minimum(first_block + jnp.arange(nb, dtype=jnp.int32), TREE // SEGLEN - 1)
    own_seg = seg_blocks[own]
    own_par = par_blocks[own]
    is_leaf = ((own_seg != 0) & (own_par != 0)).astype(jnp.int32)
    match = (seg_blocks[None, :] == own_par[:, None]) & (is_leaf[:, None] > 0)
    par_block = jnp.sum(
        jnp.where(match, jnp.arange(TREE // SEGLEN, dtype=jnp.int32)[None, :], 0), axis=1
    )
    info = jnp.concatenate([own, par_block, (own_seg != 0).astype(jnp.int32), is_leaf])
    query_limit = jnp.where(
        row_seg == 0, tree_offset + jnp.arange(rows_here, dtype=jnp.int32), TRUNK - 1
    )

    def pad_rows(value):
        empty = jnp.zeros((nb * SEGLEN,) + value.shape[1:], value.dtype)
        return lax.dynamic_update_slice_in_dim(empty, value, shift, 0)

    def cut_rows(value):
        return lax.dynamic_slice_in_dim(value, shift, rows_here, 0)

    inverse = 10000.0 ** (-(jnp.arange(HALF, dtype=F32) * 2.0 / ROPE))
    angles = row_pos.astype(F32)[:, None] * inverse[None, :]
    cos_half, sin_half = jnp.cos(angles), jnp.sin(angles)
    cosine = jnp.concatenate([cos_half, cos_half], -1)
    sine = jnp.concatenate([sin_half, sin_half], -1)
    cos_pair = pad_rows(jnp.concatenate([cos_half] * 4, -1))
    sin_pair = pad_rows(jnp.concatenate([-sin_half, -sin_half, sin_half, sin_half], -1))
    limit_rows = pad_rows(query_limit)

    offset = shift.astype(jnp.int32).reshape(1)
    q_nope, q_rope, latent_ext, latent_raw, hidden, query_mid, lower_mid = project(
        nb,
        offset,
        tokens_in,
        front,
        (
            query_in,
            query_out,
            lower_in,
            lower_out,
            upper_in,
            mixer_gain[None, :],
            latent_gain[None, :],
            cos_half,
            sin_half,
        ),
    )
    grad_payload, latent_ext = lax.optimization_barrier((grad_payload, latent_ext))
    all_grad = lax.all_gather(grad_payload, "expert", axis=0, tiled=True)
    rank = query_mid.shape[1]
    if fast:
        all_latent = gather_blocks([latent_ext], 1, (2,), 2)[0].reshape(TREE, LATW)
    else:
        all_latent = lax.all_gather(latent_ext, "expert", axis=0, tiled=True)
    tree_latent = lax.dynamic_slice_in_dim(all_latent, local_tree * TREE, TREE, 0)
    sh_in = sh_in.reshape(D, 2 * padded_shared)
    out_rows, tree_latent = lax.optimization_barrier((shared_out, tree_latent))
    out_rows = pieces_dp(out_rows)
    attended, level, keys_values = attend(
        nb, info, q_nope, q_rope, cos_pair, sin_pair, limit_rows, tree_latent, mix_up, up_extra
    )
    attended, out_rows = lax.optimization_barrier((attended, out_rows))
    mixed_state, feed_payload, router_probs, output_mid = mix(
        offset,
        attended,
        tokens_in,
        mix_out,
        front,
        output_in,
        output_out,
        feed_gain[None, :],
        experts_all,
    )

    router_probs, out_rows = lax.optimization_barrier((router_probs, out_rows))
    sh_out = joined_dp(out_rows).reshape(planes * hidden_shared, D)
    sh_out = jnp.pad(sh_out, ((0, fill), (0, 0)))
    first_expert = (group_pos * owned).astype(jnp.int32).reshape(1)
    grad_perm, grad_shared = spread_grad(first_expert, all_grad, sh_out, groups, owned, cap)
    flat = (owned, groups * cap)
    grad_inner = expert_grads(grad_perm.reshape(*flat, D), expert_out)

    all_feed = lax.all_gather(feed_payload, "expert", axis=0, tiled=True)

    all_feed, grad_inner = lax.optimization_barrier((all_feed, grad_inner))

    feed_perm, gates, inner_shared, gact_shared = spread_feed(
        first_expert, all_feed, all_grad, grad_shared, sh_in, groups, owned, cap, experts_all
    )
    gates = gates.reshape(*flat, 128)
    slot_perm, inner = run_experts(
        first_expert,
        feed_perm.reshape(*flat, D),
        grad_inner,
        gates,
        expert_in,
        experts_all,
    )
    grad_part = collect(
        first_expert,
        slot_perm.reshape(owned, groups, cap, D + 128),
        all_grad,
        gact_shared,
        sh_in,
        (D + 128,),
        True,
    )[0]
    grad_sum = lax.psum_scatter(grad_part, "expert", scatter_dimension=0, tiled=True)
    inner, grad_part = lax.optimization_barrier((inner, grad_part))
    rows_perm = expert_rows(inner, gates, expert_out)
    row_part, late_part = collect(
        first_expert,
        rows_perm.reshape(owned, groups, cap, D),
        all_grad,
        inner_shared,
        sh_out,
        (1280, D - 1280),
        False,
    )

    level, grad_part = lax.optimization_barrier((level, grad_part))
    far, near = chances(
        nb, info, q_nope, q_rope, cos_pair, sin_pair, limit_rows, tree_latent, keys_values, level
    )
    grad_sum, far, row_part = lax.optimization_barrier((grad_sum, far, row_part))
    row_sum = lax.psum_scatter(row_part, "expert", scatter_dimension=0, tiled=True)
    grad_mixed, grad_output_mid, grad_attended = turn(
        nb,
        offset,
        grad_sum,
        router_probs,
        mixed_state,
        cotangent,
        feed_gain[None, :],
        front,
        output_in,
        output_out,
        mix_out,
    )

    dq_nope, dq_rope, grad_up, grad_tree = attend_back(
        nb,
        info,
        q_nope,
        q_rope,
        cos_pair,
        sin_pair,
        tree_latent,
        keys_values,
        mix_up,
        up_extra,
        grad_attended,
        attended,
        far,
        near,
        upper_extra,
        rank,
    )
    own_tree = grad_tree
    if trees_here > 1:
        grad_tree = lax.dynamic_update_slice_in_dim(
            jnp.zeros((groups * rows_here, grad_tree.shape[1]), BF), grad_tree, local_tree * TREE, 0
        )
    if fast:
        grad_latent = scatter_blocks(grad_tree.reshape(groups, rows_here, -1), 4, 5, F32)
    else:
        grad_latent = lax.psum_scatter(
            grad_tree, "expert", scatter_dimension=0, tiled=True
        ).astype(F32)
    row_sum, late_part, grad_latent = lax.optimization_barrier((row_sum, late_part, grad_latent))
    late_sum = lax.psum_scatter(late_part, "expert", scatter_dimension=0, tiled=True)
    offsets, end = [], 0
    for width in (
        query_entry.shape[2],
        query_exit.shape[2],
        lower_entry.shape[2],
        lower_exit.shape[2],
        upper_entry.shape[2],
        upper_exit.shape[2],
        output_entry.shape[2],
        output_exit.shape[2],
    ):
        offsets.append((end, width))
        end += -(-width // 128) * 128
    total = -(-end // (128 * PLANE)) * 128 * PLANE
    grad_front, joined, grad_query_mid, grad_lower_mid = join(
        tuple(offsets),
        total,
        offset,
        [
            dq_nope,
            dq_rope,
            query_out,
            query_mid,
            hidden,
            grad_latent.astype(F32),
            latent_raw,
            latent_gain[None, :],
            cos_half,
            sin_half,
            lower_out,
            lower_mid,
            own_tree,
            tree_latent,
            grad_up,
            output_mid,
            grad_mixed,
            grad_output_mid,
            attended,
        ],
    )

    adapters = query_entry.shape[0]
    if fast:
        full, grad_input = exchange_banks(
            joined,
            planes,
            6,
            front,
            [
                grad_front,
                grad_query_mid,
                grad_lower_mid,
                query_in,
                lower_in,
                tokens_in,
                mixer_gain[None, :],
                grad_mixed,
            ],
        )
        banks = place_banks(full, adapter_index, tuple(offsets), adapters)
    else:
        grad_hidden = (
            product_t(grad_front, front)
            + product(grad_query_mid, query_in)
            + product(grad_lower_mid, lower_in)
        )
        inputs = tokens_in.astype(F32)
        _, norm_one_back = jax.vjp(lambda operand: normed(operand, mixer_gain), inputs)
        grad_input = (grad_mixed + norm_one_back(grad_hidden)[0]).astype(BF)
        gradients = [joined[:, at : at + width] for at, width in offsets]
        banks = reduce_banks(gradients, local_tree, trees_here, adapter_index, adapters)
    late_sum, grad_input = lax.optimization_barrier((late_sum, grad_input))
    row_sum = jnp.concatenate([row_sum, late_sum], 1).astype(F32)
    block_output = (mixed_state + row_sum).astype(BF)
    return (block_output, grad_input, *banks)


def solution(mesh):
    tokens = P(("dp", "expert"), None)
    in_specs = (
        tokens,
        tokens,
        P("dp"),
        P("dp"),
        P(),
        tokens,
        P(),
        P(),
        P(),
        *([tokens] * 7),
        P("expert", None, None),
        P("expert", None, None),
        *([P()] * 8),
    )
    out_specs = (tokens, tokens, *([P()] * 8))
    return jax.shard_map(body, mesh=mesh, in_specs=in_specs, out_specs=out_specs, check_vma=False)
```
